32 devices in a mesh: context: 4 (over z), dp: 4 (over y, core), head: 2 (over x).
Axes of the slice: x: 2, y: 2, z: 4, core: 2. Of those that a mesh axis runs over, the one named last changes fastest.
Arguments:
- inputs: bfloat16 [4, 512, 2304], P('dp', 'context', 'head'), may hold values from -6 to 6
- output_grad: bfloat16 [4, 512, 2304], P('dp', 'context', 'head'), may hold values from -6 to 6
- qkv_weight: bfloat16 [2304, 3, 4096], P(None, None, 'head'), may hold values from -0.125 to 0.125
- out_weight: bfloat16 [2304, 4096], P(None, 'head'), may hold values from -0.09375 to 0.09375
- down_weight: bfloat16 [2304, 128], replicated, may hold values from -0.125 to 0.125
- up_weight: bfloat16 [128, 4096], P(None, 'head'), may hold values from -0.5 to 0.5
- beta_weight: bfloat16 [2304, 32], P(None, 'head'), may hold values from -0.125 to 0.125
- gate_bias: float32 [4096], P('head'), may hold values from -9 to -1.6, as said below
Outputs:
- layer_out: bfloat16 [4, 512, 2304], P('dp', 'context', 'head')
- input_grad: bfloat16 [4, 512, 2304], P('dp', 'context', 'head')
- qkv_grad: bfloat16 [2304, 3, 4096], P(('context', 'dp'), None, 'head')
- out_grad: bfloat16 [2304, 4096], P(('context', 'dp'), 'head')
- up_grad: float32 [128, 4096], P(None, 'head')
- down_grad: float32 [2304, 128], replicated
- beta_grad: float32 [2304, 32], P(None, 'head')
- bias_grad: float32 [4096], P('head')
The draws below stay inside these ranges and needn't reach their ends.
Inputs may be any that keep to these rules, and one draw needn't show every extreme that they name: `gate_bias`: offsets of the decay gate, one per channel.
All inputs are finite; a program needn't handle non-finite values.
Results may differ from the reference program's by a relative error of at most 0.02.
Values may be sent and summed in bfloat16 or wider, within the bound.
A program may use at most 192 MiB of HBM per device.

```python
import math
import jax
import jax.numpy as jnp
from jax import lax

D = 2304
H = 32
DK = 128
RANK = 128
SPAN = 64
TOK_DEV = 128
SEQS = 4
LENGTH = 512
N_HEAD = 2


def draw_gate_bias(key, part):
    choose_key, slow_key, fast_key = jax.random.split(key, 3)
    channels = H * DK
    fast_share = 0.5
    picked = jax.random.uniform(choose_key, (channels,), jnp.float32) < fast_share
    slow_rate = jnp.exp(jax.random.uniform(slow_key, (channels,), jnp.float32, math.log(0.3 / LENGTH), math.log(1.0 / LENGTH)))
    fast_rate = jnp.exp(jax.random.uniform(fast_key, (channels,), jnp.float32, math.log(1.0 / 60.0), math.log(1.0 / 25.0)))
    fraction = 4.0 * jnp.where(picked, fast_rate, slow_rate)
    return jnp.log(fraction / (1.0 - fraction)).astype(jnp.float32)


def block_scale(rng, extent, cuts, smallest, largest):
    factor_of = 1.0
    for position, parts in cuts:
        draws = jax.random.uniform(jax.random.fold_in(jax.random.fold_in(rng, 6), position), (parts,), jnp.float32, smallest / len(cuts), largest / len(cuts))
        factor_of = factor_of * jnp.repeat(jnp.exp(draws), extent[position] // parts).reshape((-1,) + (1,) * (len(extent) - 1 - position))
    return factor_of


def normal_values(stream_key, shape, width, reach, shards=(), kind=jnp.bfloat16):
    drawn = width * jax.random.normal(stream_key, shape, jnp.float32)
    if shards:
        drawn = drawn * block_scale(stream_key, shape, shards, -0.22, 0.18)
    return jnp.clip(drawn, -reach, reach).astype(kind)


def setup_inputs(seed: int = 0) -> dict:
    splits = jax.random.split(jax.random.key(seed), 9)
    inputs = normal_values(splits[0], (SEQS, LENGTH, D), 1.0, 6.0, ((0, 4), (1, 4), (2, 2)))
    output_grad = normal_values(splits[1], (SEQS, LENGTH, D), 1.0, 6.0, ((0, 4), (1, 4), (2, 2)))
    qkv_weight = normal_values(splits[2], (D, 3, H * DK), D ** -0.5, 0.125, ((2, 2),))
    out_weight = normal_values(splits[3], (D, H * DK), (H * DK) ** -0.5, 0.09375, ((1, 2),))
    down_weight = normal_values(splits[4], (D, RANK), D ** -0.5, 0.125)
    up_weight = normal_values(splits[5], (RANK, H * DK), RANK ** -0.5, 0.5, ((1, 2),))
    beta_weight = normal_values(splits[6], (D, H), D ** -0.5, 0.125, ((1, 2),))
    gate_bias = draw_gate_bias(jax.random.fold_in(splits[8], 71), 0)
    return dict(inputs=inputs, output_grad=output_grad, qkv_weight=qkv_weight, out_weight=out_weight, down_weight=down_weight, up_weight=up_weight, beta_weight=beta_weight, gate_bias=gate_bias)


epsilon = 1e-06
highest = lax.Precision.HIGHEST

def product(pattern, left, right):
    return jnp.einsum(pattern, left, right, precision=highest)

def dense(left, right):
    return jnp.dot(left.astype(jnp.float32), right.astype(jnp.float32), preferred_element_type=jnp.float32)

def activate(projected, gate_pre, beta_logit):
    token_count = projected.shape[0]
    head_count = beta_logit.shape[1]
    head_width = projected.shape[2] // head_count
    blocks = projected.reshape(token_count, 3, head_count, head_width)

    def normalize(values):
        return values * lax.rsqrt(lax.optimization_barrier(jnp.sum(values * values, axis=-1, keepdims=True)) + epsilon)
    queries = jnp.swapaxes(normalize(blocks[:, 0]), 0, 1)
    key_rows = jnp.swapaxes(normalize(blocks[:, 1]), 0, 1)
    value_rows = jnp.swapaxes(blocks[:, 2], 0, 1)
    decays = jnp.swapaxes((-0.25 * jax.nn.sigmoid(gate_pre)).reshape(token_count, head_count, head_width), 0, 1)
    betas = jnp.swapaxes(jax.nn.sigmoid(beta_logit), 0, 1)
    return (queries, key_rows, value_rows, decays, betas)

def span_terms(queries, key_rows, value_rows, decays, betas):
    leading = queries.shape[:-2]
    block_count = queries.shape[-2] // SPAN

    def blocked(member):
        return member.reshape(leading + (block_count, SPAN) + member.shape[-1:])
    queries, key_rows, value_rows, decays = (blocked(queries), blocked(key_rows), blocked(value_rows), blocked(decays))
    betas = betas.reshape(leading + (block_count, SPAN))
    cumulative = jnp.cumsum(decays, axis=-2)
    middle = cumulative[..., SPAN // 2 - 1:SPAN // 2, :]
    final_decay = cumulative[..., SPAN - 1:, :]
    key_fwd = jnp.exp(cumulative - middle) * key_rows
    key_back = jnp.exp(middle - cumulative) * key_rows
    query_fwd = jnp.exp(cumulative - middle) * queries
    key_start = jnp.exp(cumulative) * key_rows
    query_start = jnp.exp(cumulative) * queries
    key_end = jnp.exp(final_decay - cumulative) * key_rows
    row_index = lax.broadcasted_iota(jnp.int32, (SPAN, SPAN), 0)
    col_index = lax.broadcasted_iota(jnp.int32, (SPAN, SPAN), 1)
    strict = (row_index > col_index).astype(jnp.float32)
    lower_mask = (row_index >= col_index).astype(jnp.float32)
    coupling = betas[..., :, None] * product('...tc,...sc->...ts', key_fwd, key_back) * strict
    powers = -coupling
    inverse = jnp.eye(SPAN, dtype=jnp.float32) + powers
    for section in range(1, (SPAN - 1).bit_length()):
        powers = product('...ts,...su->...tu', powers, powers)
        inverse = inverse + product('...ts,...su->...tu', inverse, powers)
    solver = inverse * betas[..., None, :]
    solved_values = product('...ts,...sc->...tc', solver, value_rows)
    solved_keys = product('...ts,...sc->...tc', solver, key_start)
    scores = product('...tc,...sc->...ts', query_fwd, key_back) * lower_mask
    query_eff = query_start - product('...ts,...sc->...tc', scores, solved_keys)
    local_out = product('...ts,...sc->...tc', scores, solved_values)
    side = queries.shape[-1]
    diagonal = jnp.eye(side, dtype=jnp.float32) * jnp.exp(final_decay)[..., 0, :, None]
    transition = diagonal - product('...sc,...sd->...cd', key_end, solved_keys)
    offset = product('...sc,...sd->...cd', key_end, solved_values)
    return (query_eff, local_out, transition, offset)

def chain(terms, state_in):

    def advance(carried, pieces):
        query_eff, local_out, transition, offset = pieces
        emitted = product('...tc,...cd->...td', query_eff, carried) + local_out
        return (product('...cd,...de->...ce', transition, carried) + offset, emitted)
    moved = tuple((jnp.moveaxis(member, -3, 0) for member in terms))
    final_state, emitted = lax.scan(advance, state_in, moved)
    return (jnp.moveaxis(emitted, 0, -3), final_state)

def reference(inputs, output_grad, qkv_weight, out_weight, down_weight, up_weight, beta_weight, gate_bias):
    seq_count, seq_len, model_width = inputs.shape
    flat_in = inputs.reshape(-1, model_width)
    token_count = flat_in.shape[0]
    all_width = qkv_weight.shape[2]
    head_count = beta_weight.shape[1]
    head_width = all_width // head_count
    qkv_flat = qkv_weight.reshape(model_width, 3 * all_width)
    projected = dense(flat_in, qkv_flat).reshape(token_count, 3, all_width)
    low_rank = dense(flat_in, down_weight).astype(jnp.bfloat16)
    gate_pre = dense(low_rank, up_weight) + gate_bias
    beta_logit = dense(flat_in, beta_weight)
    acts, act_vjp = jax.vjp(activate, projected, gate_pre, beta_logit)

    def per_sequence(queries, key_rows, value_rows, decays, betas):
        shaped = [member.reshape((head_count, seq_count, seq_len) + member.shape[2:]) for member in (queries, key_rows, value_rows, decays, betas)]
        return span_terms(*shaped)
    terms, terms_vjp = jax.vjp(per_sequence, *acts)
    start_state = jnp.zeros((head_count, seq_count, head_width, head_width), jnp.float32)
    (mixed_blocks, final_state), chain_vjp = jax.vjp(chain, terms, start_state)
    mixed = jnp.transpose(mixed_blocks.reshape(head_count, seq_count, seq_len, head_width), (1, 2, 0, 3))
    mixed = mixed.reshape(token_count, all_width).astype(jnp.bfloat16)
    layer_out = dense(mixed, out_weight.T).astype(jnp.bfloat16).reshape(inputs.shape)
    flat_grad = output_grad.reshape(-1, model_width)
    mixed_grad = dense(flat_grad, out_weight)
    grad_blocks = jnp.transpose(mixed_grad.reshape(seq_count, seq_len, head_count, head_width), (2, 0, 1, 3))
    grad_blocks = grad_blocks.reshape(mixed_blocks.shape)
    term_grads, unused_state = chain_vjp((grad_blocks, jnp.zeros_like(final_state)))
    proj_grad, pre_grad, logit_grad = act_vjp(terms_vjp(term_grads))
    proj_low = proj_grad.astype(jnp.bfloat16).reshape(token_count, 3 * all_width)
    gate_low = pre_grad.astype(jnp.bfloat16)
    logit_low = logit_grad.astype(jnp.bfloat16)
    group_width = all_width // N_HEAD
    input_part = dense(proj_low, qkv_flat.T) + dense(logit_low, beta_weight.T)
    down_grad = jnp.zeros((model_width, down_weight.shape[1]), jnp.float32)
    for group in range(N_HEAD):
        low_grad = dense(gate_low[:, group * group_width:(group + 1) * group_width], up_weight[:, group * group_width:(group + 1) * group_width].T).astype(jnp.bfloat16)
        input_part = input_part + dense(low_grad, down_weight.T)
        down_grad = down_grad + dense(flat_in.T, low_grad)
    input_grad = input_part.astype(jnp.bfloat16).reshape(inputs.shape)
    block_total = token_count // TOK_DEV

    def block_rows(member):
        return member.reshape(block_total, TOK_DEV, member.shape[-1])
    stacked = (block_rows(flat_in), block_rows(proj_low), block_rows(flat_grad), block_rows(mixed))

    def accumulate(carried, pieces):
        input_rows, proj_rows, grad_rows, mixed_rows = pieces
        first = lax.optimization_barrier(dense(input_rows.T, proj_rows).astype(jnp.bfloat16)).astype(jnp.float32)
        second = lax.optimization_barrier(dense(grad_rows.T, mixed_rows).astype(jnp.bfloat16)).astype(jnp.float32)
        return ((carried[0] + first, carried[1] + second), None)
    start_sums = (jnp.zeros((model_width, 3 * all_width), jnp.float32), jnp.zeros((model_width, all_width), jnp.float32))
    (qkv_sum, out_sum), unused_rows = lax.scan(accumulate, start_sums, stacked)
    qkv_grad = qkv_sum.reshape(model_width, 3, all_width).astype(jnp.bfloat16)
    out_grad = out_sum.astype(jnp.bfloat16)
    up_grad = dense(low_rank.T, gate_low)
    beta_grad = dense(flat_in.T, logit_low)
    bias_grad = lax.optimization_barrier(jnp.sum(pre_grad, axis=0))
    return (layer_out, input_grad, qkv_grad, out_grad, up_grad, down_grad, beta_grad, bias_grad)
```

```python
import jax
import jax.numpy as jnp
from jax import lax
from jax.experimental import pallas as pl
from jax.experimental.pallas import tpu as pltpu
from jax.sharding import PartitionSpec as P

SPAN = 64
epsilon = 1e-06


def mm(left, right, left_dim, right_dim):
    return lax.dot_general(
        left.astype(jnp.bfloat16),
        right.astype(jnp.bfloat16),
        (((left_dim,), (right_dim,)), ((), ())),
        preferred_element_type=jnp.float32,
    )


def halves(value):
    high = value.astype(jnp.bfloat16)
    return high, (value - high.astype(jnp.float32)).astype(jnp.bfloat16)


def mask_mm(mask, value, mask_dim, value_dim):
    high, low = halves(value)
    return mm(mask, high, mask_dim, value_dim) + mm(mask, low, mask_dim, value_dim)


def square_mm(rows, square):
    row_high, row_low = halves(rows)
    high, low = halves(square)
    return mm(row_high, low, 1, 0) + mm(row_low, high, 1, 0) + mm(row_high, high, 1, 0)


def norm_of(values):
    return lax.rsqrt(jnp.sum(values * values, axis=-1, keepdims=True) + epsilon)


def recurrence_kernel(
    proj_ref, gate_ref, beta_ref, grad_ref,
    mixed_ref, proj_low_ref, gate_low_ref, logit_ref, bias_ref,
    state_ref, inverse_ref, scores_ref, coupling_ref, u_ref, carry_ref,
):
    heads, slots, width, _ = state_ref.shape
    blocks = slots - 1
    all_width = heads * width
    row_index = lax.broadcasted_iota(jnp.int32, (SPAN, SPAN), 0)
    col_index = lax.broadcasted_iota(jnp.int32, (SPAN, SPAN), 1)
    lower = row_index >= col_index
    strict = row_index > col_index
    eye = (row_index == col_index).astype(jnp.float32)
    lower_mask = lower.astype(jnp.bfloat16)
    ones = jnp.ones((SPAN, width), jnp.bfloat16)
    one_rows = jnp.ones((8, width), jnp.bfloat16)
    head_list = range(heads)

    def columns(head, part=0):
        return slice(part * all_width + head * width, part * all_width + (head + 1) * width)

    def prepare(rows):
        sig = lax.logistic(gate_ref[rows, :])
        decays = -0.25 * sig
        cumulative = mask_mm(lower_mask, decays, 1, 0)
        betas = lax.logistic(beta_ref[rows, :])
        made = []
        for head in head_list:
            cum = cumulative[:, columns(head)]
            query_raw = proj_ref[rows, columns(head, 0)]
            key_raw = proj_ref[rows, columns(head, 1)]
            query_norm, key_norm = norm_of(query_raw), norm_of(key_raw)
            queries, keys = query_raw * query_norm, key_raw * key_norm
            middle, final = cum[SPAN // 2 - 1 : SPAN // 2], cum[SPAN - 1 :]
            grow, back = jnp.exp(cum - middle), jnp.exp(middle - cum)
            start, end = jnp.exp(middle), jnp.exp(final - middle)
            key_fwd, key_back, query_fwd = grow * keys, back * keys, grow * queries
            made.append(dict(
                sig=sig[:, columns(head)],
                beta=betas[:, head : head + 1],
                queries=queries, keys=keys, query_norm=query_norm, key_norm=key_norm,
                grow=grow, back=back, start=start, end=end, final=final,
                key_fwd=key_fwd, key_back=key_back, query_fwd=query_fwd,
                key_start=key_fwd * start, query_start=query_fwd * start, key_end=key_back * end,
                decay=jnp.exp(sum(mm(half, ones, 0, 0) for half in halves(decays[:, columns(head)]))),
                values=proj_ref[rows, columns(head, 2)],
            ))
        return made

    def rows_of(block):
        return pl.ds(pl.multiple_of(block * SPAN, SPAN), SPAN)

    def forward(block, carried):
        rows = rows_of(block)
        made = prepare(rows)
        powers, inverses = [], []
        for head, it in enumerate(made):
            both = mm(jnp.concatenate([it["key_fwd"], it["query_fwd"]], axis=0), it["key_back"], 1, 1)
            coupling = jnp.where(strict, both[:SPAN], 0.0)
            scores = jnp.where(lower, both[SPAN:], 0.0)
            coupling_ref[head, block] = coupling
            scores_ref[head, block] = scores.astype(jnp.bfloat16)
            power = -it["beta"] * coupling
            powers.append(power)
            inverses.append(eye + power)
        powers = [square_mm(power, power) for power in powers]
        for section in range(2, (SPAN - 1).bit_length()):
            stacked = [
                square_mm(jnp.concatenate([inverse, power], axis=0), power)
                for inverse, power in zip(inverses, powers)
            ]
            inverses = [inverse + both[:SPAN] for inverse, both in zip(inverses, stacked)]
            powers = [both[SPAN:] for both in stacked]
        inverses = [inverse + square_mm(inverse, power) for inverse, power in zip(inverses, powers)]
        for head in head_list:
            inverse_ref[head, block] = inverses[head].astype(jnp.bfloat16)
        froms = [
            mm(jnp.concatenate([it["key_start"], it["query_start"]], axis=0), state_ref[head, block], 1, 0)
            for head, it in enumerate(made)
        ]
        us = [
            mm(inverse, it["beta"] * (it["values"] - both[:SPAN]), 1, 0)
            for inverse, it, both in zip(inverses, made, froms)
        ]
        for head, it in enumerate(made):
            state_ref[head, block + 1] = it["decay"] * state_ref[head, block] + mm(
                it["key_end"], us[head], 0, 0
            )
            u_ref[head, block] = us[head].astype(jnp.bfloat16)
            mixed = froms[head][SPAN:] + mm(scores_ref[head, block], us[head], 1, 0)
            mixed_ref[rows, columns(head)] = mixed.astype(jnp.bfloat16)
        return carried

    def backward(step, carried):
        block = blocks - 1 - step
        rows = rows_of(block)
        made = prepare(rows)
        grads = [grad_ref[rows, columns(head)] for head in head_list]
        dus = [
            mm(scores_ref[head, block], grads[head], 0, 0) + mm(it["key_end"], carry_ref[head], 1, 0)
            for head, it in enumerate(made)
        ]
        drs = [mm(inverse_ref[head, block], dus[head], 0, 0) for head in head_list]
        logits = jnp.zeros((SPAN, heads), jnp.float32)
        head_index = lax.broadcasted_iota(jnp.int32, (SPAN, heads), 1)
        for head, it in enumerate(made):
            beta, dr, out_grad = it["beta"], drs[head], grads[head]
            state, carry, u = state_ref[head, block], carry_ref[head], u_ref[head, block]
            scaled = beta * dr
            pair = jnp.concatenate([out_grad, -dr], axis=0)
            both = mm(pair, u, 1, 1)
            scores_grad = jnp.where(lower, both[:SPAN], 0.0)
            inner_grad = jnp.where(strict, both[SPAN:], 0.0)
            pair = jnp.concatenate([out_grad, -scaled], axis=0)
            both = mm(pair, state, 1, 1)
            query_start_grad, key_start_grad = both[:SPAN], both[SPAN:]
            key_end_grad = mm(u, carry, 1, 1)
            carry_ref[head] = it["decay"] * carry + mm(
                jnp.concatenate([it["query_start"], it["key_start"]], axis=0), pair, 0, 0
            )
            rest = it["values"] - mm(it["key_start"], state, 1, 0)
            beta_grad = jnp.sum(dr * rest, axis=1, keepdims=True) + jnp.sum(
                inner_grad * coupling_ref[head, block], axis=1, keepdims=True
            )
            square_grads = jnp.concatenate([scores_grad, beta * inner_grad], axis=0)
            both = mm(square_grads, it["key_back"], 1, 0)
            query_fwd_grad, key_fwd_grad = both[:SPAN], both[SPAN:]
            key_back_grad = mm(
                square_grads, jnp.concatenate([it["query_fwd"], it["key_fwd"]], axis=0), 0, 0
            )
            end_term = it["key_end"] * key_end_grad
            query_grow = query_fwd_grad + it["start"] * query_start_grad
            key_grow = key_fwd_grad + it["start"] * key_start_grad
            key_decay = key_back_grad + it["end"] * key_end_grad
            cum_grad = (
                it["query_fwd"] * query_grow + it["key_fwd"] * key_grow - it["key_back"] * key_decay
            )
            final_grad = jnp.sum(end_term, axis=0, keepdims=True) + jnp.exp(it["final"]) * mask_mm(
                one_rows, state * carry, 1, 1
            )[:1]
            decay_grad = mask_mm(lower_mask, cum_grad, 0, 0) + final_grad
            sig = it["sig"]
            gate_grad = decay_grad * (-0.25 * sig * (1.0 - sig))
            query_grad = it["grow"] * query_grow
            key_grad = it["grow"] * key_grow + it["back"] * key_decay

            def through_norm(values, inverse_norm, grad):
                return inverse_norm * (grad - values * jnp.sum(values * grad, axis=1, keepdims=True))

            parts = (
                through_norm(it["queries"], it["query_norm"], query_grad),
                through_norm(it["keys"], it["key_norm"], key_grad),
                scaled,
            )
            for part, value in enumerate(parts):
                proj_low_ref[rows, columns(head, part)] = value.astype(jnp.bfloat16)
            gate_low_ref[rows, columns(head)] = gate_grad.astype(jnp.bfloat16)
            bias_ref[:, columns(head)] += jnp.sum(gate_grad, axis=0, keepdims=True)
            logits = jnp.where(head_index == head, beta_grad * beta * (1.0 - beta), logits)
        logit_ref[rows, :] = logits
        return carried

    for head in head_list:
        state_ref[head, 0] = jnp.zeros((width, width), jnp.float32)
        carry_ref[head] = jnp.zeros((width, width), jnp.float32)
    bias_ref[...] = jnp.zeros_like(bias_ref)
    lax.fori_loop(0, blocks, forward, 0)
    lax.fori_loop(0, blocks, backward, 0)


def recurrence(projected, gate_pre, beta_logit, mixed_grad):
    tokens, all_width = gate_pre.shape
    heads = beta_logit.shape[1]
    width = all_width // heads
    blocks = tokens // SPAN
    vmem = pl.BlockSpec(memory_space=pltpu.VMEM)
    return pl.pallas_call(
        recurrence_kernel,
        in_specs=[vmem] * 4,
        out_specs=[vmem] * 5,
        out_shape=[
            jax.ShapeDtypeStruct((tokens, all_width), jnp.bfloat16),
            jax.ShapeDtypeStruct((tokens, 3 * all_width), jnp.bfloat16),
            jax.ShapeDtypeStruct((tokens, all_width), jnp.bfloat16),
            jax.ShapeDtypeStruct((tokens, heads), jnp.float32),
            jax.ShapeDtypeStruct((1, all_width), jnp.float32),
        ],
        scratch_shapes=[
            pltpu.VMEM((heads, blocks + 1, width, width), jnp.float32),
            pltpu.VMEM((heads, blocks, SPAN, SPAN), jnp.bfloat16),
            pltpu.VMEM((heads, blocks, SPAN, SPAN), jnp.bfloat16),
            pltpu.VMEM((heads, blocks, SPAN, SPAN), jnp.float32),
            pltpu.VMEM((heads, blocks, SPAN, width), jnp.bfloat16),
            pltpu.VMEM((heads, width, width), jnp.float32),
        ],
        compiler_params=pltpu.CompilerParams(vmem_limit_bytes=40 * 1024 * 1024),
    )(projected, gate_pre, beta_logit, mixed_grad)


def shards(
    inputs, output_grad, qkv_weight, out_weight, down_weight, up_weight, beta_weight, gate_bias
):
    count = lax.axis_size("context")
    member = lax.axis_index("context")
    f32 = jnp.float32

    def gather(block):
        whole = lax.all_gather(block[0], "context", axis=0, tiled=True)
        return lax.all_gather(whole, "head", axis=1, tiled=True)

    def own(array, axis):
        size = array.shape[axis] // count
        return lax.dynamic_slice_in_dim(array, member * size, size, axis=axis)

    rows_in, rows_grad = gather(inputs), gather(output_grad)
    tokens, model_width = rows_in.shape
    own_qkv = own(jnp.transpose(qkv_weight, (1, 0, 2)), 2)
    own_out = own(out_weight, 1)
    own_up = own(up_weight, 1)
    own_beta = own(beta_weight, 1)
    own_bias = own(gate_bias, 0)
    heads = own_beta.shape[1]
    all_width = own_up.shape[1]
    projected = jnp.concatenate(
        [jnp.dot(rows_in, own_qkv[part], preferred_element_type=f32) for part in range(3)], axis=1
    )
    low_rank = jnp.dot(rows_in, down_weight, preferred_element_type=f32).astype(jnp.bfloat16)
    gate_pre = jnp.dot(low_rank, own_up, preferred_element_type=f32) + own_bias
    beta_logit = jnp.dot(rows_in, own_beta, preferred_element_type=f32)
    mixed_grad = jnp.dot(rows_grad, own_out, preferred_element_type=f32)
    mixed, proj_low, gate_low, logit_grad, bias_term = recurrence(
        projected, gate_pre, beta_logit, mixed_grad
    )
    mixed_own = lax.all_to_all(mixed, "context", 0, 1, tiled=True)
    out_part = jnp.einsum("tc,dc->td", mixed_own, out_weight, preferred_element_type=f32)
    layer_out = lax.psum_scatter(
        out_part.astype(jnp.bfloat16), "head", scatter_dimension=1, tiled=True
    )[None]
    logit_low = logit_grad.astype(jnp.bfloat16)
    low_grad = jnp.einsum("tc,rc->tr", gate_low, own_up, preferred_element_type=f32)
    low_grad = low_grad.astype(jnp.bfloat16)
    input_part = jnp.einsum("tr,dr->td", low_grad, down_weight, preferred_element_type=f32)
    input_part += jnp.einsum("th,dh->td", logit_low, own_beta, preferred_element_type=f32)
    for part in range(3):
        input_part += jnp.einsum(
            "tc,dc->td",
            proj_low[:, part * all_width : (part + 1) * all_width],
            own_qkv[part],
            preferred_element_type=f32,
        )
    input_grad = lax.psum_scatter(
        input_part.astype(jnp.bfloat16), "head", scatter_dimension=1, tiled=True
    )
    input_grad = lax.psum_scatter(input_grad, "context", scatter_dimension=0, tiled=True)[None]

    def weight_term(rows, columns):
        term = jnp.einsum("tr,tc->rc", rows, columns, preferred_element_type=f32)
        return term.astype(jnp.bfloat16)

    dp_count = lax.axis_size("dp")
    term = jnp.concatenate([weight_term(rows_in, proj_low), weight_term(rows_grad, mixed)], axis=1)
    slab = model_width // (count * dp_count)
    term = term.reshape(count, dp_count, slab, 4 * all_width)
    term = lax.psum_scatter(term, "dp", scatter_dimension=1)
    term = lax.all_to_all(term, "context", 0, 0, tiled=True)
    term = jnp.transpose(term.reshape(count, slab, 4, all_width), (2, 1, 0, 3))
    term = term.reshape(4, slab, count * all_width)
    qkv_grad = jnp.transpose(term[:3], (1, 0, 2))
    out_grad = term[3]

    up_term = jnp.einsum("tr,tc->rc", low_rank, gate_low, preferred_element_type=f32)
    beta_term = jnp.einsum("td,th->dh", rows_in, logit_low, preferred_element_type=f32)
    down_term = jnp.einsum("td,tr->dr", rows_in, low_grad, preferred_element_type=f32)
    small = [up_term, beta_term, bias_term]
    packed = jnp.concatenate([term.reshape(-1, 128) for term in small], axis=0)
    packed = lax.psum(packed.astype(jnp.bfloat16), "dp")
    packed = lax.all_gather(packed, "context").astype(f32)
    results, start = [], 0
    for term in small:
        length = term.size // 128
        whole = packed[:, start : start + length].reshape((count,) + term.shape)
        results.append(jnp.transpose(whole, (1, 0, 2)).reshape(term.shape[0], -1))
        start += length
    up_grad, beta_grad, bias_grad = results
    down_grad = lax.psum(lax.psum(down_term.astype(jnp.bfloat16), ("context", "dp")).astype(f32), "head")
    return (layer_out, input_grad, qkv_grad, out_grad, up_grad, down_grad, beta_grad, bias_grad[0])


def solution(mesh):
    return jax.shard_map(
        shards,
        mesh=mesh,
        in_specs=(
            P("dp", "context", "head"),
            P("dp", "context", "head"),
            P(None, None, "head"),
            P(None, "head"),
            P(),
            P(None, "head"),
            P(None, "head"),
            P("head"),
        ),
        out_specs=(
            P("dp", "context", "head"),
            P("dp", "context", "head"),
            P(("context", "dp"), None, "head"),
            P(("context", "dp"), "head"),
            P(None, "head"),
            P(),
            P(None, "head"),
            P("head"),
        ),
        check_vma=False,
    )
```

```python
import jax
import jax.numpy as jnp
from jax import lax
from jax.experimental import pallas as pl
from jax.experimental.pallas import tpu as pltpu
from jax.sharding import PartitionSpec as P

SPAN = 64
epsilon = 1e-06


def mm(left, right, left_dim, right_dim):
    return lax.dot_general(
        left.astype(jnp.bfloat16),
        right.astype(jnp.bfloat16),
        (((left_dim,), (right_dim,)), ((), ())),
        preferred_element_type=jnp.float32,
    )


def halves(value):
    high = value.astype(jnp.bfloat16)
    return high, (value - high.astype(jnp.float32)).astype(jnp.bfloat16)


def mask_mm(mask, value, mask_dim, value_dim):
    high, low = halves(value)
    return mm(mask, high, mask_dim, value_dim) + mm(mask, low, mask_dim, value_dim)


def square_mm(rows, square):
    row_high, row_low = halves(rows)
    high, low = halves(square)
    return mm(row_high, low, 1, 0) + mm(row_low, high, 1, 0) + mm(row_high, high, 1, 0)


def norm_of(values):
    return lax.rsqrt(jnp.sum(values * values, axis=-1, keepdims=True) + epsilon)


def recurrence_kernel(
    proj_ref, gate_ref, beta_ref, grad_ref,
    mixed_ref, proj_low_ref, gate_low_ref, logit_ref, bias_ref,
    state_ref, inverse_ref, scores_ref, coupling_ref, u_ref, carry_ref,
):
    heads, slots, width, _ = state_ref.shape
    blocks = slots - 1
    all_width = heads * width
    row_index = lax.broadcasted_iota(jnp.int32, (SPAN, SPAN), 0)
    col_index = lax.broadcasted_iota(jnp.int32, (SPAN, SPAN), 1)
    lower = row_index >= col_index
    strict = row_index > col_index
    eye = (row_index == col_index).astype(jnp.float32)
    lower_mask = lower.astype(jnp.bfloat16)
    ones = jnp.ones((SPAN, width), jnp.bfloat16)
    one_rows = jnp.ones((8, width), jnp.bfloat16)
    head_list = range(heads)

    def columns(head, part=0):
        return slice(part * all_width + head * width, part * all_width + (head + 1) * width)

    def prepare(rows):
        sig = lax.logistic(gate_ref[rows, :])
        decays = -0.25 * sig
        cumulative = mask_mm(lower_mask, decays, 1, 0)
        betas = lax.logistic(beta_ref[rows, :])
        made = []
        for head in head_list:
            cum = cumulative[:, columns(head)]
            query_raw = proj_ref[rows, columns(head, 0)]
            key_raw = proj_ref[rows, columns(head, 1)]
            query_norm, key_norm = norm_of(query_raw), norm_of(key_raw)
            queries, keys = query_raw * query_norm, key_raw * key_norm
            middle, final = cum[SPAN // 2 - 1 : SPAN // 2], cum[SPAN - 1 :]
            grow, back = jnp.exp(cum - middle), jnp.exp(middle - cum)
            start, end = jnp.exp(middle), jnp.exp(final - middle)
            key_fwd, key_back, query_fwd = grow * keys, back * keys, grow * queries
            made.append(dict(
                sig=sig[:, columns(head)],
                beta=betas[:, head : head + 1],
                queries=queries, keys=keys, query_norm=query_norm, key_norm=key_norm,
                grow=grow, back=back, start=start, end=end, final=final,
                key_fwd=key_fwd, key_back=key_back, query_fwd=query_fwd,
                key_start=key_fwd * start, query_start=query_fwd * start, key_end=key_back * end,
                decay=jnp.exp(sum(mm(half, ones, 0, 0) for half in halves(decays[:, columns(head)]))),
                values=proj_ref[rows, columns(head, 2)],
            ))
        return made

    def rows_of(block):
        return pl.ds(pl.multiple_of(block * SPAN, SPAN), SPAN)

    def forward(block, carried):
        rows = rows_of(block)
        made = prepare(rows)
        powers, inverses = [], []
        for head, it in enumerate(made):
            both = mm(jnp.concatenate([it["key_fwd"], it["query_fwd"]], axis=0), it["key_back"], 1, 1)
            coupling = jnp.where(strict, both[:SPAN], 0.0)
            scores = jnp.where(lower, both[SPAN:], 0.0)
            coupling_ref[head, block] = coupling
            scores_ref[head, block] = scores.astype(jnp.bfloat16)
            power = -it["beta"] * coupling
            powers.append(power)
            inverses.append(eye + power)
        powers = [square_mm(power, power) for power in powers]
        for section in range(2, (SPAN - 1).bit_length()):
            stacked = [
                square_mm(jnp.concatenate([inverse, power], axis=0), power)
                for inverse, power in zip(inverses, powers)
            ]
            inverses = [inverse + both[:SPAN] for inverse, both in zip(inverses, stacked)]
            powers = [both[SPAN:] for both in stacked]
        inverses = [inverse + square_mm(inverse, power) for inverse, power in zip(inverses, powers)]
        for head in head_list:
            inverse_ref[head, block] = inverses[head].astype(jnp.bfloat16)
        froms = [
            mm(jnp.concatenate([it["key_start"], it["query_start"]], axis=0), state_ref[head, block], 1, 0)
            for head, it in enumerate(made)
        ]
        us = [
            mm(inverse, it["beta"] * (it["values"] - both[:SPAN]), 1, 0)
            for inverse, it, both in zip(inverses, made, froms)
        ]
        for head, it in enumerate(made):
            state_ref[head, block + 1] = it["decay"] * state_ref[head, block] + mm(
                it["key_end"], us[head], 0, 0
            )
            u_ref[head, block] = us[head].astype(jnp.bfloat16)
            mixed = froms[head][SPAN:] + mm(scores_ref[head, block], us[head], 1, 0)
            mixed_ref[rows, columns(head)] = mixed.astype(jnp.bfloat16)
        return carried

    def backward(step, carried):
        block = blocks - 1 - step
        rows = rows_of(block)
        made = prepare(rows)
        grads = [grad_ref[rows, columns(head)] for head in head_list]
        dus = [
            mm(scores_ref[head, block], grads[head], 0, 0) + mm(it["key_end"], carry_ref[head], 1, 0)
            for head, it in enumerate(made)
        ]
        drs = [mm(inverse_ref[head, block], dus[head], 0, 0) for head in head_list]
        logits = jnp.zeros((SPAN, heads), jnp.float32)
        head_index = lax.broadcasted_iota(jnp.int32, (SPAN, heads), 1)
        for head, it in enumerate(made):
            beta, dr, out_grad = it["beta"], drs[head], grads[head]
            state, carry, u = state_ref[head, block], carry_ref[head], u_ref[head, block]
            scaled = beta * dr
            pair = jnp.concatenate([out_grad, -dr], axis=0)
            both = mm(pair, u, 1, 1)
            scores_grad = jnp.where(lower, both[:SPAN], 0.0)
            inner_grad = jnp.where(strict, both[SPAN:], 0.0)
            pair = jnp.concatenate([out_grad, -scaled], axis=0)
            both = mm(pair, state, 1, 1)
            query_start_grad, key_start_grad = both[:SPAN], both[SPAN:]
            key_end_grad = mm(u, carry, 1, 1)
            carry_ref[head] = it["decay"] * carry + mm(
                jnp.concatenate([it["query_start"], it["key_start"]], axis=0), pair, 0, 0
            )
            rest = it["values"] - mm(it["key_start"], state, 1, 0)
            beta_grad = jnp.sum(dr * rest, axis=1, keepdims=True) + jnp.sum(
                inner_grad * coupling_ref[head, block], axis=1, keepdims=True
            )
            square_grads = jnp.concatenate([scores_grad, beta * inner_grad], axis=0)
            both = mm(square_grads, it["key_back"], 1, 0)
            query_fwd_grad, key_fwd_grad = both[:SPAN], both[SPAN:]
            key_back_grad = mm(
                square_grads, jnp.concatenate([it["query_fwd"], it["key_fwd"]], axis=0), 0, 0
            )
            end_term = it["key_end"] * key_end_grad
            query_grow = query_fwd_grad + it["start"] * query_start_grad
            key_grow = key_fwd_grad + it["start"] * key_start_grad
            key_decay = key_back_grad + it["end"] * key_end_grad
            cum_grad = (
                it["query_fwd"] * query_grow + it["key_fwd"] * key_grow - it["key_back"] * key_decay
            )
            final_grad = jnp.sum(end_term, axis=0, keepdims=True) + jnp.exp(it["final"]) * mask_mm(
                one_rows, state * carry, 1, 1
            )[:1]
            decay_grad = mask_mm(lower_mask, cum_grad, 0, 0) + final_grad
            sig = it["sig"]
            gate_grad = decay_grad * (-0.25 * sig * (1.0 - sig))
            query_grad = it["grow"] * query_grow
            key_grad = it["grow"] * key_grow + it["back"] * key_decay

            def through_norm(values, inverse_norm, grad):
                return inverse_norm * (grad - values * jnp.sum(values * grad, axis=1, keepdims=True))

            parts = (
                through_norm(it["queries"], it["query_norm"], query_grad),
                through_norm(it["keys"], it["key_norm"], key_grad),
                scaled,
            )
            for part, value in enumerate(parts):
                proj_low_ref[rows, columns(head, part)] = value.astype(jnp.bfloat16)
            gate_low_ref[rows, columns(head)] = gate_grad.astype(jnp.bfloat16)
            bias_ref[:, columns(head)] += jnp.sum(gate_grad, axis=0, keepdims=True)
            logits = jnp.where(head_index == head, beta_grad * beta * (1.0 - beta), logits)
        logit_ref[rows, :] = logits
        return carried

    for head in head_list:
        state_ref[head, 0] = jnp.zeros((width, width), jnp.float32)
        carry_ref[head] = jnp.zeros((width, width), jnp.float32)
    bias_ref[...] = jnp.zeros_like(bias_ref)
    lax.fori_loop(0, blocks, forward, 0)
    lax.fori_loop(0, blocks, backward, 0)


def recurrence(projected, gate_pre, beta_logit, mixed_grad):
    tokens, all_width = gate_pre.shape
    heads = beta_logit.shape[1]
    width = all_width // heads
    blocks = tokens // SPAN
    vmem = pl.BlockSpec(memory_space=pltpu.VMEM)
    return pl.pallas_call(
        recurrence_kernel,
        in_specs=[vmem] * 4,
        out_specs=[vmem] * 5,
        out_shape=[
            jax.ShapeDtypeStruct((tokens, all_width), jnp.bfloat16),
            jax.ShapeDtypeStruct((tokens, 3 * all_width), jnp.bfloat16),
            jax.ShapeDtypeStruct((tokens, all_width), jnp.bfloat16),
            jax.ShapeDtypeStruct((tokens, heads), jnp.float32),
            jax.ShapeDtypeStruct((1, all_width), jnp.float32),
        ],
        scratch_shapes=[
            pltpu.VMEM((heads, blocks + 1, width, width), jnp.float32),
            pltpu.VMEM((heads, blocks, SPAN, SPAN), jnp.bfloat16),
            pltpu.VMEM((heads, blocks, SPAN, SPAN), jnp.bfloat16),
            pltpu.VMEM((heads, blocks, SPAN, SPAN), jnp.float32),
            pltpu.VMEM((heads, blocks, SPAN, width), jnp.bfloat16),
            pltpu.VMEM((heads, width, width), jnp.float32),
        ],
        compiler_params=pltpu.CompilerParams(vmem_limit_bytes=40 * 1024 * 1024),
    )(projected, gate_pre, beta_logit, mixed_grad)

MESH = pl.DeviceIdType.MESH


def exchange_kernel(
    rows_ref, grads_ref, proj_ref, mixed_ref, part_ref, layer_ref,
    qkv_ref, out_ref, input_ref, layer_out_ref,
    keep, send_one, recv_one, send_two, recv_two, done_rows,
    head_recv, part_send, part_recv, layer_recv,
    one_send, one_recv, two_send, two_recv, far_send, far_recv, local_sem,
    head_send_sem, head_recv_sem, part_send_sem, part_recv_sem, layer_send_sem, layer_recv_sem,
):
    count, width = rows_ref.shape[0], mixed_ref.shape[1]
    groups = part_ref.shape[0]
    slab = rows_ref.shape[2]
    member, row, group = (lax.axis_index(name) for name in ("context", "dp", "head"))
    near = row + 1 - 2 * lax.rem(row, 2)
    across = lax.rem(row + 2, 4)
    opposite = 3 - row

    def peer(axis, index):
        return {axis: index}

    def context_at(offset):
        return lax.rem(member + offset, count)

    def head_at(offset):
        return lax.rem(group + offset, groups)

    barrier = pltpu.get_barrier_semaphore()
    peers = [peer("context", context_at(offset)) for offset in range(1, count)]
    peers += [peer("head", head_at(offset)) for offset in range(1, groups)]
    peers += [peer("dp", near), peer("dp", across)]
    for target in peers:
        pl.semaphore_signal(barrier, inc=1, device_id=target, device_id_type=MESH)
    pl.semaphore_wait(barrier, len(peers))

    offsets = sorted(range(1, count), key=lambda k: -min(k, count - k)) + [0]

    def remote(source, target, send_sem, recv_sem, device):
        return pltpu.make_async_remote_copy(
            src_ref=source, dst_ref=target, send_sem=send_sem, recv_sem=recv_sem,
            device_id=device, device_id_type=MESH,
        )

    def layer_copy(offset):
        return remote(
            layer_ref.at[head_at(offset)], layer_recv.at[offset],
            layer_send_sem.at[offset], layer_recv_sem.at[offset], peer("head", head_at(offset)),
        )

    def head_copy(step, offset):
        return remote(
            part_ref.at[head_at(offset), context_at(offsets[step])], head_recv.at[offset, step],
            head_send_sem.at[offset, step], head_recv_sem.at[offset, step],
            peer("head", head_at(offset)),
        )

    for offset in range(1, groups):
        layer_copy(offset).start()
    for step in range(count):
        for offset in range(1, groups):
            head_copy(step, offset).start()

    def one_copy(step):
        return remote(
            send_one.at[step], recv_one.at[step], one_send.at[step], one_recv.at[step],
            peer("dp", near),
        )

    def two_copy(step):
        return remote(
            send_two.at[step], recv_two.at[step], two_send.at[step], two_recv.at[step],
            peer("dp", across),
        )

    def owner_ref(part, index):
        columns = pl.ds(pl.multiple_of(index * width, width), width)
        return out_ref.at[:, columns] if part == 3 else qkv_ref.at[part, :, columns]

    def far_copy(step, part):
        offset = offsets[step]
        return remote(
            done_rows.at[step, :, pl.ds(part * width, width)], owner_ref(part, member),
            far_send.at[step, part], far_recv.at[offset, part], peer("context", context_at(offset)),
        )

    def far_arrival(offset, part):
        source = lax.rem(member + count - offset, count)
        return remote(
            done_rows.at[0, :, pl.ds(part * width, width)], owner_ref(part, source),
            far_send.at[0, part], far_recv.at[offset, part], peer("context", source),
        )

    def part_copy(step):
        offset = offsets[step]
        return remote(
            part_send.at[step], part_recv.at[offset],
            part_send_sem.at[step], part_recv_sem.at[offset], peer("context", context_at(offset)),
        )

    def products(step, targets):
        chosen = context_at(offsets[step])

        def fill(part, carried):
            columns = pl.ds(pl.multiple_of(part * width, width), width)
            for index, store in targets:
                value = jnp.dot(
                    rows_ref[chosen, index], proj_ref[:, columns], preferred_element_type=jnp.float32
                )
                store(columns, value)
            return carried

        lax.fori_loop(0, 3, fill, 0)
        columns = pl.ds(3 * width, width)
        for index, store in targets:
            value = jnp.dot(
                grads_ref[chosen, index], mixed_ref[...], preferred_element_type=jnp.float32
            )
            store(columns, value)

    def sender(step, slot):
        def store(columns, value):
            send_one[step, slot, :, columns] = value.astype(jnp.bfloat16)

        return store

    def keeper(step, slot):
        def store(columns, value):
            keep[step % 3, slot, :, columns] = value

        return store

    def over_columns(body):
        def one(part, carried):
            body(pl.ds(pl.multiple_of(part * width, width), width))
            return carried

        lax.fori_loop(0, 4, one, 0)

    def first(step):
        products(step, [(near, sender(step, 0)), (opposite, sender(step, 1))])
        one_copy(step).start()
        products(step, [(row, keeper(step, 0)), (across, keeper(step, 1))])

    def second(step):
        one_copy(step).wait_recv()

        def add(columns):
            send_two[step, :, columns] = (
                keep[step % 3, 1, :, columns] + recv_one[step, 1, :, columns].astype(jnp.float32)
            ).astype(jnp.bfloat16)

        over_columns(add)
        two_copy(step).start()

    def third(step):
        two_copy(step).wait_recv()

        def add(columns):
            done_rows[step, :, columns] = (
                keep[step % 3, 0, :, columns]
                + recv_one[step, 0, :, columns].astype(jnp.float32)
                + recv_two[step, :, columns].astype(jnp.float32)
            ).astype(jnp.bfloat16)

        over_columns(add)
        for part in range(4):
            if offsets[step]:
                far_copy(step, part).start()
            else:
                own_copy(step, part).start()

    def own_copy(step, part):
        return pltpu.make_async_copy(
            done_rows.at[step, :, pl.ds(part * width, width)], owner_ref(part, member),
            local_sem.at[part],
        )

    def partial(step):
        for offset in range(1, groups):
            head_copy(step, offset).wait_recv()
        total = part_ref[group, context_at(offsets[step])].astype(jnp.float32)
        for offset in range(1, groups):
            total = total + head_recv[offset, step].astype(jnp.float32)
        part_send[step] = total.astype(jnp.bfloat16)
        if offsets[step]:
            part_copy(step).start()

    for step in range(count + 2):
        if step < count:
            first(step)
        if 0 <= step - 1 < count:
            second(step - 1)
        if step < count:
            partial(step)
        if step >= 2:
            third(step - 2)

    for offset in range(1, groups):
        layer_copy(offset).wait_recv()
    total = layer_ref[group].astype(jnp.float32)
    for offset in range(1, groups):
        total = total + layer_recv[offset].astype(jnp.float32)
    layer_out_ref[...] = total.astype(jnp.bfloat16)
    total = part_send[count - 1].astype(jnp.float32)
    for step in range(count - 1):
        offset = offsets[step]
        part_copy(step).wait_recv()
        total = total + part_recv[offset].astype(jnp.float32)
    input_ref[...] = total.astype(jnp.bfloat16)
    for step in range(count - 1):
        for part in range(4):
            far_arrival(offsets[step], part).wait_recv()
    for part in range(4):
        own_copy(count - 1, part).wait()
    for step in range(count):
        one_copy(step).wait_send()
        two_copy(step).wait_send()
        for offset in range(1, groups):
            head_copy(step, offset).wait_send()
        if offsets[step]:
            part_copy(step).wait_send()
            for part in range(4):
                far_copy(step, part).wait_send()
    for offset in range(1, groups):
        layer_copy(offset).wait_send()


def exchange(rows, grads, proj_low, mixed, parts, layer_parts):
    count, _, slab, tokens = rows.shape
    width = mixed.shape[1]
    groups, _, block, features = parts.shape
    bf16 = jnp.bfloat16
    vmem = pl.BlockSpec(memory_space=pltpu.VMEM)
    hbm = pl.BlockSpec(memory_space=pl.ANY)
    dma = pltpu.SemaphoreType.DMA
    return pl.pallas_call(
        exchange_kernel,
        in_specs=[vmem] * 6,
        out_specs=[hbm, hbm, vmem, vmem],
        out_shape=[
            jax.ShapeDtypeStruct((3, slab, count * width), bf16),
            jax.ShapeDtypeStruct((slab, count * width), bf16),
            jax.ShapeDtypeStruct((block, features), bf16),
            jax.ShapeDtypeStruct((block, features), bf16),
        ],
        scratch_shapes=[
            pltpu.VMEM((3, 2, slab, 4 * width), jnp.float32),
            pltpu.VMEM((count, 2, slab, 4 * width), bf16),
            pltpu.VMEM((count, 2, slab, 4 * width), bf16),
            pltpu.VMEM((count, slab, 4 * width), bf16),
            pltpu.VMEM((count, slab, 4 * width), bf16),
            pltpu.VMEM((count, slab, 4 * width), bf16),
            pltpu.VMEM((groups, count, block, features), bf16),
            pltpu.VMEM((count, block, features), bf16),
            pltpu.VMEM((count, block, features), bf16),
            pltpu.VMEM((groups, block, features), bf16),
            dma((count,)), dma((count,)), dma((count,)), dma((count,)),
            dma((count, 4)), dma((count, 4)), dma((4,)),
            dma((groups, count)), dma((groups, count)),
            dma((count,)), dma((count,)),
            dma((groups,)), dma((groups,)),
        ],
        compiler_params=pltpu.CompilerParams(
            collective_id=1, has_side_effects=True, vmem_limit_bytes=56 * 1024 * 1024
        ),
    )(rows, grads, proj_low, mixed, parts, layer_parts)


def shards(
    inputs, output_grad, qkv_weight, out_weight, down_weight, up_weight, beta_weight, gate_bias
):
    count = lax.axis_size("context")
    member = lax.axis_index("context")
    f32 = jnp.float32

    def gather(block):
        whole = lax.all_gather(block[0], "context", axis=0, tiled=True)
        return lax.all_gather(whole, "head", axis=1, tiled=True)

    def own(array, axis):
        size = array.shape[axis] // count
        return lax.dynamic_slice_in_dim(array, member * size, size, axis=axis)

    rows_in, rows_grad = gather(inputs), gather(output_grad)
    tokens, model_width = rows_in.shape
    own_qkv = own(jnp.transpose(qkv_weight, (1, 0, 2)), 2)
    own_out = own(out_weight, 1)
    own_up = own(up_weight, 1)
    own_beta = own(beta_weight, 1)
    own_bias = own(gate_bias, 0)
    heads = own_beta.shape[1]
    all_width = own_up.shape[1]
    projected = jnp.concatenate(
        [jnp.dot(rows_in, own_qkv[part], preferred_element_type=f32) for part in range(3)], axis=1
    )
    low_rank = jnp.dot(rows_in, down_weight, preferred_element_type=f32).astype(jnp.bfloat16)
    gate_pre = jnp.dot(low_rank, own_up, preferred_element_type=f32) + own_bias
    beta_logit = jnp.dot(rows_in, own_beta, preferred_element_type=f32)
    mixed_grad = jnp.dot(rows_grad, own_out, preferred_element_type=f32)
    mixed, proj_low, gate_low, logit_grad, bias_term = recurrence(
        projected, gate_pre, beta_logit, mixed_grad
    )
    mixed_own = lax.all_to_all(mixed, "context", 0, 1, tiled=True)
    out_part = jnp.einsum("tc,dc->td", mixed_own, out_weight, preferred_element_type=f32)
    groups = lax.axis_size("head")

    def by_group(value):
        whole = value.astype(jnp.bfloat16).reshape(value.shape[0], groups, -1)
        return jnp.transpose(whole, (1, 0, 2))

    logit_low = logit_grad.astype(jnp.bfloat16)
    low_grad = jnp.einsum("tc,rc->tr", gate_low, own_up, preferred_element_type=f32)
    low_grad = low_grad.astype(jnp.bfloat16)
    input_part = jnp.einsum("tr,dr->td", low_grad, down_weight, preferred_element_type=f32)
    input_part += jnp.einsum("th,dh->td", logit_low, own_beta, preferred_element_type=f32)
    for part in range(3):
        input_part += jnp.einsum(
            "tc,dc->td",
            proj_low[:, part * all_width : (part + 1) * all_width],
            own_qkv[part],
            preferred_element_type=f32,
        )
    slab = model_width // (count * lax.axis_size("dp"))

    def slabs(rows):
        return jnp.transpose(rows).reshape(count, -1, slab, tokens)

    parts = by_group(input_part)
    parts = parts.reshape(groups, count, tokens // count, -1)
    qkv_grad, out_grad, input_grad, layer_out = exchange(
        slabs(rows_in), slabs(rows_grad), proj_low, mixed, parts, by_group(out_part)
    )
    qkv_grad = jnp.transpose(qkv_grad, (1, 0, 2))
    up_term = jnp.einsum("tr,tc->rc", low_rank, gate_low, preferred_element_type=f32)
    beta_term = jnp.einsum("td,th->dh", rows_in, logit_low, preferred_element_type=f32)
    down_term = jnp.einsum("td,tr->dr", rows_in, low_grad, preferred_element_type=f32)
    small = [up_term, beta_term, bias_term]
    packed = jnp.concatenate([term.reshape(-1, 128) for term in small], axis=0)
    packed = lax.psum(packed.astype(jnp.bfloat16), "dp")
    packed = lax.all_gather(packed, "context").astype(f32)
    results, start = [], 0
    for term in small:
        length = term.size // 128
        whole = packed[:, start : start + length].reshape((count,) + term.shape)
        results.append(jnp.transpose(whole, (1, 0, 2)).reshape(term.shape[0], -1))
        start += length
    up_grad, beta_grad, bias_grad = results
    down_grad = lax.psum(lax.psum(down_term.astype(jnp.bfloat16), ("context", "dp")).astype(f32), "head")
    return (layer_out[None], input_grad[None], qkv_grad, out_grad, up_grad, down_grad, beta_grad, bias_grad[0])


def solution(mesh):
    return jax.shard_map(
        shards,
        mesh=mesh,
        in_specs=(
            P("dp", "context", "head"),
            P("dp", "context", "head"),
            P(None, None, "head"),
            P(None, "head"),
            P(),
            P(None, "head"),
            P(None, "head"),
            P("head"),
        ),
        out_specs=(
            P("dp", "context", "head"),
            P("dp", "context", "head"),
            P(("context", "dp"), None, "head"),
            P(("context", "dp"), "head"),
            P(None, "head"),
            P(),
            P(None, "head"),
            P("head"),
        ),
        check_vma=False,
    )
```

```python
import jax
import jax.numpy as jnp
from jax import lax
from jax.experimental import pallas as pl
from jax.experimental.pallas import tpu as pltpu
from jax.sharding import PartitionSpec as P

SPAN = 64
epsilon = 1e-06


def mm(left, right, left_dim, right_dim):
    return lax.dot_general(
        left.astype(jnp.bfloat16),
        right.astype(jnp.bfloat16),
        (((left_dim,), (right_dim,)), ((), ())),
        preferred_element_type=jnp.float32,
    )


def halves(value):
    high = value.astype(jnp.bfloat16)
    return high, (value - high.astype(jnp.float32)).astype(jnp.bfloat16)


def mask_mm(mask, value, mask_dim, value_dim):
    high, low = halves(value)
    return mm(mask, high, mask_dim, value_dim) + mm(mask, low, mask_dim, value_dim)


def square_mm(rows, square):
    row_high, row_low = halves(rows)
    high, low = halves(square)
    return mm(row_high, low, 1, 0) + mm(row_low, high, 1, 0) + mm(row_high, high, 1, 0)


def norm_of(values):
    return lax.rsqrt(jnp.sum(values * values, axis=-1, keepdims=True) + epsilon)


def recurrence_kernel(
    proj_ref, gate_ref, beta_ref, grad_ref,
    mixed_ref, proj_low_ref, gate_low_ref, logit_ref, bias_ref,
    state_ref, inverse_ref, scores_ref, coupling_ref, u_ref, carry_ref,
):
    heads, slots, width, _ = state_ref.shape
    blocks = slots - 1
    all_width = heads * width
    row_index = lax.broadcasted_iota(jnp.int32, (SPAN, SPAN), 0)
    col_index = lax.broadcasted_iota(jnp.int32, (SPAN, SPAN), 1)
    lower = row_index >= col_index
    strict = row_index > col_index
    eye = (row_index == col_index).astype(jnp.float32)
    lower_mask = lower.astype(jnp.bfloat16)
    ones = jnp.ones((SPAN, width), jnp.bfloat16)
    one_rows = jnp.ones((8, width), jnp.bfloat16)
    head_list = range(heads)

    def columns(head, part=0):
        return slice(part * all_width + head * width, part * all_width + (head + 1) * width)

    def prepare(rows):
        sig = lax.logistic(gate_ref[rows, :])
        decays = -0.25 * sig
        cumulative = mask_mm(lower_mask, decays, 1, 0)
        betas = lax.logistic(beta_ref[rows, :])
        made = []
        for head in head_list:
            cum = cumulative[:, columns(head)]
            query_raw = proj_ref[rows, columns(head, 0)]
            key_raw = proj_ref[rows, columns(head, 1)]
            query_norm, key_norm = norm_of(query_raw), norm_of(key_raw)
            queries, keys = query_raw * query_norm, key_raw * key_norm
            middle, final = cum[SPAN // 2 - 1 : SPAN // 2], cum[SPAN - 1 :]
            grow, back = jnp.exp(cum - middle), jnp.exp(middle - cum)
            start, end = jnp.exp(middle), jnp.exp(final - middle)
            key_fwd, key_back, query_fwd = grow * keys, back * keys, grow * queries
            made.append(dict(
                sig=sig[:, columns(head)],
                beta=betas[:, head : head + 1],
                queries=queries, keys=keys, query_norm=query_norm, key_norm=key_norm,
                grow=grow, back=back, start=start, end=end, final=final,
                key_fwd=key_fwd, key_back=key_back, query_fwd=query_fwd,
                key_start=key_fwd * start, query_start=query_fwd * start, key_end=key_back * end,
                decay=jnp.exp(sum(mm(half, ones, 0, 0) for half in halves(decays[:, columns(head)]))),
                values=proj_ref[rows, columns(head, 2)],
            ))
        return made

    def rows_of(block):
        return pl.ds(pl.multiple_of(block * SPAN, SPAN), SPAN)

    def forward(block, carried):
        rows = rows_of(block)
        made = prepare(rows)
        powers, inverses = [], []
        for head, it in enumerate(made):
            both = mm(jnp.concatenate([it["key_fwd"], it["query_fwd"]], axis=0), it["key_back"], 1, 1)
            coupling = jnp.where(strict, both[:SPAN], 0.0)
            scores = jnp.where(lower, both[SPAN:], 0.0)
            coupling_ref[head, block] = coupling
            scores_ref[head, block] = scores.astype(jnp.bfloat16)
            power = -it["beta"] * coupling
            powers.append(power)
            inverses.append(eye + power)
        powers = [square_mm(power, power) for power in powers]
        for section in range(2, (SPAN - 1).bit_length()):
            stacked = [
                square_mm(jnp.concatenate([inverse, power], axis=0), power)
                for inverse, power in zip(inverses, powers)
            ]
            inverses = [inverse + both[:SPAN] for inverse, both in zip(inverses, stacked)]
            powers = [both[SPAN:] for both in stacked]
        inverses = [inverse + square_mm(inverse, power) for inverse, power in zip(inverses, powers)]
        for head in head_list:
            inverse_ref[head, block] = inverses[head].astype(jnp.bfloat16)
        froms = [
            mm(jnp.concatenate([it["key_start"], it["query_start"]], axis=0), state_ref[head, block], 1, 0)
            for head, it in enumerate(made)
        ]
        us = [
            mm(inverse, it["beta"] * (it["values"] - both[:SPAN]), 1, 0)
            for inverse, it, both in zip(inverses, made, froms)
        ]
        for head, it in enumerate(made):
            state_ref[head, block + 1] = it["decay"] * state_ref[head, block] + mm(
                it["key_end"], us[head], 0, 0
            )
            u_ref[head, block] = us[head].astype(jnp.bfloat16)
            mixed = froms[head][SPAN:] + mm(scores_ref[head, block], us[head], 1, 0)
            mixed_ref[rows, columns(head)] = mixed.astype(jnp.bfloat16)
        return carried

    def backward(step, carried):
        block = blocks - 1 - step
        rows = rows_of(block)
        made = prepare(rows)
        grads = [grad_ref[rows, columns(head)] for head in head_list]
        dus = [
            mm(scores_ref[head, block], grads[head], 0, 0) + mm(it["key_end"], carry_ref[head], 1, 0)
            for head, it in enumerate(made)
        ]
        drs = [mm(inverse_ref[head, block], dus[head], 0, 0) for head in head_list]
        logits = jnp.zeros((SPAN, heads), jnp.float32)
        head_index = lax.broadcasted_iota(jnp.int32, (SPAN, heads), 1)
        for head, it in enumerate(made):
            beta, dr, out_grad = it["beta"], drs[head], grads[head]
            state, carry, u = state_ref[head, block], carry_ref[head], u_ref[head, block]
            scaled = beta * dr
            pair = jnp.concatenate([out_grad, -dr], axis=0)
            both = mm(pair, u, 1, 1)
            scores_grad = jnp.where(lower, both[:SPAN], 0.0)
            inner_grad = jnp.where(strict, both[SPAN:], 0.0)
            pair = jnp.concatenate([out_grad, -scaled], axis=0)
            both = mm(pair, state, 1, 1)
            query_start_grad, key_start_grad = both[:SPAN], both[SPAN:]
            key_end_grad = mm(u, carry, 1, 1)
            carry_ref[head] = it["decay"] * carry + mm(
                jnp.concatenate([it["query_start"], it["key_start"]], axis=0), pair, 0, 0
            )
            rest = it["values"] - mm(it["key_start"], state, 1, 0)
            beta_grad = jnp.sum(dr * rest, axis=1, keepdims=True) + jnp.sum(
                inner_grad * coupling_ref[head, block], axis=1, keepdims=True
            )
            square_grads = jnp.concatenate([scores_grad, beta * inner_grad], axis=0)
            both = mm(square_grads, it["key_back"], 1, 0)
            query_fwd_grad, key_fwd_grad = both[:SPAN], both[SPAN:]
            key_back_grad = mm(
                square_grads, jnp.concatenate([it["query_fwd"], it["key_fwd"]], axis=0), 0, 0
            )
            end_term = it["key_end"] * key_end_grad
            query_grow = query_fwd_grad + it["start"] * query_start_grad
            key_grow = key_fwd_grad + it["start"] * key_start_grad
            key_decay = key_back_grad + it["end"] * key_end_grad
            cum_grad = (
                it["query_fwd"] * query_grow + it["key_fwd"] * key_grow - it["key_back"] * key_decay
            )
            final_grad = jnp.sum(end_term, axis=0, keepdims=True) + jnp.exp(it["final"]) * mask_mm(
                one_rows, state * carry, 1, 1
            )[:1]
            decay_grad = mask_mm(lower_mask, cum_grad, 0, 0) + final_grad
            sig = it["sig"]
            gate_grad = decay_grad * (-0.25 * sig * (1.0 - sig))
            query_grad = it["grow"] * query_grow
            key_grad = it["grow"] * key_grow + it["back"] * key_decay

            def through_norm(values, inverse_norm, grad):
                return inverse_norm * (grad - values * jnp.sum(values * grad, axis=1, keepdims=True))

            parts = (
                through_norm(it["queries"], it["query_norm"], query_grad),
                through_norm(it["keys"], it["key_norm"], key_grad),
                scaled,
            )
            for part, value in enumerate(parts):
                proj_low_ref[rows, columns(head, part)] = value.astype(jnp.bfloat16)
            gate_low_ref[rows, columns(head)] = gate_grad.astype(jnp.bfloat16)
            bias_ref[:, columns(head)] += jnp.sum(gate_grad, axis=0, keepdims=True)
            logits = jnp.where(head_index == head, beta_grad * beta * (1.0 - beta), logits)
        logit_ref[rows, :] = logits
        return carried

    for head in head_list:
        state_ref[head, 0] = jnp.zeros((width, width), jnp.float32)
        carry_ref[head] = jnp.zeros((width, width), jnp.float32)
    bias_ref[...] = jnp.zeros_like(bias_ref)
    lax.fori_loop(0, blocks, forward, 0)
    lax.fori_loop(0, blocks, backward, 0)


def recurrence(projected, gate_pre, beta_logit, mixed_grad):
    tokens, all_width = gate_pre.shape
    heads = beta_logit.shape[1]
    width = all_width // heads
    blocks = tokens // SPAN
    vmem = pl.BlockSpec(memory_space=pltpu.VMEM)
    return pl.pallas_call(
        recurrence_kernel,
        in_specs=[vmem] * 4,
        out_specs=[vmem] * 5,
        out_shape=[
            jax.ShapeDtypeStruct((tokens, all_width), jnp.bfloat16),
            jax.ShapeDtypeStruct((tokens, 3 * all_width), jnp.bfloat16),
            jax.ShapeDtypeStruct((tokens, all_width), jnp.bfloat16),
            jax.ShapeDtypeStruct((tokens, heads), jnp.float32),
            jax.ShapeDtypeStruct((1, all_width), jnp.float32),
        ],
        scratch_shapes=[
            pltpu.VMEM((heads, blocks + 1, width, width), jnp.float32),
            pltpu.VMEM((heads, blocks, SPAN, SPAN), jnp.bfloat16),
            pltpu.VMEM((heads, blocks, SPAN, SPAN), jnp.bfloat16),
            pltpu.VMEM((heads, blocks, SPAN, SPAN), jnp.float32),
            pltpu.VMEM((heads, blocks, SPAN, width), jnp.bfloat16),
            pltpu.VMEM((heads, width, width), jnp.float32),
        ],
        compiler_params=pltpu.CompilerParams(vmem_limit_bytes=40 * 1024 * 1024),
    )(projected, gate_pre, beta_logit, mixed_grad)

MESH = pl.DeviceIdType.MESH


def remote(source, target, send_sem, recv_sem, axis, index):
    return pltpu.make_async_remote_copy(
        src_ref=source, dst_ref=target, send_sem=send_sem, recv_sem=recv_sem,
        device_id={axis: index}, device_id_type=MESH,
    )


def meet(peers):
    barrier = pltpu.get_barrier_semaphore()
    for axis, index in peers:
        pl.semaphore_signal(barrier, inc=1, device_id={axis: index}, device_id_type=MESH)
    pl.semaphore_wait(barrier, len(peers))


def project_kernel(
    input_ref, grad_ref, qkv_ref, out_weight_ref, down_ref, up_ref, beta_weight_ref, bias_ref,
    proj_ref, gate_ref, beta_ref, mixed_grad_ref, turned_ref, turned_grad_ref, low_rank_ref,
    gathered, weights, out_weights, up_own,
    own_sem, weight_sem, far_send, far_recv, head_send, head_recv,
):
    groups, count, block, features = gathered.shape[1:]
    heads = beta_ref.shape[1]
    width = up_own.shape[1]
    member, group = lax.axis_index("context"), lax.axis_index("head")
    tokens = count * block
    f32, bf16 = jnp.float32, jnp.bfloat16

    def context_at(offset):
        return lax.rem(member + offset, count)

    def head_at(offset):
        return lax.rem(group + offset, groups)

    meet(
        [("context", context_at(offset)) for offset in range(1, count)]
        + [("head", head_at(offset)) for offset in range(1, groups)]
    )
    near_first = sorted(range(1, count), key=lambda k: min(k, count - k))
    sources = (input_ref, grad_ref)

    def own_copy(which):
        return pltpu.make_async_copy(
            sources[which], gathered.at[which, group, member], own_sem.at[which]
        )

    def far_copy(which, offset):
        return remote(
            sources[which], gathered.at[which, group, member],
            far_send.at[which, offset], far_recv.at[which, offset], "context", context_at(offset),
        )

    def head_copy(which, back, offset):
        source = lax.rem(member + count - back, count)
        place = gathered.at[which, group, source]
        return remote(
            place if back else sources[which], place,
            head_send.at[which, back, offset], head_recv.at[which, back, offset],
            "head", head_at(offset),
        )

    def begin(which):
        own_copy(which).start()
        for offset in range(1, groups):
            head_copy(which, 0, offset).start()
        for offset in near_first:
            far_copy(which, offset).start()

    def pass_on(which):
        for back in near_first:
            far_copy(which, back).wait_recv()
            for offset in range(1, groups):
                head_copy(which, back, offset).start()

    def arrive(which):
        own_copy(which).wait()
        for back in range(count):
            for offset in range(1, groups):
                head_copy(which, back, offset).wait_recv()

    mine = pl.ds(pl.multiple_of(member * width, width), width)
    loads = [
        pltpu.make_async_copy(
            qkv_ref.at[part, :, mine], weights.at[:, pl.ds(part * width, width)], weight_sem.at[part]
        )
        for part in range(3)
    ]
    loads.append(pltpu.make_async_copy(out_weight_ref.at[:, mine], out_weights, weight_sem.at[3]))
    loads.append(pltpu.make_async_copy(up_ref.at[:, mine], up_own, weight_sem.at[4]))

    begin(0)
    for load in loads:
        load.start()
    pass_on(0)
    begin(1)
    for load in loads:
        load.wait()
    arrive(0)

    tile = min(width, 256)

    def rows_of(which, part):
        return gathered[which, part].reshape(tokens, features)

    def product(which, right_ref, columns):
        total = None
        for part in range(groups):
            value = jnp.dot(
                rows_of(which, part),
                right_ref[pl.ds(part * features, features), columns],
                preferred_element_type=f32,
            )
            total = value if total is None else total + value
        return total

    def project(step, carried):
        columns = pl.ds(pl.multiple_of(step * tile, tile), tile)
        proj_ref[:, columns] = product(0, weights, columns)
        return carried

    lax.fori_loop(0, 3 * width // tile, project, 0)
    low_rank = product(0, down_ref, slice(None)).astype(bf16)
    low_rank_ref[...] = low_rank
    gate_ref[...] = jnp.dot(low_rank, up_own[...], preferred_element_type=f32) + bias_ref[:, mine]
    logits = None
    for part in range(groups):
        value = lax.dot_general(
            rows_of(0, part), beta_weight_ref[:, part * features : (part + 1) * features],
            (((1,), (1,)), ((), ())), preferred_element_type=f32,
        )
        logits = value if logits is None else logits + value
    lane = lax.broadcasted_iota(jnp.int32, logits.shape, 1)
    for head in range(heads):
        picked = jnp.where(lane == member * heads + head, logits, 0.0)
        beta_ref[:, head : head + 1] = jnp.sum(picked, axis=1, keepdims=True)
    pass_on(1)

    def turn(which, target_ref):
        for part in range(groups):
            for index in range(count):
                target_ref[part * features : (part + 1) * features, index * block : (index + 1) * block] = (
                    gathered[which, part, index].T
                )

    turn(0, turned_ref)
    arrive(1)

    def project_grad(step, carried):
        columns = pl.ds(pl.multiple_of(step * tile, tile), tile)
        mixed_grad_ref[:, columns] = product(1, out_weights, columns)
        return carried

    lax.fori_loop(0, width // tile, project_grad, 0)
    turn(1, turned_grad_ref)
    for which in range(2):
        for offset in range(1, count):
            far_copy(which, offset).wait_send()
        for back in range(count):
            for offset in range(1, groups):
                head_copy(which, back, offset).wait_send()


def project(inputs, output_grad, qkv, out_weight, down_weight, up_weight, beta_turned, gate_bias):
    count, groups = lax.axis_size("context"), lax.axis_size("head")
    block, features = inputs.shape
    tokens, model_width = count * block, groups * features
    all_width = out_weight.shape[1] // count
    heads = beta_turned.shape[0] // count
    rank = down_weight.shape[1]
    f32, bf16 = jnp.float32, jnp.bfloat16
    vmem = pl.BlockSpec(memory_space=pltpu.VMEM)
    hbm = pl.BlockSpec(memory_space=pl.ANY)
    dma = pltpu.SemaphoreType.DMA
    shape = jax.ShapeDtypeStruct
    return pl.pallas_call(
        project_kernel,
        in_specs=[hbm, hbm, hbm, hbm, vmem, hbm, vmem, vmem],
        out_specs=[vmem] * 7,
        out_shape=[
            shape((tokens, 3 * all_width), f32),
            shape((tokens, all_width), f32),
            shape((tokens, heads), f32),
            shape((tokens, all_width), f32),
            shape((model_width, tokens), bf16),
            shape((model_width, tokens), bf16),
            shape((tokens, rank), bf16),
        ],
        scratch_shapes=[
            pltpu.VMEM((2, groups, count, block, features), bf16),
            pltpu.VMEM((model_width, 3 * all_width), bf16),
            pltpu.VMEM((model_width, all_width), bf16),
            pltpu.VMEM((rank, all_width), bf16),
            dma((2,)), dma((5,)),
            dma((2, count)), dma((2, count)),
            dma((2, count, groups)), dma((2, count, groups)),
        ],
        compiler_params=pltpu.CompilerParams(
            collective_id=2, has_side_effects=True, vmem_limit_bytes=48 * 1024 * 1024
        ),
    )(inputs, output_grad, qkv, out_weight, down_weight, up_weight, beta_turned, gate_bias)


def exchange_kernel(
    rows_ref, grads_ref, proj_ref, mixed_ref, part_ref, layer_ref,
    qkv_ref, out_ref, input_ref, layer_out_ref,
    keep, send_one, recv_one, send_two, recv_two, done_rows,
    head_recv, part_send, part_recv, layer_recv,
    one_send, one_recv, two_send, two_recv, far_send, far_recv, local_sem,
    head_send_sem, head_recv_sem, part_send_sem, part_recv_sem, layer_send_sem, layer_recv_sem,
):
    count, width = rows_ref.shape[0], mixed_ref.shape[1]
    groups = part_ref.shape[0]
    slab = rows_ref.shape[2]
    member, row, group = (lax.axis_index(name) for name in ("context", "dp", "head"))
    near = row + 1 - 2 * lax.rem(row, 2)
    across = lax.rem(row + 2, 4)
    opposite = 3 - row

    def peer(axis, index):
        return {axis: index}

    def context_at(offset):
        return lax.rem(member + offset, count)

    def head_at(offset):
        return lax.rem(group + offset, groups)

    barrier = pltpu.get_barrier_semaphore()
    peers = [peer("context", context_at(offset)) for offset in range(1, count)]
    peers += [peer("head", head_at(offset)) for offset in range(1, groups)]
    peers += [peer("dp", near), peer("dp", across)]
    for target in peers:
        pl.semaphore_signal(barrier, inc=1, device_id=target, device_id_type=MESH)
    pl.semaphore_wait(barrier, len(peers))

    offsets = sorted(range(1, count), key=lambda k: -min(k, count - k)) + [0]

    def remote(source, target, send_sem, recv_sem, device):
        return pltpu.make_async_remote_copy(
            src_ref=source, dst_ref=target, send_sem=send_sem, recv_sem=recv_sem,
            device_id=device, device_id_type=MESH,
        )

    def layer_copy(offset):
        return remote(
            layer_ref.at[head_at(offset)], layer_recv.at[offset],
            layer_send_sem.at[offset], layer_recv_sem.at[offset], peer("head", head_at(offset)),
        )

    def head_copy(step, offset):
        return remote(
            part_ref.at[head_at(offset), context_at(offsets[step])], head_recv.at[offset, step],
            head_send_sem.at[offset, step], head_recv_sem.at[offset, step],
            peer("head", head_at(offset)),
        )

    for offset in range(1, groups):
        layer_copy(offset).start()
    for step in range(count):
        for offset in range(1, groups):
            head_copy(step, offset).start()

    def one_copy(step):
        return remote(
            send_one.at[step], recv_one.at[step], one_send.at[step], one_recv.at[step],
            peer("dp", near),
        )

    def two_copy(step):
        return remote(
            send_two.at[step], recv_two.at[step], two_send.at[step], two_recv.at[step],
            peer("dp", across),
        )

    def owner_ref(part, index):
        columns = pl.ds(pl.multiple_of(index * width, width), width)
        return out_ref.at[:, columns] if part == 3 else qkv_ref.at[part, :, columns]

    def far_copy(step, part):
        offset = offsets[step]
        return remote(
            done_rows.at[step, :, pl.ds(part * width, width)], owner_ref(part, member),
            far_send.at[step, part], far_recv.at[offset, part], peer("context", context_at(offset)),
        )

    def far_arrival(offset, part):
        source = lax.rem(member + count - offset, count)
        return remote(
            done_rows.at[0, :, pl.ds(part * width, width)], owner_ref(part, source),
            far_send.at[0, part], far_recv.at[offset, part], peer("context", source),
        )

    def part_copy(step):
        offset = offsets[step]
        return remote(
            part_send.at[step], part_recv.at[offset],
            part_send_sem.at[step], part_recv_sem.at[offset], peer("context", context_at(offset)),
        )

    def products(step, targets):
        chosen = context_at(offsets[step])

        def fill(part, carried):
            columns = pl.ds(pl.multiple_of(part * width, width), width)
            for index, store in targets:
                value = jnp.dot(
                    rows_ref[chosen, index], proj_ref[:, columns], preferred_element_type=jnp.float32
                )
                store(columns, value)
            return carried

        lax.fori_loop(0, 3, fill, 0)
        columns = pl.ds(3 * width, width)
        for index, store in targets:
            value = jnp.dot(
                grads_ref[chosen, index], mixed_ref[...], preferred_element_type=jnp.float32
            )
            store(columns, value)

    def sender(step, slot):
        def store(columns, value):
            send_one[step, slot, :, columns] = value.astype(jnp.bfloat16)

        return store

    def keeper(step, slot):
        def store(columns, value):
            keep[step % 3, slot, :, columns] = value

        return store

    def over_columns(body):
        def one(part, carried):
            body(pl.ds(pl.multiple_of(part * width, width), width))
            return carried

        lax.fori_loop(0, 4, one, 0)

    def first(step):
        products(step, [(near, sender(step, 0)), (opposite, sender(step, 1))])
        one_copy(step).start()
        products(step, [(row, keeper(step, 0)), (across, keeper(step, 1))])

    def second(step):
        one_copy(step).wait_recv()

        def add(columns):
            send_two[step, :, columns] = (
                keep[step % 3, 1, :, columns] + recv_one[step, 1, :, columns].astype(jnp.float32)
            ).astype(jnp.bfloat16)

        over_columns(add)
        two_copy(step).start()

    def third(step):
        two_copy(step).wait_recv()

        def add(columns):
            done_rows[step, :, columns] = (
                keep[step % 3, 0, :, columns]
                + recv_one[step, 0, :, columns].astype(jnp.float32)
                + recv_two[step, :, columns].astype(jnp.float32)
            ).astype(jnp.bfloat16)

        over_columns(add)
        for part in range(4):
            if offsets[step]:
                far_copy(step, part).start()
            else:
                own_copy(step, part).start()

    def own_copy(step, part):
        return pltpu.make_async_copy(
            done_rows.at[step, :, pl.ds(part * width, width)], owner_ref(part, member),
            local_sem.at[part],
        )

    def partial(step):
        for offset in range(1, groups):
            head_copy(step, offset).wait_recv()
        total = part_ref[group, context_at(offsets[step])].astype(jnp.float32)
        for offset in range(1, groups):
            total = total + head_recv[offset, step].astype(jnp.float32)
        part_send[step] = total.astype(jnp.bfloat16)
        if offsets[step]:
            part_copy(step).start()

    for step in range(count + 2):
        if step < count:
            first(step)
        if 0 <= step - 1 < count:
            second(step - 1)
        if step < count:
            partial(step)
        if step >= 2:
            third(step - 2)

    for offset in range(1, groups):
        layer_copy(offset).wait_recv()
    total = layer_ref[group].astype(jnp.float32)
    for offset in range(1, groups):
        total = total + layer_recv[offset].astype(jnp.float32)
    layer_out_ref[...] = total.astype(jnp.bfloat16)
    total = part_send[count - 1].astype(jnp.float32)
    for step in range(count - 1):
        offset = offsets[step]
        part_copy(step).wait_recv()
        total = total + part_recv[offset].astype(jnp.float32)
    input_ref[...] = total.astype(jnp.bfloat16)
    for step in range(count - 1):
        for part in range(4):
            far_arrival(offsets[step], part).wait_recv()
    for part in range(4):
        own_copy(count - 1, part).wait()
    for step in range(count):
        one_copy(step).wait_send()
        two_copy(step).wait_send()
        for offset in range(1, groups):
            head_copy(step, offset).wait_send()
        if offsets[step]:
            part_copy(step).wait_send()
            for part in range(4):
                far_copy(step, part).wait_send()
    for offset in range(1, groups):
        layer_copy(offset).wait_send()


def exchange(rows, grads, proj_low, mixed, parts, layer_parts):
    count, _, slab, tokens = rows.shape
    width = mixed.shape[1]
    groups, _, block, features = parts.shape
    bf16 = jnp.bfloat16
    vmem = pl.BlockSpec(memory_space=pltpu.VMEM)
    hbm = pl.BlockSpec(memory_space=pl.ANY)
    dma = pltpu.SemaphoreType.DMA
    return pl.pallas_call(
        exchange_kernel,
        in_specs=[vmem] * 6,
        out_specs=[hbm, hbm, vmem, vmem],
        out_shape=[
            jax.ShapeDtypeStruct((3, slab, count * width), bf16),
            jax.ShapeDtypeStruct((slab, count * width), bf16),
            jax.ShapeDtypeStruct((block, features), bf16),
            jax.ShapeDtypeStruct((block, features), bf16),
        ],
        scratch_shapes=[
            pltpu.VMEM((3, 2, slab, 4 * width), jnp.float32),
            pltpu.VMEM((count, 2, slab, 4 * width), bf16),
            pltpu.VMEM((count, 2, slab, 4 * width), bf16),
            pltpu.VMEM((count, slab, 4 * width), bf16),
            pltpu.VMEM((count, slab, 4 * width), bf16),
            pltpu.VMEM((count, slab, 4 * width), bf16),
            pltpu.VMEM((groups, count, block, features), bf16),
            pltpu.VMEM((count, block, features), bf16),
            pltpu.VMEM((count, block, features), bf16),
            pltpu.VMEM((groups, block, features), bf16),
            dma((count,)), dma((count,)), dma((count,)), dma((count,)),
            dma((count, 4)), dma((count, 4)), dma((4,)),
            dma((groups, count)), dma((groups, count)),
            dma((count,)), dma((count,)),
            dma((groups,)), dma((groups,)),
        ],
        compiler_params=pltpu.CompilerParams(
            collective_id=1, has_side_effects=True, vmem_limit_bytes=56 * 1024 * 1024
        ),
    )(rows, grads, proj_low, mixed, parts, layer_parts)


def shards(
    inputs, output_grad, qkv_weight, out_weight, down_weight, up_weight, beta_weight, gate_bias
):
    count = lax.axis_size("context")
    member = lax.axis_index("context")
    f32 = jnp.float32

    def own(array, axis):
        size = array.shape[axis] // count
        return lax.dynamic_slice_in_dim(array, member * size, size, axis=axis)

    model_width, rank = down_weight.shape
    tokens = count * inputs.shape[1]
    own_qkv = own(jnp.transpose(qkv_weight, (1, 0, 2)), 2)
    own_out = own(out_weight, 1)
    own_up = own(up_weight, 1)
    own_beta = own(beta_weight, 1)
    heads = own_beta.shape[1]
    all_width = own_up.shape[1]
    projected, gate_pre, beta_logit, mixed_grad, turned, turned_grad, low_rank = project(
        inputs[0], output_grad[0], jnp.transpose(qkv_weight, (1, 0, 2)), out_weight, down_weight,
        up_weight, beta_weight.T, gate_bias[None],
    )
    mixed, proj_low, gate_low, logit_grad, bias_term = recurrence(
        projected, gate_pre, beta_logit, mixed_grad
    )
    mixed_own = lax.all_to_all(mixed, "context", 0, 1, tiled=True)
    out_part = jnp.einsum("tc,dc->td", mixed_own, out_weight, preferred_element_type=f32)
    groups = lax.axis_size("head")

    def by_group(value):
        whole = value.astype(jnp.bfloat16).reshape(value.shape[0], groups, -1)
        return jnp.transpose(whole, (1, 0, 2))

    logit_low = logit_grad.astype(jnp.bfloat16)
    low_grad = jnp.einsum("tc,rc->tr", gate_low, own_up, preferred_element_type=f32)
    low_grad = low_grad.astype(jnp.bfloat16)
    input_part = jnp.einsum("tr,dr->td", low_grad, down_weight, preferred_element_type=f32)
    input_part += jnp.einsum("th,dh->td", logit_low, own_beta, preferred_element_type=f32)
    for part in range(3):
        input_part += jnp.einsum(
            "tc,dc->td",
            proj_low[:, part * all_width : (part + 1) * all_width],
            own_qkv[part],
            preferred_element_type=f32,
        )
    slab = model_width // (count * lax.axis_size("dp"))

    def slabs(turned_rows):
        return turned_rows.reshape(count, -1, slab, tokens)

    parts = by_group(input_part)
    parts = parts.reshape(groups, count, tokens // count, -1)
    qkv_grad, out_grad, input_grad, layer_out = exchange(
        slabs(turned), slabs(turned_grad), proj_low, mixed, parts, by_group(out_part)
    )
    qkv_grad = jnp.transpose(qkv_grad, (1, 0, 2))
    up_term = jnp.einsum("tr,tc->rc", low_rank, gate_low, preferred_element_type=f32)
    beta_term = jnp.einsum("dt,th->dh", turned, logit_low, preferred_element_type=f32)
    down_term = jnp.einsum("dt,tr->dr", turned, low_grad, preferred_element_type=f32)
    small = [up_term, beta_term, bias_term]
    packed = jnp.concatenate([term.reshape(-1, 128) for term in small], axis=0)
    packed = lax.psum(packed.astype(jnp.bfloat16), "dp")
    packed = lax.all_gather(packed, "context").astype(f32)
    results, start = [], 0
    for term in small:
        length = term.size // 128
        whole = packed[:, start : start + length].reshape((count,) + term.shape)
        results.append(jnp.transpose(whole, (1, 0, 2)).reshape(term.shape[0], -1))
        start += length
    up_grad, beta_grad, bias_grad = results
    down_grad = lax.psum(lax.psum(down_term.astype(jnp.bfloat16), ("context", "dp")).astype(f32), "head")
    return (layer_out[None], input_grad[None], qkv_grad, out_grad, up_grad, down_grad, beta_grad, bias_grad[0])


def solution(mesh):
    return jax.shard_map(
        shards,
        mesh=mesh,
        in_specs=(
            P("dp", "context", "head"),
            P("dp", "context", "head"),
            P(None, None, "head"),
            P(None, "head"),
            P(),
            P(None, "head"),
            P(None, "head"),
            P("head"),
        ),
        out_specs=(
            P("dp", "context", "head"),
            P("dp", "context", "head"),
            P(("context", "dp"), None, "head"),
            P(("context", "dp"), "head"),
            P(None, "head"),
            P(),
            P(None, "head"),
            P("head"),
        ),
        check_vma=False,
    )
```

```python
import jax
import jax.numpy as jnp
from jax import lax
from jax.experimental import pallas as pl
from jax.experimental.pallas import tpu as pltpu
from jax.sharding import PartitionSpec as P

SPAN = 64
epsilon = 1e-06


def mm(left, right, left_dim, right_dim):
    return lax.dot_general(
        left.astype(jnp.bfloat16),
        right.astype(jnp.bfloat16),
        (((left_dim,), (right_dim,)), ((), ())),
        preferred_element_type=jnp.float32,
    )


def halves(value):
    high = value.astype(jnp.bfloat16)
    return high, (value - high.astype(jnp.float32)).astype(jnp.bfloat16)


def mask_mm(mask, value, mask_dim, value_dim):
    high, low = halves(value)
    return mm(mask, high, mask_dim, value_dim) + mm(mask, low, mask_dim, value_dim)


def square_mm(rows, square):
    row_high, row_low = halves(rows)
    high, low = halves(square)
    return mm(row_high, low, 1, 0) + mm(row_low, high, 1, 0) + mm(row_high, high, 1, 0)


def norm_of(values):
    return lax.rsqrt(jnp.sum(values * values, axis=-1, keepdims=True) + epsilon)


def recurrence_kernel(
    proj_ref, gate_ref, beta_ref, grad_ref,
    mixed_ref, proj_low_ref, gate_low_ref, logit_ref, bias_ref,
    state_ref, inverse_ref, scores_ref, coupling_ref, u_ref, carry_ref,
):
    heads, slots, width, _ = state_ref.shape
    blocks = slots - 1
    all_width = heads * width
    row_index = lax.broadcasted_iota(jnp.int32, (SPAN, SPAN), 0)
    col_index = lax.broadcasted_iota(jnp.int32, (SPAN, SPAN), 1)
    lower = row_index >= col_index
    strict = row_index > col_index
    eye = (row_index == col_index).astype(jnp.float32)
    lower_mask = lower.astype(jnp.bfloat16)
    ones = jnp.ones((SPAN, width), jnp.bfloat16)
    one_rows = jnp.ones((8, width), jnp.bfloat16)
    head_list = range(heads)

    def columns(head, part=0):
        return slice(part * all_width + head * width, part * all_width + (head + 1) * width)

    def prepare(rows):
        sig = lax.logistic(gate_ref[rows, :])
        decays = -0.25 * sig
        cumulative = mask_mm(lower_mask, decays, 1, 0)
        betas = lax.logistic(beta_ref[rows, :])
        made = []
        for head in head_list:
            cum = cumulative[:, columns(head)]
            query_raw = proj_ref[rows, columns(head, 0)]
            key_raw = proj_ref[rows, columns(head, 1)]
            query_norm, key_norm = norm_of(query_raw), norm_of(key_raw)
            queries, keys = query_raw * query_norm, key_raw * key_norm
            middle, final = cum[SPAN // 2 - 1 : SPAN // 2], cum[SPAN - 1 :]
            grow, back = jnp.exp(cum - middle), jnp.exp(middle - cum)
            start, end = jnp.exp(middle), jnp.exp(final - middle)
            key_fwd, key_back, query_fwd = grow * keys, back * keys, grow * queries
            made.append(dict(
                sig=sig[:, columns(head)],
                beta=betas[:, head : head + 1],
                queries=queries, keys=keys, query_norm=query_norm, key_norm=key_norm,
                grow=grow, back=back, start=start, end=end, final=final,
                key_fwd=key_fwd, key_back=key_back, query_fwd=query_fwd,
                key_start=key_fwd * start, query_start=query_fwd * start, key_end=key_back * end,
                decay=jnp.exp(sum(mm(half, ones, 0, 0) for half in halves(decays[:, columns(head)]))),
                values=proj_ref[rows, columns(head, 2)],
            ))
        return made

    def rows_of(block):
        return pl.ds(pl.multiple_of(block * SPAN, SPAN), SPAN)

    def forward(block, carried):
        rows = rows_of(block)
        made = prepare(rows)
        powers, inverses = [], []
        for head, it in enumerate(made):
            both = mm(jnp.concatenate([it["key_fwd"], it["query_fwd"]], axis=0), it["key_back"], 1, 1)
            coupling = jnp.where(strict, both[:SPAN], 0.0)
            scores = jnp.where(lower, both[SPAN:], 0.0)
            coupling_ref[head, block] = coupling
            scores_ref[head, block] = scores.astype(jnp.bfloat16)
            power = -it["beta"] * coupling
            powers.append(power)
            inverses.append(eye + power)
        powers = [square_mm(power, power) for power in powers]
        for section in range(2, (SPAN - 1).bit_length()):
            stacked = [
                square_mm(jnp.concatenate([inverse, power], axis=0), power)
                for inverse, power in zip(inverses, powers)
            ]
            inverses = [inverse + both[:SPAN] for inverse, both in zip(inverses, stacked)]
            powers = [both[SPAN:] for both in stacked]
        inverses = [inverse + square_mm(inverse, power) for inverse, power in zip(inverses, powers)]
        for head in head_list:
            inverse_ref[head, block] = inverses[head].astype(jnp.bfloat16)
        froms = [
            mm(jnp.concatenate([it["key_start"], it["query_start"]], axis=0), state_ref[head, block], 1, 0)
            for head, it in enumerate(made)
        ]
        us = [
            mm(inverse, it["beta"] * (it["values"] - both[:SPAN]), 1, 0)
            for inverse, it, both in zip(inverses, made, froms)
        ]
        for head, it in enumerate(made):
            state_ref[head, block + 1] = it["decay"] * state_ref[head, block] + mm(
                it["key_end"], us[head], 0, 0
            )
            u_ref[head, block] = us[head].astype(jnp.bfloat16)
            mixed = froms[head][SPAN:] + mm(scores_ref[head, block], us[head], 1, 0)
            mixed_ref[rows, columns(head)] = mixed.astype(jnp.bfloat16)
        return carried

    def backward(step, carried):
        block = blocks - 1 - step
        rows = rows_of(block)
        made = prepare(rows)
        grads = [grad_ref[rows, columns(head)] for head in head_list]
        dus = [
            mm(scores_ref[head, block], grads[head], 0, 0) + mm(it["key_end"], carry_ref[head], 1, 0)
            for head, it in enumerate(made)
        ]
        drs = [mm(inverse_ref[head, block], dus[head], 0, 0) for head in head_list]
        logits = jnp.zeros((SPAN, heads), jnp.float32)
        head_index = lax.broadcasted_iota(jnp.int32, (SPAN, heads), 1)
        for head, it in enumerate(made):
            beta, dr, out_grad = it["beta"], drs[head], grads[head]
            state, carry, u = state_ref[head, block], carry_ref[head], u_ref[head, block]
            scaled = beta * dr
            pair = jnp.concatenate([out_grad, -dr], axis=0)
            both = mm(pair, u, 1, 1)
            scores_grad = jnp.where(lower, both[:SPAN], 0.0)
            inner_grad = jnp.where(strict, both[SPAN:], 0.0)
            pair = jnp.concatenate([out_grad, -scaled], axis=0)
            both = mm(pair, state, 1, 1)
            query_start_grad, key_start_grad = both[:SPAN], both[SPAN:]
            key_end_grad = mm(u, carry, 1, 1)
            carry_ref[head] = it["decay"] * carry + mm(
                jnp.concatenate([it["query_start"], it["key_start"]], axis=0), pair, 0, 0
            )
            rest = it["values"] - mm(it["key_start"], state, 1, 0)
            beta_grad = jnp.sum(dr * rest, axis=1, keepdims=True) + jnp.sum(
                inner_grad * coupling_ref[head, block], axis=1, keepdims=True
            )
            square_grads = jnp.concatenate([scores_grad, beta * inner_grad], axis=0)
            both = mm(square_grads, it["key_back"], 1, 0)
            query_fwd_grad, key_fwd_grad = both[:SPAN], both[SPAN:]
            key_back_grad = mm(
                square_grads, jnp.concatenate([it["query_fwd"], it["key_fwd"]], axis=0), 0, 0
            )
            end_term = it["key_end"] * key_end_grad
            query_grow = query_fwd_grad + it["start"] * query_start_grad
            key_grow = key_fwd_grad + it["start"] * key_start_grad
            key_decay = key_back_grad + it["end"] * key_end_grad
            cum_grad = (
                it["query_fwd"] * query_grow + it["key_fwd"] * key_grow - it["key_back"] * key_decay
            )
            final_grad = jnp.sum(end_term, axis=0, keepdims=True) + jnp.exp(it["final"]) * mask_mm(
                one_rows, state * carry, 1, 1
            )[:1]
            decay_grad = mask_mm(lower_mask, cum_grad, 0, 0) + final_grad
            sig = it["sig"]
            gate_grad = decay_grad * (-0.25 * sig * (1.0 - sig))
            query_grad = it["grow"] * query_grow
            key_grad = it["grow"] * key_grow + it["back"] * key_decay

            def through_norm(values, inverse_norm, grad):
                return inverse_norm * (grad - values * jnp.sum(values * grad, axis=1, keepdims=True))

            parts = (
                through_norm(it["queries"], it["query_norm"], query_grad),
                through_norm(it["keys"], it["key_norm"], key_grad),
                scaled,
            )
            for part, value in enumerate(parts):
                proj_low_ref[rows, columns(head, part)] = value.astype(jnp.bfloat16)
            gate_low_ref[rows, columns(head)] = gate_grad.astype(jnp.bfloat16)
            bias_ref[:, columns(head)] += jnp.sum(gate_grad, axis=0, keepdims=True)
            logits = jnp.where(head_index == head, beta_grad * beta * (1.0 - beta), logits)
        logit_ref[rows, :] = logits
        return carried

    for head in head_list:
        state_ref[head, 0] = jnp.zeros((width, width), jnp.float32)
        carry_ref[head] = jnp.zeros((width, width), jnp.float32)
    bias_ref[...] = jnp.zeros_like(bias_ref)
    lax.fori_loop(0, blocks, forward, 0)
    lax.fori_loop(0, blocks, backward, 0)


def recurrence(projected, gate_pre, beta_logit, mixed_grad):
    tokens, all_width = gate_pre.shape
    heads = beta_logit.shape[1]
    width = all_width // heads
    blocks = tokens // SPAN
    vmem = pl.BlockSpec(memory_space=pltpu.VMEM)
    return pl.pallas_call(
        recurrence_kernel,
        in_specs=[vmem] * 4,
        out_specs=[vmem] * 5,
        out_shape=[
            jax.ShapeDtypeStruct((tokens, all_width), jnp.bfloat16),
            jax.ShapeDtypeStruct((tokens, 3 * all_width), jnp.bfloat16),
            jax.ShapeDtypeStruct((tokens, all_width), jnp.bfloat16),
            jax.ShapeDtypeStruct((tokens, heads), jnp.float32),
            jax.ShapeDtypeStruct((1, all_width), jnp.float32),
        ],
        scratch_shapes=[
            pltpu.VMEM((heads, blocks + 1, width, width), jnp.float32),
            pltpu.VMEM((heads, blocks, SPAN, SPAN), jnp.bfloat16),
            pltpu.VMEM((heads, blocks, SPAN, SPAN), jnp.bfloat16),
            pltpu.VMEM((heads, blocks, SPAN, SPAN), jnp.float32),
            pltpu.VMEM((heads, blocks, SPAN, width), jnp.bfloat16),
            pltpu.VMEM((heads, width, width), jnp.float32),
        ],
        compiler_params=pltpu.CompilerParams(vmem_limit_bytes=40 * 1024 * 1024),
    )(projected, gate_pre, beta_logit, mixed_grad)

MESH = pl.DeviceIdType.MESH


def remote(source, target, send_sem, recv_sem, axis, index):
    return pltpu.make_async_remote_copy(
        src_ref=source, dst_ref=target, send_sem=send_sem, recv_sem=recv_sem,
        device_id={axis: index}, device_id_type=MESH,
    )


def meet(peers):
    barrier = pltpu.get_barrier_semaphore()
    for axis, index in peers:
        pl.semaphore_signal(barrier, inc=1, device_id={axis: index}, device_id_type=MESH)
    pl.semaphore_wait(barrier, len(peers))


def project_kernel(
    input_ref, grad_ref, qkv_ref, out_weight_ref, down_ref, up_ref, beta_weight_ref, bias_ref,
    proj_ref, gate_ref, beta_ref, mixed_grad_ref, turned_ref, turned_grad_ref, low_rank_ref,
    gathered, weights, out_weights, up_own,
    own_sem, weight_sem, far_send, far_recv, head_send, head_recv,
):
    groups, count, block, features = gathered.shape[1:]
    heads = beta_ref.shape[1]
    width = up_own.shape[1]
    member, group = lax.axis_index("context"), lax.axis_index("head")
    tokens = count * block
    f32, bf16 = jnp.float32, jnp.bfloat16

    def context_at(offset):
        return lax.rem(member + offset, count)

    def head_at(offset):
        return lax.rem(group + offset, groups)

    meet(
        [("context", context_at(offset)) for offset in range(1, count)]
        + [("head", head_at(offset)) for offset in range(1, groups)]
    )
    near_first = sorted(range(1, count), key=lambda k: min(k, count - k))
    sources = (input_ref, grad_ref)

    def own_copy(which):
        return pltpu.make_async_copy(
            sources[which], gathered.at[which, group, member], own_sem.at[which]
        )

    def far_copy(which, offset):
        return remote(
            sources[which], gathered.at[which, group, member],
            far_send.at[which, offset], far_recv.at[which, offset], "context", context_at(offset),
        )

    def head_copy(which, back, offset):
        source = lax.rem(member + count - back, count)
        place = gathered.at[which, group, source]
        return remote(
            place if back else sources[which], place,
            head_send.at[which, back, offset], head_recv.at[which, back, offset],
            "head", head_at(offset),
        )

    def begin(which):
        own_copy(which).start()
        for offset in range(1, groups):
            head_copy(which, 0, offset).start()
        for offset in near_first:
            far_copy(which, offset).start()

    def pass_on(which):
        for back in near_first:
            far_copy(which, back).wait_recv()
            for offset in range(1, groups):
                head_copy(which, back, offset).start()

    def arrive(which):
        own_copy(which).wait()
        for back in range(count):
            for offset in range(1, groups):
                head_copy(which, back, offset).wait_recv()

    mine = pl.ds(pl.multiple_of(member * width, width), width)
    loads = [
        pltpu.make_async_copy(
            qkv_ref.at[part, :, mine], weights.at[:, pl.ds(part * width, width)], weight_sem.at[part]
        )
        for part in range(3)
    ]
    loads.append(pltpu.make_async_copy(out_weight_ref.at[:, mine], out_weights, weight_sem.at[3]))
    loads.append(pltpu.make_async_copy(up_ref.at[:, mine], up_own, weight_sem.at[4]))

    begin(0)
    for load in loads:
        load.start()
    pass_on(0)
    begin(1)
    for load in loads:
        load.wait()
    arrive(0)

    tile = min(width, 256)

    def rows_of(which, part):
        return gathered[which, part].reshape(tokens, features)

    def product(which, right_ref, columns):
        total = None
        for part in range(groups):
            value = jnp.dot(
                rows_of(which, part),
                right_ref[pl.ds(part * features, features), columns],
                preferred_element_type=f32,
            )
            total = value if total is None else total + value
        return total

    def project(step, carried):
        columns = pl.ds(pl.multiple_of(step * tile, tile), tile)
        proj_ref[:, columns] = product(0, weights, columns)
        return carried

    lax.fori_loop(0, 3 * width // tile, project, 0)
    low_rank = product(0, down_ref, slice(None)).astype(bf16)
    low_rank_ref[...] = low_rank
    gate_ref[...] = jnp.dot(low_rank, up_own[...], preferred_element_type=f32) + bias_ref[:, mine]
    logits = None
    for part in range(groups):
        value = lax.dot_general(
            rows_of(0, part), beta_weight_ref[:, part * features : (part + 1) * features],
            (((1,), (1,)), ((), ())), preferred_element_type=f32,
        )
        logits = value if logits is None else logits + value
    lane = lax.broadcasted_iota(jnp.int32, logits.shape, 1)
    for head in range(heads):
        picked = jnp.where(lane == member * heads + head, logits, 0.0)
        beta_ref[:, head : head + 1] = jnp.sum(picked, axis=1, keepdims=True)
    pass_on(1)

    def turn(which, target_ref):
        for part in range(groups):
            for index in range(count):
                target_ref[part * features : (part + 1) * features, index * block : (index + 1) * block] = (
                    gathered[which, part, index].T
                )

    turn(0, turned_ref)
    arrive(1)

    def project_grad(step, carried):
        columns = pl.ds(pl.multiple_of(step * tile, tile), tile)
        mixed_grad_ref[:, columns] = product(1, out_weights, columns)
        return carried

    lax.fori_loop(0, width // tile, project_grad, 0)
    turn(1, turned_grad_ref)
    for which in range(2):
        for offset in range(1, count):
            far_copy(which, offset).wait_send()
        for back in range(count):
            for offset in range(1, groups):
                head_copy(which, back, offset).wait_send()


def project(inputs, output_grad, qkv, out_weight, down_weight, up_weight, beta_turned, gate_bias):
    count, groups = lax.axis_size("context"), lax.axis_size("head")
    block, features = inputs.shape
    tokens, model_width = count * block, groups * features
    all_width = out_weight.shape[1] // count
    heads = beta_turned.shape[0] // count
    rank = down_weight.shape[1]
    f32, bf16 = jnp.float32, jnp.bfloat16
    vmem = pl.BlockSpec(memory_space=pltpu.VMEM)
    hbm = pl.BlockSpec(memory_space=pl.ANY)
    dma = pltpu.SemaphoreType.DMA
    shape = jax.ShapeDtypeStruct
    return pl.pallas_call(
        project_kernel,
        in_specs=[hbm, hbm, hbm, hbm, vmem, hbm, vmem, vmem],
        out_specs=[vmem] * 7,
        out_shape=[
            shape((tokens, 3 * all_width), f32),
            shape((tokens, all_width), f32),
            shape((tokens, heads), f32),
            shape((tokens, all_width), f32),
            shape((model_width, tokens), bf16),
            shape((model_width, tokens), bf16),
            shape((tokens, rank), bf16),
        ],
        scratch_shapes=[
            pltpu.VMEM((2, groups, count, block, features), bf16),
            pltpu.VMEM((model_width, 3 * all_width), bf16),
            pltpu.VMEM((model_width, all_width), bf16),
            pltpu.VMEM((rank, all_width), bf16),
            dma((2,)), dma((5,)),
            dma((2, count)), dma((2, count)),
            dma((2, count, groups)), dma((2, count, groups)),
        ],
        compiler_params=pltpu.CompilerParams(
            collective_id=2, has_side_effects=True, vmem_limit_bytes=48 * 1024 * 1024
        ),
    )(inputs, output_grad, qkv, out_weight, down_weight, up_weight, beta_turned, gate_bias)


def exchange_kernel(
    turned_ref, turned_grad_ref, proj_ref, mixed_ref, gate_ref, logit_ref, low_rank_ref, bias_ref,
    qkv_weight_ref, out_weight_ref, down_ref, up_ref, beta_weight_ref,
    qkv_ref, out_ref, input_ref, layer_out_ref, up_out_ref, down_out_ref, beta_out_ref, bias_out_ref,
    keep, send_one, recv_one, send_two, recv_two, done_rows,
    parts, head_recv, part_send, part_recv,
    weights, out_weights, up_own, mixed_all, layer_send, layer_recv, layer_own,
    low_grad, logit_keep, up_full, up_slots, up_one, up_two, up_across, up_all,
    down_slots, down_one, down_two, down_across, down_done, down_far, down_group, down_all,
    beta_own, beta_one, beta_sum, beta_two, beta_done, beta_far,
    send_sems, recv_sems, local_sems,
):
    count, block, width = mixed_all.shape
    groups = parts.shape[0]
    features = parts.shape[3]
    slab = done_rows.shape[1]
    heads = logit_ref.shape[1]
    rank = down_ref.shape[1]
    tokens = count * block
    quarter = rank // 4
    f32, bf16 = jnp.float32, jnp.bfloat16
    member, row, group = (lax.axis_index(name) for name in ("context", "dp", "head"))
    near = row + 1 - 2 * lax.rem(row, 2)
    across = lax.rem(row + 2, 4)
    opposite = 3 - row
    slots = (near, opposite, row, across)

    def context_at(offset):
        return lax.rem(member + offset, count)

    def head_at(offset):
        return lax.rem(group + offset, groups)

    meet(
        [("context", context_at(offset)) for offset in range(1, count)]
        + [("head", head_at(offset)) for offset in range(1, groups)]
        + [("dp", near), ("dp", across)]
    )
    offsets = sorted(range(1, count), key=lambda k: -min(k, count - k)) + [0]
    far_offsets = offsets[:-1]
    numbers, flying = {}, {}

    def begin(key, source, target, axis, index):
        number = numbers.setdefault(key, len(numbers))
        flying[key] = remote(
            source, target, send_sems.at[number], recv_sems.at[number], axis, index
        )
        flying[key].start()

    def arrived(*key):
        flying[key].wait_recv()

    def dot(left, right, left_dim=1, right_dim=0):
        return lax.dot_general(
            left, right, (((left_dim,), (right_dim,)), ((), ())), preferred_element_type=f32
        )

    def slab_rows(chosen, index):
        step = 16 if slab % 16 == 0 else 8
        return pl.ds(pl.multiple_of((chosen * 4 + index) * slab, step), slab)

    mine = pl.ds(pl.multiple_of(member * width, width), width)

    def features_of(index):
        step = 16 if features % 16 == 0 else 8
        return pl.multiple_of(index * features, step)

    loads = [
        pltpu.make_async_copy(
            qkv_weight_ref.at[part, :, mine], weights.at[:, pl.ds(part * width, width)],
            local_sems.at[part],
        )
        for part in range(3)
    ]
    up_load = pltpu.make_async_copy(up_ref.at[:, mine], up_own, local_sems.at[3])

    def out_load(offset):
        return pltpu.make_async_copy(
            out_weight_ref.at[pl.ds(features_of(head_at(offset)), features), :], out_weights,
            local_sems.at[4],
        )

    group_order = list(range(1, groups)) + [0]
    for offset in far_offsets:
        chosen = context_at(offset)
        begin(
            ("mixed", offset),
            mixed_ref.at[pl.ds(pl.multiple_of(chosen * block, block), block), :],
            mixed_all.at[member], "context", chosen,
        )
    up_load.start()
    for load in loads:
        load.start()
    out_load(group_order[0]).start()
    mixed_all[member] = mixed_ref[pl.ds(pl.multiple_of(member * block, block), block), :]

    lane = lax.broadcasted_iota(jnp.int32, (tokens, beta_own.shape[0]), 1)
    logit_all = jnp.zeros(lane.shape, f32)
    for head in range(heads):
        logit_all = jnp.where(lane == member * heads + head, logit_ref[:, head : head + 1], logit_all)
    logit_low = logit_all.astype(bf16)
    logit_keep[...] = logit_low[:, : count * heads]
    beta_own[...] = dot(logit_low, turned_ref[...], 0, 1).astype(bf16)
    begin(("beta", 1), beta_own, beta_one, "dp", near)
    up_load.wait()
    low_grad[...] = dot(gate_ref[...], up_own[...], 1, 1).astype(bf16)

    def down_terms(chosen, carried):
        for slot, index in enumerate(slots):
            down_slots[slot // 2, chosen, slot % 2] = dot(
                turned_ref[slab_rows(chosen, index), :], low_grad[...]
            ).astype(bf16)
        return carried

    lax.fori_loop(0, count, down_terms, 0)
    begin(("down", 1), down_slots.at[0], down_one, "dp", near)
    up_full[...] = dot(low_rank_ref[...], gate_ref[...], 0, 0)
    for slot, index in enumerate(slots):
        rows = pl.ds(pl.multiple_of(index * quarter, 8), quarter)
        up_slots[slot, :quarter] = up_full[rows, :].astype(bf16)
        up_slots[slot, quarter:] = jnp.broadcast_to(bias_ref[...], (16, width)).astype(bf16)
    begin(("up", 1), up_slots.at[pl.ds(0, 2)], up_one, "dp", near)

    def products(step, targets):
        chosen = context_at(offsets[step])

        def fill(part, carried):
            columns = pl.ds(pl.multiple_of(part * width, width), width)
            for index, store in targets:
                store(columns, dot(turned_ref[slab_rows(chosen, index), :], proj_ref[:, columns]))
            return carried

        lax.fori_loop(0, 3, fill, 0)
        columns = pl.ds(3 * width, width)
        for index, store in targets:
            store(columns, dot(turned_grad_ref[slab_rows(chosen, index), :], mixed_ref[...]))

    def sender(step, slot):
        def store(columns, value):
            send_one[step, slot, :, columns] = value.astype(bf16)

        return store

    def keeper(step, slot):
        def store(columns, value):
            keep[step % 3, slot, :, columns] = value.astype(keep.dtype)

        return store

    def over_columns(body):
        def one(part, carried):
            body(pl.ds(pl.multiple_of(part * width, width), width))
            return carried

        lax.fori_loop(0, 4, one, 0)

    def first(step):
        products(step, [(near, sender(step, 0)), (opposite, sender(step, 1))])
        begin(("one", step), send_one.at[step], recv_one.at[step], "dp", near)
        products(step, [(row, keeper(step, 0)), (across, keeper(step, 1))])

    def second(step):
        arrived("one", step)

        def add(columns):
            send_two[step, :, columns] = (
                keep[step % 3, 1, :, columns].astype(f32) + recv_one[step, 1, :, columns].astype(f32)
            ).astype(bf16)

        over_columns(add)
        begin(("two", step), send_two.at[step], recv_two.at[step], "dp", across)

    def owner_ref(part):
        return out_ref.at[:, mine] if part == 3 else qkv_ref.at[part, :, mine]

    def own_copy(step, part):
        return pltpu.make_async_copy(
            done_rows.at[step, :, pl.ds(part * width, width)], owner_ref(part), local_sems.at[part]
        )

    def third(step):
        arrived("two", step)

        def add(columns):
            done_rows[step, :, columns] = (
                keep[step % 3, 0, :, columns].astype(f32)
                + recv_one[step, 0, :, columns].astype(f32)
                + recv_two[step, :, columns].astype(f32)
            ).astype(bf16)

        over_columns(add)
        offset = offsets[step]
        for part in range(4):
            if offset:
                begin(
                    ("far", offset, part), done_rows.at[step, :, pl.ds(part * width, width)],
                    owner_ref(part), "context", context_at(offset),
                )
            else:
                own_copy(step, part).start()

    tile = 384 if features % 384 == 0 else features

    def input_parts():
        for load in loads:
            load.wait()
        for offset in group_order:
            chosen = head_at(offset)
            base = features_of(chosen)

            def some(step, carried, chosen=chosen, base=base):
                if tile == features:
                    lanes, rows = slice(None), pl.ds(base, tile)
                else:
                    lanes = pl.ds(pl.multiple_of(step * tile, tile), tile)
                    rows = pl.ds(pl.multiple_of(base + step * tile, 128), tile)
                for index in range(count):
                    span = slice(index * block, (index + 1) * block)
                    value = dot(proj_ref[span, :], weights[rows, :], 1, 1)
                    value = value + dot(low_grad[span, :], down_ref[rows, :], 1, 1)
                    value = value + dot(logit_keep[span, :], beta_weight_ref[rows, :], 1, 1)
                    parts[chosen, index, :, lanes] = value.astype(bf16)
                return carried

            lax.fori_loop(0, features // tile, some, 0)
            if offset:
                for place in offsets:
                    begin(
                        ("part", offset, place), parts.at[chosen, context_at(place)],
                        head_recv.at[offset - 1, context_at(place)], "head", chosen,
                    )

    def partial(step):
        place = offsets[step]
        chosen = context_at(place)
        total = parts[group, chosen].astype(f32)
        for offset in range(1, groups):
            arrived("part", offset, place)
            total = total + head_recv[offset - 1, chosen].astype(f32)
        part_send[step] = total.astype(bf16)
        if place:
            begin(("sum", place), part_send.at[step], part_recv.at[place], "context", chosen)

    def layer_half(offset, store):
        out_load(offset).wait()

        def some(step, carried):
            if tile == features:
                rows = slice(None)
            else:
                rows = pl.ds(pl.multiple_of(step * tile, tile), tile)
            value = None
            for index in range(count):
                one = dot(
                    mixed_all[index], out_weights[rows, index * width : (index + 1) * width], 1, 1
                )
                value = one if value is None else value + one
            store(rows, value)
            return carried

        lax.fori_loop(0, features // tile, some, 0)

    def layer_peers():
        for offset in far_offsets:
            arrived("mixed", offset)
        for place, offset in enumerate(group_order[:-1]):

            def store(lanes, value, offset=offset):
                layer_send[offset - 1, :, lanes] = value.astype(bf16)

            layer_half(offset, store)
            out_load(group_order[place + 1]).start()
            begin(
                ("layer", offset), layer_send.at[offset - 1], layer_recv.at[offset - 1],
                "head", head_at(offset),
            )

    def layer_mine():
        def store(lanes, value):
            layer_own[:, lanes] = value

        layer_half(0, store)

    def small_two():
        for name in ("beta", "down", "up"):
            arrived(name, 1)
        beta_sum[...] = (beta_own[...].astype(f32) + beta_one[...].astype(f32)).astype(bf16)
        begin(("beta", 2), beta_sum, beta_two, "dp", across)
        for index in range(count):
            down_two[index] = (
                down_slots[1, index, 1].astype(f32) + down_one[index, 1].astype(f32)
            ).astype(bf16)
        begin(("down", 2), down_two, down_across, "dp", across)
        up_two[...] = (up_slots[3].astype(f32) + up_one[1].astype(f32)).astype(bf16)
        begin(("up", 2), up_two, up_across, "dp", across)

    def small_three():
        for name in ("beta", "down", "up"):
            arrived(name, 2)
        for index in range(count):
            down_done[index] = (
                down_slots[1, index, 0].astype(f32)
                + down_one[index, 0].astype(f32)
                + down_across[index].astype(f32)
            ).astype(bf16)
        up_all[member, row] = (
            up_slots[2].astype(f32) + up_one[0].astype(f32) + up_across[...].astype(f32)
        ).astype(bf16)
        beta_done[...] = (beta_sum[...].astype(f32) + beta_two[...].astype(f32)).astype(bf16)
        for offset in far_offsets:
            chosen = context_at(offset)
            begin(("down", "far", offset), down_done.at[chosen], down_far.at[offset], "context", chosen)
            begin(
                ("up", "far", offset), up_all.at[member, row], up_all.at[member, row],
                "context", chosen,
            )
            begin(("beta", "far", offset), beta_done, beta_far.at[offset], "context", chosen)

    def small_four():
        total = down_done[member].astype(f32)
        for offset in far_offsets:
            arrived("down", "far", offset)
            total = total + down_far[offset].astype(f32)
        down_group[group] = total.astype(bf16)
        for offset in range(1, groups):
            begin(
                ("down", "head", offset), down_group.at[group], down_group.at[group],
                "head", head_at(offset),
            )

    def small_five():
        for offset in range(1, groups):
            arrived("down", "head", offset)
        total = down_group[0].astype(f32)
        for index in range(1, groups):
            total = total + down_group[index].astype(f32)
        down_all[member, row] = total.astype(bf16)
        for offset in far_offsets:
            begin(
                ("down", "all", offset), down_all.at[member, row], down_all.at[member, row],
                "context", context_at(offset),
            )

    def small_six():
        for offset in far_offsets:
            arrived("down", "all", offset)
            arrived("up", "far", offset)
        begin(("up", "near"), up_all.at[:, row], up_all.at[:, row], "dp", near)
        begin(("down", "near"), down_all.at[:, row], down_all.at[:, row], "dp", near)

    def small_seven():
        arrived("up", "near")
        arrived("down", "near")
        for place, index in enumerate((row, near)):
            begin(("up", "across", place), up_all.at[:, index], up_all.at[:, index], "dp", across)
            begin(
                ("down", "across", place), down_all.at[:, index], down_all.at[:, index], "dp", across
            )

    def small_last():
        for place in range(2):
            arrived("up", "across", place)
            arrived("down", "across", place)
        for index in range(count):
            columns = slice(index * width, (index + 1) * width)
            for part in range(4):
                up_out_ref[part * quarter : (part + 1) * quarter, columns] = up_all[
                    index, part, :quarter
                ].astype(f32)
                start = (index * 4 + part) * slab
                down_out_ref[start : start + slab, :] = down_all[index, part].astype(f32)
            bias_out_ref[:, columns] = up_all[index, 0, quarter : quarter + 1].astype(f32)
        total = beta_done[...].astype(f32)
        for offset in far_offsets:
            arrived("beta", "far", offset)
            total = total + beta_far[offset].astype(f32)
        beta_out_ref[...] = total[: count * heads]

    small = {0: small_two, 1: small_three, 2: small_four, 3: small_five, 4: small_six, 5: small_seven}
    layer = {1: layer_peers, 2: layer_mine}
    for step in range(count + 2):
        if step < count:
            first(step)
        if step == 0:
            input_parts()
        if 0 <= step - 1 < count:
            second(step - 1)
        if step < count:
            partial(step)
        if step in small:
            small[step]()
        if step in layer:
            layer[step]()
        if step >= 2:
            third(step - 2)

    total = layer_own[...]
    for offset in range(1, groups):
        arrived("layer", offset)
        total = total + layer_recv[offset - 1].astype(f32)
    layer_out_ref[...] = total.astype(bf16)
    total = part_send[count - 1].astype(f32)
    for offset in far_offsets:
        arrived("sum", offset)
        total = total + part_recv[offset].astype(f32)
    input_ref[...] = total.astype(bf16)
    small_last()
    for offset in far_offsets:
        for part in range(4):
            arrived("far", offset, part)
    for part in range(4):
        own_copy(count - 1, part).wait()
    for copy in flying.values():
        copy.wait_send()


def exchange(
    turned, turned_grad, proj_low, mixed, gate_low, logit_grad, low_rank, bias_term,
    qkv_weight, out_weight, down_weight, up_weight, beta_weight,
):
    count, groups, parts = (lax.axis_size(name) for name in ("context", "head", "dp"))
    assert parts == 4
    model_width, tokens = turned.shape
    width, rank = mixed.shape[1], down_weight.shape[1]
    head_count = beta_weight.shape[1]
    slab, block, features = model_width // (count * parts), tokens // count, model_width // groups
    quarter = rank // parts
    lines = max(16, head_count)
    f32, bf16 = jnp.float32, jnp.bfloat16
    vmem = pl.BlockSpec(memory_space=pltpu.VMEM)
    hbm = pl.BlockSpec(memory_space=pl.ANY)
    dma = pltpu.SemaphoreType.DMA
    shape = jax.ShapeDtypeStruct
    copies = 24 * count
    return pl.pallas_call(
        exchange_kernel,
        in_specs=[vmem] * 8 + [hbm, hbm, vmem, hbm, vmem],
        out_specs=[hbm, hbm] + [vmem] * 6,
        out_shape=[
            shape((3, slab, count * width), bf16),
            shape((slab, count * width), bf16),
            shape((block, features), bf16),
            shape((block, features), bf16),
            shape((rank, count * width), f32),
            shape((model_width, rank), f32),
            shape((head_count, model_width), f32),
            shape((1, count * width), f32),
        ],
        scratch_shapes=[
            pltpu.VMEM((3, 2, slab, 4 * width), bf16),
            pltpu.VMEM((count, 2, slab, 4 * width), bf16),
            pltpu.VMEM((count, 2, slab, 4 * width), bf16),
            pltpu.VMEM((count, slab, 4 * width), bf16),
            pltpu.VMEM((count, slab, 4 * width), bf16),
            pltpu.VMEM((count, slab, 4 * width), bf16),
            pltpu.VMEM((groups, count, block, features), bf16),
            pltpu.VMEM((groups - 1, count, block, features), bf16),
            pltpu.VMEM((count, block, features), bf16),
            pltpu.VMEM((count, block, features), bf16),
            pltpu.VMEM((model_width, 3 * width), bf16),
            pltpu.VMEM((features, count * width), bf16),
            pltpu.VMEM((rank, width), bf16),
            pltpu.VMEM((count, block, width), bf16),
            pltpu.VMEM((groups - 1, block, features), bf16),
            pltpu.VMEM((groups - 1, block, features), bf16),
            pltpu.VMEM((block, features), f32),
            pltpu.VMEM((tokens, rank), bf16),
            pltpu.VMEM((tokens, head_count), bf16),
            pltpu.VMEM((rank, width), f32),
            pltpu.VMEM((4, quarter + 16, width), bf16),
            pltpu.VMEM((2, quarter + 16, width), bf16),
            pltpu.VMEM((quarter + 16, width), bf16),
            pltpu.VMEM((quarter + 16, width), bf16),
            pltpu.VMEM((count, 4, quarter + 16, width), bf16),
            pltpu.VMEM((2, count, 2, slab, rank), bf16),
            pltpu.VMEM((count, 2, slab, rank), bf16),
            pltpu.VMEM((count, slab, rank), bf16),
            pltpu.VMEM((count, slab, rank), bf16),
            pltpu.VMEM((count, slab, rank), bf16),
            pltpu.VMEM((count, slab, rank), bf16),
            pltpu.VMEM((groups, slab, rank), bf16),
            pltpu.VMEM((count, 4, slab, rank), bf16),
            pltpu.VMEM((lines, model_width), bf16),
            pltpu.VMEM((lines, model_width), bf16),
            pltpu.VMEM((lines, model_width), bf16),
            pltpu.VMEM((lines, model_width), bf16),
            pltpu.VMEM((lines, model_width), bf16),
            pltpu.VMEM((count, lines, model_width), bf16),
            dma((copies,)), dma((copies,)), dma((5,)),
        ],
        compiler_params=pltpu.CompilerParams(
            collective_id=1, has_side_effects=True, vmem_limit_bytes=60 * 1024 * 1024
        ),
    )(
        turned, turned_grad, proj_low, mixed, gate_low, logit_grad, low_rank, bias_term,
        qkv_weight, out_weight, down_weight, up_weight, beta_weight,
    )


def shards(
    inputs, output_grad, qkv_weight, out_weight, down_weight, up_weight, beta_weight, gate_bias
):
    qkv_turned = jnp.transpose(qkv_weight, (1, 0, 2))
    projected, gate_pre, beta_logit, mixed_grad, turned, turned_grad, low_rank = project(
        inputs[0], output_grad[0], qkv_turned, out_weight, down_weight, up_weight, beta_weight.T,
        gate_bias[None],
    )
    mixed, proj_low, gate_low, logit_grad, bias_term = recurrence(
        projected, gate_pre, beta_logit, mixed_grad
    )
    qkv_grad, out_grad, input_grad, layer_out, up_grad, down_grad, beta_grad, bias_grad = exchange(
        turned, turned_grad, proj_low, mixed, gate_low, logit_grad, low_rank, bias_term,
        qkv_turned, out_weight, down_weight, up_weight, beta_weight,
    )
    qkv_grad = jnp.transpose(qkv_grad, (1, 0, 2))
    return (
        layer_out[None], input_grad[None], qkv_grad, out_grad, up_grad, down_grad, beta_grad.T,
        bias_grad[0],
    )


def solution(mesh):
    return jax.shard_map(
        shards,
        mesh=mesh,
        in_specs=(
            P("dp", "context", "head"),
            P("dp", "context", "head"),
            P(None, None, "head"),
            P(None, "head"),
            P(),
            P(None, "head"),
            P(None, "head"),
            P("head"),
        ),
        out_specs=(
            P("dp", "context", "head"),
            P("dp", "context", "head"),
            P(("context", "dp"), None, "head"),
            P(("context", "dp"), "head"),
            P(None, "head"),
            P(),
            P(None, "head"),
            P("head"),
        ),
        check_vma=False,
    )
```

```python
import jax
import jax.numpy as jnp
from jax import lax
from jax.experimental import pallas as pl
from jax.experimental.pallas import tpu as pltpu
from jax.sharding import PartitionSpec as P

SPAN = 64
epsilon = 1e-06


def mm(left, right, left_dim, right_dim):
    return lax.dot_general(
        left.astype(jnp.bfloat16),
        right.astype(jnp.bfloat16),
        (((left_dim,), (right_dim,)), ((), ())),
        preferred_element_type=jnp.float32,
    )


def halves(value):
    high = value.astype(jnp.bfloat16)
    return high, (value - high.astype(jnp.float32)).astype(jnp.bfloat16)


def mask_mm(mask, value, mask_dim, value_dim):
    high, low = halves(value)
    return mm(mask, high, mask_dim, value_dim) + mm(mask, low, mask_dim, value_dim)


def square_mm(rows, square):
    row_high, row_low = halves(rows)
    high, low = halves(square)
    return mm(row_high, low, 1, 0) + mm(row_low, high, 1, 0) + mm(row_high, high, 1, 0)


def norm_of(values):
    return lax.rsqrt(jnp.sum(values * values, axis=-1, keepdims=True) + epsilon)


def recurrence_kernel(
    proj_ref, gate_ref, beta_ref, grad_ref,
    mixed_ref, proj_low_ref, gate_low_ref, logit_ref, bias_ref,
    state_ref, inverse_ref, scores_ref, coupling_ref, u_ref, carry_ref,
):
    heads, slots, width, _ = state_ref.shape
    blocks = slots - 1
    all_width = heads * width
    row_index = lax.broadcasted_iota(jnp.int32, (SPAN, SPAN), 0)
    col_index = lax.broadcasted_iota(jnp.int32, (SPAN, SPAN), 1)
    lower = row_index >= col_index
    strict = row_index > col_index
    eye = (row_index == col_index).astype(jnp.float32)
    lower_mask = lower.astype(jnp.bfloat16)
    ones = jnp.ones((SPAN, width), jnp.bfloat16)
    one_rows = jnp.ones((8, width), jnp.bfloat16)
    head_list = range(heads)

    def columns(head, part=0):
        return slice(part * all_width + head * width, part * all_width + (head + 1) * width)

    def prepare(rows):
        sig = lax.logistic(gate_ref[rows, :])
        decays = -0.25 * sig
        cumulative = mask_mm(lower_mask, decays, 1, 0)
        betas = lax.logistic(beta_ref[rows, :])
        made = []
        for head in head_list:
            cum = cumulative[:, columns(head)]
            query_raw = proj_ref[rows, columns(head, 0)]
            key_raw = proj_ref[rows, columns(head, 1)]
            query_norm, key_norm = norm_of(query_raw), norm_of(key_raw)
            queries, keys = query_raw * query_norm, key_raw * key_norm
            middle, final = cum[SPAN // 2 - 1 : SPAN // 2], cum[SPAN - 1 :]
            grow, back = jnp.exp(cum - middle), jnp.exp(middle - cum)
            start, end = jnp.exp(middle), jnp.exp(final - middle)
            key_fwd, key_back, query_fwd = grow * keys, back * keys, grow * queries
            made.append(dict(
                sig=sig[:, columns(head)],
                beta=betas[:, head : head + 1],
                queries=queries, keys=keys, query_norm=query_norm, key_norm=key_norm,
                grow=grow, back=back, start=start, end=end, final=final,
                key_fwd=key_fwd, key_back=key_back, query_fwd=query_fwd,
                key_start=key_fwd * start, query_start=query_fwd * start, key_end=key_back * end,
                decay=jnp.exp(sum(mm(half, ones, 0, 0) for half in halves(decays[:, columns(head)]))),
                values=proj_ref[rows, columns(head, 2)],
            ))
        return made

    def rows_of(block):
        return pl.ds(pl.multiple_of(block * SPAN, SPAN), SPAN)

    def forward(block, carried):
        rows = rows_of(block)
        made = prepare(rows)
        powers, inverses = [], []
        for head, it in enumerate(made):
            both = mm(jnp.concatenate([it["key_fwd"], it["query_fwd"]], axis=0), it["key_back"], 1, 1)
            coupling = jnp.where(strict, both[:SPAN], 0.0)
            scores = jnp.where(lower, both[SPAN:], 0.0)
            coupling_ref[head, block] = coupling
            scores_ref[head, block] = scores.astype(jnp.bfloat16)
            power = -it["beta"] * coupling
            powers.append(power)
            inverses.append(eye + power)
        powers = [square_mm(power, power) for power in powers]
        for section in range(2, (SPAN - 1).bit_length()):
            stacked = [
                square_mm(jnp.concatenate([inverse, power], axis=0), power)
                for inverse, power in zip(inverses, powers)
            ]
            inverses = [inverse + both[:SPAN] for inverse, both in zip(inverses, stacked)]
            powers = [both[SPAN:] for both in stacked]
        inverses = [inverse + square_mm(inverse, power) for inverse, power in zip(inverses, powers)]
        for head in head_list:
            inverse_ref[head, block] = inverses[head].astype(jnp.bfloat16)
        froms = [
            mm(jnp.concatenate([it["key_start"], it["query_start"]], axis=0), state_ref[head, block], 1, 0)
            for head, it in enumerate(made)
        ]
        us = [
            mm(inverse, it["beta"] * (it["values"] - both[:SPAN]), 1, 0)
            for inverse, it, both in zip(inverses, made, froms)
        ]
        for head, it in enumerate(made):
            state_ref[head, block + 1] = it["decay"] * state_ref[head, block] + mm(
                it["key_end"], us[head], 0, 0
            )
            u_ref[head, block] = us[head].astype(jnp.bfloat16)
            mixed = froms[head][SPAN:] + mm(scores_ref[head, block], us[head], 1, 0)
            mixed_ref[rows, columns(head)] = mixed.astype(jnp.bfloat16)
        return carried

    def backward(step, carried):
        block = blocks - 1 - step
        rows = rows_of(block)
        made = prepare(rows)
        grads = [grad_ref[rows, columns(head)] for head in head_list]
        dus = [
            mm(scores_ref[head, block], grads[head], 0, 0) + mm(it["key_end"], carry_ref[head], 1, 0)
            for head, it in enumerate(made)
        ]
        drs = [mm(inverse_ref[head, block], dus[head], 0, 0) for head in head_list]
        logits = jnp.zeros((SPAN, heads), jnp.float32)
        head_index = lax.broadcasted_iota(jnp.int32, (SPAN, heads), 1)
        for head, it in enumerate(made):
            beta, dr, out_grad = it["beta"], drs[head], grads[head]
            state, carry, u = state_ref[head, block], carry_ref[head], u_ref[head, block]
            scaled = beta * dr
            pair = jnp.concatenate([out_grad, -dr], axis=0)
            both = mm(pair, u, 1, 1)
            scores_grad = jnp.where(lower, both[:SPAN], 0.0)
            inner_grad = jnp.where(strict, both[SPAN:], 0.0)
            pair = jnp.concatenate([out_grad, -scaled], axis=0)
            both = mm(pair, state, 1, 1)
            query_start_grad, key_start_grad = both[:SPAN], both[SPAN:]
            key_end_grad = mm(u, carry, 1, 1)
            carry_ref[head] = it["decay"] * carry + mm(
                jnp.concatenate([it["query_start"], it["key_start"]], axis=0), pair, 0, 0
            )
            rest = it["values"] - mm(it["key_start"], state, 1, 0)
            beta_grad = jnp.sum(dr * rest, axis=1, keepdims=True) + jnp.sum(
                inner_grad * coupling_ref[head, block], axis=1, keepdims=True
            )
            square_grads = jnp.concatenate([scores_grad, beta * inner_grad], axis=0)
            both = mm(square_grads, it["key_back"], 1, 0)
            query_fwd_grad, key_fwd_grad = both[:SPAN], both[SPAN:]
            key_back_grad = mm(
                square_grads, jnp.concatenate([it["query_fwd"], it["key_fwd"]], axis=0), 0, 0
            )
            end_term = it["key_end"] * key_end_grad
            query_grow = query_fwd_grad + it["start"] * query_start_grad
            key_grow = key_fwd_grad + it["start"] * key_start_grad
            key_decay = key_back_grad + it["end"] * key_end_grad
            cum_grad = (
                it["query_fwd"] * query_grow + it["key_fwd"] * key_grow - it["key_back"] * key_decay
            )
            final_grad = jnp.sum(end_term, axis=0, keepdims=True) + jnp.exp(it["final"]) * mask_mm(
                one_rows, state * carry, 1, 1
            )[:1]
            decay_grad = mask_mm(lower_mask, cum_grad, 0, 0) + final_grad
            sig = it["sig"]
            gate_grad = decay_grad * (-0.25 * sig * (1.0 - sig))
            query_grad = it["grow"] * query_grow
            key_grad = it["grow"] * key_grow + it["back"] * key_decay

            def through_norm(values, inverse_norm, grad):
                return inverse_norm * (grad - values * jnp.sum(values * grad, axis=1, keepdims=True))

            parts = (
                through_norm(it["queries"], it["query_norm"], query_grad),
                through_norm(it["keys"], it["key_norm"], key_grad),
                scaled,
            )
            for part, value in enumerate(parts):
                proj_low_ref[rows, columns(head, part)] = value.astype(jnp.bfloat16)
            gate_low_ref[rows, columns(head)] = gate_grad.astype(jnp.bfloat16)
            bias_ref[:, columns(head)] += jnp.sum(gate_grad, axis=0, keepdims=True)
            logits = jnp.where(head_index == head, beta_grad * beta * (1.0 - beta), logits)
        logit_ref[rows, :] = logits
        return carried

    for head in head_list:
        state_ref[head, 0] = jnp.zeros((width, width), jnp.float32)
        carry_ref[head] = jnp.zeros((width, width), jnp.float32)
    bias_ref[...] = jnp.zeros_like(bias_ref)
    lax.fori_loop(0, blocks, forward, 0)
    lax.fori_loop(0, blocks, backward, 0)


def recurrence(projected, gate_pre, beta_logit, mixed_grad):
    tokens, all_width = gate_pre.shape
    heads = beta_logit.shape[1]
    width = all_width // heads
    blocks = tokens // SPAN
    vmem = pl.BlockSpec(memory_space=pltpu.VMEM)
    return pl.pallas_call(
        recurrence_kernel,
        in_specs=[vmem] * 4,
        out_specs=[vmem] * 5,
        out_shape=[
            jax.ShapeDtypeStruct((tokens, all_width), jnp.bfloat16),
            jax.ShapeDtypeStruct((tokens, 3 * all_width), jnp.bfloat16),
            jax.ShapeDtypeStruct((tokens, all_width), jnp.bfloat16),
            jax.ShapeDtypeStruct((tokens, heads), jnp.float32),
            jax.ShapeDtypeStruct((1, all_width), jnp.float32),
        ],
        scratch_shapes=[
            pltpu.VMEM((heads, blocks + 1, width, width), jnp.float32),
            pltpu.VMEM((heads, blocks, SPAN, SPAN), jnp.bfloat16),
            pltpu.VMEM((heads, blocks, SPAN, SPAN), jnp.bfloat16),
            pltpu.VMEM((heads, blocks, SPAN, SPAN), jnp.float32),
            pltpu.VMEM((heads, blocks, SPAN, width), jnp.bfloat16),
            pltpu.VMEM((heads, width, width), jnp.float32),
        ],
        compiler_params=pltpu.CompilerParams(vmem_limit_bytes=40 * 1024 * 1024),
    )(projected, gate_pre, beta_logit, mixed_grad)

MESH = pl.DeviceIdType.MESH


def remote(source, target, send_sem, recv_sem, axis, index):
    return pltpu.make_async_remote_copy(
        src_ref=source, dst_ref=target, send_sem=send_sem, recv_sem=recv_sem,
        device_id={axis: index}, device_id_type=MESH,
    )


def meet(peers):
    barrier = pltpu.get_barrier_semaphore()
    for axis, index in peers:
        pl.semaphore_signal(barrier, inc=1, device_id={axis: index}, device_id_type=MESH)
    pl.semaphore_wait(barrier, len(peers))


def project_kernel(
    input_ref, grad_ref, qkv_ref, out_weight_ref, down_hbm, up_ref, beta_hbm, bias_hbm,
    proj_ref, gate_ref, beta_ref, mixed_grad_ref, turned_ref, turned_grad_ref, low_rank_ref,
    gathered, weights, out_weights, up_own, down_ref, beta_weight_ref, bias_ref,
    own_sem, weight_sem, far_send, far_recv, head_send, head_recv,
):
    groups, count, block, features = gathered.shape[1:]
    heads = beta_ref.shape[1]
    width = up_own.shape[1]
    member, group = lax.axis_index("context"), lax.axis_index("head")
    tokens = count * block
    f32, bf16 = jnp.float32, jnp.bfloat16

    def context_at(offset):
        return lax.rem(member + offset, count)

    def head_at(offset):
        return lax.rem(group + offset, groups)

    meet(
        [("context", context_at(offset)) for offset in range(1, count)]
        + [("head", head_at(offset)) for offset in range(1, groups)]
    )
    near_first = sorted(range(1, count), key=lambda k: min(k, count - k))
    sources = (input_ref, grad_ref)

    def own_copy(which):
        return pltpu.make_async_copy(
            sources[which], gathered.at[which, group, member], own_sem.at[which]
        )

    def far_copy(which, offset):
        return remote(
            sources[which], gathered.at[which, group, member],
            far_send.at[which, offset], far_recv.at[which, offset], "context", context_at(offset),
        )

    def head_copy(which, back, offset):
        source = lax.rem(member + count - back, count)
        place = gathered.at[which, group, source]
        return remote(
            place if back else sources[which], place,
            head_send.at[which, back, offset], head_recv.at[which, back, offset],
            "head", head_at(offset),
        )

    def begin(which):
        own_copy(which).start()
        for offset in range(1, groups):
            head_copy(which, 0, offset).start()
        for offset in near_first:
            far_copy(which, offset).start()

    def pass_on(which):
        for back in near_first:
            far_copy(which, back).wait_recv()
            for offset in range(1, groups):
                head_copy(which, back, offset).start()

    def arrive(which):
        own_copy(which).wait()
        for back in range(count):
            for offset in range(1, groups):
                head_copy(which, back, offset).wait_recv()

    mine = pl.ds(pl.multiple_of(member * width, width), width)
    loads = [
        pltpu.make_async_copy(
            qkv_ref.at[part, :, mine], weights.at[:, pl.ds(part * width, width)], weight_sem.at[part]
        )
        for part in range(3)
    ]
    loads.append(pltpu.make_async_copy(out_weight_ref.at[:, mine], out_weights, weight_sem.at[3]))
    loads.append(pltpu.make_async_copy(up_ref.at[:, mine], up_own, weight_sem.at[4]))
    loads.append(pltpu.make_async_copy(down_hbm, down_ref, weight_sem.at[5]))
    loads.append(pltpu.make_async_copy(beta_hbm, beta_weight_ref, weight_sem.at[6]))
    loads.append(pltpu.make_async_copy(bias_hbm.at[:, mine], bias_ref, weight_sem.at[7]))

    begin(0)
    for load in loads:
        load.start()
    pass_on(0)
    begin(1)
    for load in loads:
        load.wait()
    arrive(0)

    tile = min(width, 256)

    def rows_of(which, part):
        return gathered[which, part].reshape(tokens, features)

    def product(which, right_ref, columns):
        total = None
        for part in range(groups):
            value = jnp.dot(
                rows_of(which, part),
                right_ref[pl.ds(part * features, features), columns],
                preferred_element_type=f32,
            )
            total = value if total is None else total + value
        return total

    def project(step, carried):
        columns = pl.ds(pl.multiple_of(step * tile, tile), tile)
        proj_ref[:, columns] = product(0, weights, columns)
        return carried

    lax.fori_loop(0, 3 * width // tile, project, 0)
    low_rank = product(0, down_ref, slice(None)).astype(bf16)
    low_rank_ref[...] = low_rank
    gate_ref[...] = jnp.dot(low_rank, up_own[...], preferred_element_type=f32) + bias_ref[...]
    logits = None
    for part in range(groups):
        value = lax.dot_general(
            rows_of(0, part), beta_weight_ref[:, part * features : (part + 1) * features],
            (((1,), (1,)), ((), ())), preferred_element_type=f32,
        )
        logits = value if logits is None else logits + value
    lane = lax.broadcasted_iota(jnp.int32, logits.shape, 1)
    for head in range(heads):
        picked = jnp.where(lane == member * heads + head, logits, 0.0)
        beta_ref[:, head : head + 1] = jnp.sum(picked, axis=1, keepdims=True)
    pass_on(1)

    def turn(which, target_ref):
        for part in range(groups):
            for index in range(count):
                target_ref[part * features : (part + 1) * features, index * block : (index + 1) * block] = (
                    gathered[which, part, index].T
                )

    turn(0, turned_ref)
    arrive(1)

    def project_grad(step, carried):
        columns = pl.ds(pl.multiple_of(step * tile, tile), tile)
        mixed_grad_ref[:, columns] = product(1, out_weights, columns)
        return carried

    lax.fori_loop(0, width // tile, project_grad, 0)
    turn(1, turned_grad_ref)
    for which in range(2):
        for offset in range(1, count):
            far_copy(which, offset).wait_send()
        for back in range(count):
            for offset in range(1, groups):
                head_copy(which, back, offset).wait_send()


def project(inputs, output_grad, qkv, out_weight, down_weight, up_weight, beta_turned, gate_bias):
    count, groups = lax.axis_size("context"), lax.axis_size("head")
    block, features = inputs.shape
    tokens, model_width = count * block, groups * features
    all_width = out_weight.shape[1] // count
    heads = beta_turned.shape[0] // count
    rank = down_weight.shape[1]
    f32, bf16 = jnp.float32, jnp.bfloat16
    vmem = pl.BlockSpec(memory_space=pltpu.VMEM)
    hbm = pl.BlockSpec(memory_space=pltpu.HBM)
    dma = pltpu.SemaphoreType.DMA
    shape = jax.ShapeDtypeStruct
    return pl.pallas_call(
        project_kernel,
        in_specs=[hbm] * 8,
        out_specs=[vmem] * 7,
        out_shape=[
            shape((tokens, 3 * all_width), f32),
            shape((tokens, all_width), f32),
            shape((tokens, heads), f32),
            shape((tokens, all_width), f32),
            shape((model_width, tokens), bf16),
            shape((model_width, tokens), bf16),
            shape((tokens, rank), bf16),
        ],
        scratch_shapes=[
            pltpu.VMEM((2, groups, count, block, features), bf16),
            pltpu.VMEM((model_width, 3 * all_width), bf16),
            pltpu.VMEM((model_width, all_width), bf16),
            pltpu.VMEM((rank, all_width), bf16),
            pltpu.VMEM(down_weight.shape, bf16),
            pltpu.VMEM(beta_turned.shape, bf16),
            pltpu.VMEM((1, all_width), f32),
            dma((2,)), dma((8,)),
            dma((2, count)), dma((2, count)),
            dma((2, count, groups)), dma((2, count, groups)),
        ],
        compiler_params=pltpu.CompilerParams(
            collective_id=2, has_side_effects=True, vmem_limit_bytes=60 * 1024 * 1024
        ),
    )(inputs, output_grad, qkv, out_weight, down_weight, up_weight, beta_turned, gate_bias)


def exchange_kernel(
    turned_ref, turned_grad_ref, proj_ref, mixed_ref, gate_ref, logit_ref, low_rank_ref, bias_ref,
    qkv_weight_ref, out_weight_ref, down_hbm, up_ref, beta_hbm,
    qkv_ref, out_ref, input_ref, layer_out_ref, up_out_ref, down_out_ref, beta_out_ref, bias_out_ref,
    down_ref, beta_weight_ref, send_one, recv_one, send_two, recv_two, done_rows,
    parts, head_recv, part_send, part_recv,
    weights, out_weights, up_own, mixed_all, layer_send, layer_recv, layer_own,
    low_grad, logit_keep, up_full, up_slots, up_one, up_two, up_across, up_all,
    down_slots, down_one, down_two, down_across, down_done, down_far, down_group, down_all,
    beta_own, beta_one, beta_sum, beta_two, beta_done, beta_far,
    send_sems, recv_sems, local_sems,
):
    count, block, width = mixed_all.shape
    groups = parts.shape[0]
    features = parts.shape[3]
    slab = done_rows.shape[1]
    heads = logit_ref.shape[1]
    rank = down_ref.shape[1]
    tokens = count * block
    quarter = rank // 4
    f32, bf16 = jnp.float32, jnp.bfloat16
    member, row, group = (lax.axis_index(name) for name in ("context", "dp", "head"))
    near = row + 1 - 2 * lax.rem(row, 2)
    across = lax.rem(row + 2, 4)
    opposite = 3 - row
    slots = (near, opposite, row, across)

    def context_at(offset):
        return lax.rem(member + offset, count)

    def head_at(offset):
        return lax.rem(group + offset, groups)

    meet(
        [("context", context_at(offset)) for offset in range(1, count)]
        + [("head", head_at(offset)) for offset in range(1, groups)]
        + [("dp", near), ("dp", across)]
    )
    offsets = sorted(range(1, count), key=lambda k: -min(k, count - k)) + [0]
    far_offsets = offsets[:-1]
    numbers, flying = {}, {}

    def begin(key, source, target, axis, index):
        number = numbers.setdefault(key, len(numbers))
        flying[key] = remote(
            source, target, send_sems.at[number], recv_sems.at[number], axis, index
        )
        flying[key].start()

    def arrived(*key):
        flying[key].wait_recv()

    def dot(left, right, left_dim=1, right_dim=0):
        return lax.dot_general(
            left, right, (((left_dim,), (right_dim,)), ((), ())), preferred_element_type=f32
        )

    def slab_rows(chosen, index):
        step = 16 if slab % 16 == 0 else 8
        return pl.ds(pl.multiple_of((chosen * 4 + index) * slab, step), slab)

    mine = pl.ds(pl.multiple_of(member * width, width), width)

    def features_of(index):
        step = 16 if features % 16 == 0 else 8
        return pl.multiple_of(index * features, step)

    loads = [
        pltpu.make_async_copy(
            qkv_weight_ref.at[part, :, mine], weights.at[:, pl.ds(part * width, width)],
            local_sems.at[part],
        )
        for part in range(3)
    ]
    loads.append(pltpu.make_async_copy(down_hbm, down_ref, local_sems.at[5]))
    loads.append(pltpu.make_async_copy(beta_hbm, beta_weight_ref, local_sems.at[6]))
    up_load = pltpu.make_async_copy(up_ref.at[:, mine], up_own, local_sems.at[3])

    def out_load(offset):
        return pltpu.make_async_copy(
            out_weight_ref.at[pl.ds(features_of(head_at(offset)), features), :], out_weights,
            local_sems.at[4],
        )

    bits = [1 << place for place in range((count - 1).bit_length())]

    def flip(mask):
        index = member
        for bit in bits:
            if mask & bit:
                index = index + bit - 2 * bit * lax.rem(member // bit, 2)
        return index

    masks = [mask for bit in bits for mask in range(count) if mask & -mask == bit] + [0]
    group_order = list(range(1, groups)) + [0]
    for offset in far_offsets:
        chosen = context_at(offset)
        begin(
            ("mixed", offset),
            mixed_ref.at[pl.ds(pl.multiple_of(chosen * block, block), block), :],
            mixed_all.at[member], "context", chosen,
        )
    up_load.start()
    for load in loads:
        load.start()
    out_load(group_order[0]).start()
    mixed_all[member] = mixed_ref[pl.ds(pl.multiple_of(member * block, block), block), :]

    lane = lax.broadcasted_iota(jnp.int32, (tokens, beta_own.shape[0]), 1)
    logit_all = jnp.zeros(lane.shape, f32)
    for head in range(heads):
        logit_all = jnp.where(lane == member * heads + head, logit_ref[:, head : head + 1], logit_all)
    logit_low = logit_all.astype(bf16)
    logit_keep[...] = logit_low[:, : count * heads]
    up_load.wait()
    low_grad[...] = dot(gate_ref[...], up_own[...], 1, 1).astype(bf16)

    def small_one():
        beta_own[...] = dot(logit_low, turned_ref[...], 0, 1).astype(bf16)
        begin(("beta", 1), beta_own, beta_one, "dp", near)

        def down_terms(chosen, carried):
            for slot, index in enumerate(slots):
                down_slots[slot // 2, chosen, slot % 2] = dot(
                    turned_ref[slab_rows(chosen, index), :], low_grad[...]
                ).astype(bf16)
            return carried

        lax.fori_loop(0, count, down_terms, 0)
        begin(("down", 1), down_slots.at[0], down_one, "dp", near)
        up_full[...] = dot(low_rank_ref[...], gate_ref[...], 0, 0)
        for slot, index in enumerate(slots):
            rows = pl.ds(pl.multiple_of(index * quarter, 8), quarter)
            up_slots[slot, :quarter] = up_full[rows, :].astype(bf16)
            up_slots[slot, quarter:] = jnp.broadcast_to(bias_ref[...], (16, width)).astype(bf16)
        begin(("up", 1), up_slots.at[pl.ds(0, 2)], up_one, "dp", near)

    def products(step, targets):
        chosen = context_at(offsets[step])

        def fill(part, carried):
            columns = pl.ds(pl.multiple_of(part * width, width), width)
            for index, store in targets:
                store(columns, dot(turned_ref[slab_rows(chosen, index), :], proj_ref[:, columns]))
            return carried

        lax.fori_loop(0, 3, fill, 0)
        columns = pl.ds(3 * width, width)
        for index, store in targets:
            store(columns, dot(turned_grad_ref[slab_rows(chosen, index), :], mixed_ref[...]))

    def first(step):
        def sender(slot):
            def store(columns, value):
                send_one[step, slot, :, columns] = value.astype(bf16)

            return store

        products(step, [(near, sender(0)), (opposite, sender(1))])
        begin(("one", step), send_one.at[step], recv_one.at[step], "dp", near)

    def second(step):
        arrived("one", step)

        def store(columns, value):
            total = value + recv_one[step, 1, :, columns].astype(f32)
            send_two[step, :, columns] = total.astype(bf16)

        products(step, [(across, store)])
        begin(("two", step), send_two.at[step], recv_two.at[step], "dp", across)

    def owner_ref(part):
        return out_ref.at[:, mine] if part == 3 else qkv_ref.at[part, :, mine]

    def own_copy(step, part):
        return pltpu.make_async_copy(
            done_rows.at[step, :, pl.ds(part * width, width)], owner_ref(part), local_sems.at[part]
        )

    def third(step):
        arrived("two", step)

        def store(columns, value):
            total = value + recv_one[step, 0, :, columns].astype(f32)
            total = total + recv_two[step, :, columns].astype(f32)
            done_rows[step, :, columns] = total.astype(bf16)

        products(step, [(row, store)])
        offset = offsets[step]
        for part in range(4):
            if offset:
                begin(
                    ("far", offset, part), done_rows.at[step, :, pl.ds(part * width, width)],
                    owner_ref(part), "context", context_at(offset),
                )
            else:
                own_copy(step, part).start()

    tile = 384 if features % 384 == 0 else features

    def input_parts():
        for load in loads:
            load.wait()
        for offset in group_order:
            chosen = head_at(offset)
            base = features_of(chosen)

            def some(step, carried, chosen=chosen, base=base):
                if tile == features:
                    lanes, rows = slice(None), pl.ds(base, tile)
                else:
                    lanes = pl.ds(pl.multiple_of(step * tile, tile), tile)
                    rows = pl.ds(pl.multiple_of(base + step * tile, 128), tile)
                for index in range(count):
                    span = slice(index * block, (index + 1) * block)
                    value = dot(proj_ref[span, :], weights[rows, :], 1, 1)
                    value = value + dot(low_grad[span, :], down_ref[rows, :], 1, 1)
                    value = value + dot(logit_keep[span, :], beta_weight_ref[rows, :], 1, 1)
                    parts[chosen, index, :, lanes] = value.astype(bf16)
                return carried

            lax.fori_loop(0, features // tile, some, 0)
            if offset:
                for mask in masks:
                    begin(
                        ("part", offset, mask), parts.at[chosen, flip(mask)],
                        head_recv.at[offset - 1, flip(mask)], "head", chosen,
                    )

    taken = {mask: [] for mask in range(count)}
    part_slots = {}

    def part_total(mask):
        chosen = flip(mask)
        total = parts[group, chosen].astype(f32)
        for offset in range(1, groups):
            arrived("part", offset, mask)
            total = total + head_recv[offset - 1, chosen].astype(f32)
        for bit in taken[mask]:
            arrived("sum", bit, mask)
            total = total + part_recv[part_slots[bit, mask]].astype(f32)
        return total

    def part_step(bit):
        for mask in masks:
            if mask & -mask == bit:
                part_send[mask] = part_total(mask).astype(bf16)
                slot = part_slots.setdefault((bit, mask - bit), len(part_slots))
                begin(
                    ("sum", bit, mask - bit), part_send.at[mask], part_recv.at[slot],
                    "context", flip(bit),
                )
                taken[mask - bit].append(bit)

    def layer_half(offset, store):
        out_load(offset).wait()

        def some(step, carried):
            if tile == features:
                rows = slice(None)
            else:
                rows = pl.ds(pl.multiple_of(step * tile, tile), tile)
            value = None
            for index in range(count):
                one = dot(
                    mixed_all[index], out_weights[rows, index * width : (index + 1) * width], 1, 1
                )
                value = one if value is None else value + one
            store(rows, value)
            return carried

        lax.fori_loop(0, features // tile, some, 0)

    def layer_peers():
        for offset in far_offsets:
            arrived("mixed", offset)
        for place, offset in enumerate(group_order[:-1]):

            def store(lanes, value, offset=offset):
                layer_send[offset - 1, :, lanes] = value.astype(bf16)

            layer_half(offset, store)
            out_load(group_order[place + 1]).start()
            begin(
                ("layer", offset), layer_send.at[offset - 1], layer_recv.at[offset - 1],
                "head", head_at(offset),
            )

    def layer_mine():
        def store(lanes, value):
            layer_own[:, lanes] = value

        layer_half(0, store)

    def small_two():
        for name in ("beta", "down", "up"):
            arrived(name, 1)
        beta_sum[...] = (beta_own[...].astype(f32) + beta_one[...].astype(f32)).astype(bf16)
        begin(("beta", 2), beta_sum, beta_two, "dp", across)
        for index in range(count):
            down_two[index] = (
                down_slots[1, index, 1].astype(f32) + down_one[index, 1].astype(f32)
            ).astype(bf16)
        begin(("down", 2), down_two, down_across, "dp", across)
        up_two[...] = (up_slots[3].astype(f32) + up_one[1].astype(f32)).astype(bf16)
        begin(("up", 2), up_two, up_across, "dp", across)

    def small_three():
        for name in ("beta", "down", "up"):
            arrived(name, 2)
        for index in range(count):
            down_done[index] = (
                down_slots[1, index, 0].astype(f32)
                + down_one[index, 0].astype(f32)
                + down_across[index].astype(f32)
            ).astype(bf16)
        up_all[member, row] = (
            up_slots[2].astype(f32) + up_one[0].astype(f32) + up_across[...].astype(f32)
        ).astype(bf16)
        beta_done[0] = (beta_sum[...].astype(f32) + beta_two[...].astype(f32)).astype(bf16)
        for offset in far_offsets:
            chosen = context_at(offset)
            begin(("down", "far", offset), down_done.at[chosen], down_far.at[offset], "context", chosen)

    def spread(name, array, held, bit):
        for mask in held:
            place = array.at[flip(mask), row]
            begin((name, bit, mask), place, place, "context", flip(bit))

    def landed(name, held, bit):
        for mask in held:
            arrived(name, bit, mask)

    def up_step(bit, held):
        def run():
            spread("up far", up_all, held, bit)
            place = bits[::-1].index(bit)
            begin(("beta far", bit), beta_done.at[place], beta_far.at[place], "context", flip(bit))

        return run

    def up_wait(bit, held):
        def run():
            landed("up far", held, bit)
            place = bits[::-1].index(bit)
            arrived("beta far", bit)
            total = beta_done[place].astype(f32) + beta_far[place].astype(f32)
            beta_done[place + 1] = total.astype(bf16)

        return run

    def down_step(bit, held):
        return lambda: spread("down far", down_all, held, bit)

    def down_wait(bit, held):
        return lambda: landed("down far", held, bit)

    def small_four():
        total = down_done[member].astype(f32)
        for offset in far_offsets:
            arrived("down", "far", offset)
            total = total + down_far[offset].astype(f32)
        down_group[group] = total.astype(bf16)
        for offset in range(1, groups):
            begin(
                ("down", "head", offset), down_group.at[group], down_group.at[group],
                "head", head_at(offset),
            )

    def small_five():
        for offset in range(1, groups):
            arrived("down", "head", offset)
        total = down_group[0].astype(f32)
        for index in range(1, groups):
            total = total + down_group[index].astype(f32)
        down_all[member, row] = total.astype(bf16)

    def small_six():
        begin(("up", "near"), up_all.at[:, row], up_all.at[:, row], "dp", near)
        begin(("down", "near"), down_all.at[:, row], down_all.at[:, row], "dp", near)

    def small_seven():
        arrived("up", "near")
        arrived("down", "near")
        for place, index in enumerate((row, near)):
            begin(("up", "across", place), up_all.at[:, index], up_all.at[:, index], "dp", across)
            begin(
                ("down", "across", place), down_all.at[:, index], down_all.at[:, index], "dp", across
            )

    def small_last():
        for place in range(2):
            arrived("up", "across", place)
            arrived("down", "across", place)
        for index in range(count):
            columns = slice(index * width, (index + 1) * width)
            for part in range(4):
                up_out_ref[part * quarter : (part + 1) * quarter, columns] = up_all[
                    index, part, :quarter
                ].astype(f32)
                start = (index * 4 + part) * slab
                down_out_ref[start : start + slab, :] = down_all[index, part].astype(f32)
            bias_out_ref[:, columns] = up_all[index, 0, quarter : quarter + 1].astype(f32)
        beta_out_ref[...] = beta_done[len(bits)].astype(f32)[: count * heads]

    steps_up, steps_down, held = [], [], [0]
    for bit in bits[::-1]:
        steps_up.append((up_step(bit, list(held)), up_wait(bit, list(held))))
        steps_down.append((down_step(bit, list(held)), down_wait(bit, list(held))))
        held += [mask + bit for mask in held]
    waiting = [[small_two], [small_three, steps_up[0][0]]]
    stage = [small_four, steps_up[0][1]]
    for later in range(1, len(bits)):
        waiting.append(stage + [steps_up[later][0]])
        stage = [steps_up[later][1]]
    waiting.append(stage + [small_five, steps_down[0][0]])
    for later in range(1, len(bits)):
        waiting.append([steps_down[later - 1][1], steps_down[later][0]])
    waiting += [[steps_down[-1][1], small_six], [small_seven]]
    part_steps = [lambda bit=bit: part_step(bit) for bit in bits]

    def advance(queue):
        if queue:
            ready = queue.pop(0)
            for action in ready if isinstance(ready, list) else [ready]:
                action()

    layer_steps = [layer_peers, layer_mine]
    first(0)
    input_parts()
    second(0)
    small_one()
    for step in range(1, count):
        first(step)
        advance(waiting)
        second(step)
        advance(part_steps)
        third(step - 1)
        advance(layer_steps)
        advance(waiting)
    while waiting:
        advance(waiting)
    while part_steps:
        advance(part_steps)
    third(count - 1)

    total = layer_own[...]
    for offset in range(1, groups):
        arrived("layer", offset)
        total = total + layer_recv[offset - 1].astype(f32)
    layer_out_ref[...] = total.astype(bf16)
    input_ref[...] = part_total(0).astype(bf16)
    small_last()
    for offset in far_offsets:
        for part in range(4):
            arrived("far", offset, part)
    for part in range(4):
        own_copy(count - 1, part).wait()
    for copy in flying.values():
        copy.wait_send()


def exchange(
    turned, turned_grad, proj_low, mixed, gate_low, logit_grad, low_rank, bias_term,
    qkv_weight, out_weight, down_weight, up_weight, beta_weight,
):
    count, groups, parts = (lax.axis_size(name) for name in ("context", "head", "dp"))
    assert parts == 4
    model_width, tokens = turned.shape
    width, rank = mixed.shape[1], down_weight.shape[1]
    head_count = beta_weight.shape[1]
    slab, block, features = model_width // (count * parts), tokens // count, model_width // groups
    quarter = rank // parts
    lines = max(16, head_count)
    f32, bf16 = jnp.float32, jnp.bfloat16
    vmem = pl.BlockSpec(memory_space=pltpu.VMEM)
    hbm = pl.BlockSpec(memory_space=pltpu.HBM)
    dma = pltpu.SemaphoreType.DMA
    shape = jax.ShapeDtypeStruct
    copies = 24 * count
    return pl.pallas_call(
        exchange_kernel,
        in_specs=[vmem] * 8 + [hbm] * 5,
        out_specs=[hbm, hbm] + [vmem] * 6,
        out_shape=[
            shape((3, slab, count * width), bf16),
            shape((slab, count * width), bf16),
            shape((block, features), bf16),
            shape((block, features), bf16),
            shape((rank, count * width), f32),
            shape((model_width, rank), f32),
            shape((head_count, model_width), f32),
            shape((1, count * width), f32),
        ],
        scratch_shapes=[
            pltpu.VMEM(down_weight.shape, bf16),
            pltpu.VMEM(beta_weight.shape, bf16),
            pltpu.VMEM((count, 2, slab, 4 * width), bf16),
            pltpu.VMEM((count, 2, slab, 4 * width), bf16),
            pltpu.VMEM((count, slab, 4 * width), bf16),
            pltpu.VMEM((count, slab, 4 * width), bf16),
            pltpu.VMEM((count, slab, 4 * width), bf16),
            pltpu.VMEM((groups, count, block, features), bf16),
            pltpu.VMEM((groups - 1, count, block, features), bf16),
            pltpu.VMEM((count, block, features), bf16),
            pltpu.VMEM((count, block, features), bf16),
            pltpu.VMEM((model_width, 3 * width), bf16),
            pltpu.VMEM((features, count * width), bf16),
            pltpu.VMEM((rank, width), bf16),
            pltpu.VMEM((count, block, width), bf16),
            pltpu.VMEM((groups - 1, block, features), bf16),
            pltpu.VMEM((groups - 1, block, features), bf16),
            pltpu.VMEM((block, features), f32),
            pltpu.VMEM((tokens, rank), bf16),
            pltpu.VMEM((tokens, head_count), bf16),
            pltpu.VMEM((rank, width), f32),
            pltpu.VMEM((4, quarter + 16, width), bf16),
            pltpu.VMEM((2, quarter + 16, width), bf16),
            pltpu.VMEM((quarter + 16, width), bf16),
            pltpu.VMEM((quarter + 16, width), bf16),
            pltpu.VMEM((count, 4, quarter + 16, width), bf16),
            pltpu.VMEM((2, count, 2, slab, rank), bf16),
            pltpu.VMEM((count, 2, slab, rank), bf16),
            pltpu.VMEM((count, slab, rank), bf16),
            pltpu.VMEM((count, slab, rank), bf16),
            pltpu.VMEM((count, slab, rank), bf16),
            pltpu.VMEM((count, slab, rank), bf16),
            pltpu.VMEM((groups, slab, rank), bf16),
            pltpu.VMEM((count, 4, slab, rank), bf16),
            pltpu.VMEM((lines, model_width), bf16),
            pltpu.VMEM((lines, model_width), bf16),
            pltpu.VMEM((lines, model_width), bf16),
            pltpu.VMEM((lines, model_width), bf16),
            pltpu.VMEM((count.bit_length(), lines, model_width), bf16),
            pltpu.VMEM((count.bit_length(), lines, model_width), bf16),
            dma((copies,)), dma((copies,)), dma((7,)),
        ],
        compiler_params=pltpu.CompilerParams(
            collective_id=1, has_side_effects=True, vmem_limit_bytes=60 * 1024 * 1024
        ),
    )(
        turned, turned_grad, proj_low, mixed, gate_low, logit_grad, low_rank, bias_term,
        qkv_weight, out_weight, down_weight, up_weight, beta_weight,
    )


def finish_kernel(*refs):
    count = (len(refs) - 1) // 2
    copies = [
        pltpu.make_async_copy(refs[place], refs[count + place], refs[-1].at[place])
        for place in range(count)
    ]
    for copy in copies:
        copy.start()
    for copy in copies:
        copy.wait()


def finish(*arrays):
    anywhere = pl.BlockSpec(memory_space=pl.ANY)
    return pl.pallas_call(
        finish_kernel,
        in_specs=[anywhere] * len(arrays),
        out_specs=[pl.BlockSpec(memory_space=pltpu.HBM)] * len(arrays),
        out_shape=[jax.ShapeDtypeStruct(array.shape, array.dtype) for array in arrays],
        scratch_shapes=[pltpu.SemaphoreType.DMA((len(arrays),))],
    )(*arrays)


def shards(
    inputs, output_grad, qkv_weight, out_weight, down_weight, up_weight, beta_weight, gate_bias
):
    qkv_turned = jnp.transpose(qkv_weight, (1, 0, 2))
    projected, gate_pre, beta_logit, mixed_grad, turned, turned_grad, low_rank = project(
        inputs[0], output_grad[0], qkv_turned, out_weight, down_weight, up_weight, beta_weight.T,
        gate_bias[None],
    )
    mixed, proj_low, gate_low, logit_grad, bias_term = recurrence(
        projected, gate_pre, beta_logit, mixed_grad
    )
    results = exchange(
        turned, turned_grad, proj_low, mixed, gate_low, logit_grad, low_rank, bias_term,
        qkv_turned, out_weight, down_weight, up_weight, beta_weight,
    )
    qkv_grad, out_grad, input_grad, layer_out, up_grad, down_grad, beta_grad, bias_grad = finish(
        *results
    )
    qkv_grad = jnp.transpose(qkv_grad, (1, 0, 2))
    return (
        layer_out[None], input_grad[None], qkv_grad, out_grad, up_grad, down_grad, beta_grad.T,
        bias_grad[0],
    )


def solution(mesh):
    return jax.shard_map(
        shards,
        mesh=mesh,
        in_specs=(
            P("dp", "context", "head"),
            P("dp", "context", "head"),
            P(None, None, "head"),
            P(None, "head"),
            P(),
            P(None, "head"),
            P(None, "head"),
            P("head"),
        ),
        out_specs=(
            P("dp", "context", "head"),
            P("dp", "context", "head"),
            P(("context", "dp"), None, "head"),
            P(("context", "dp"), "head"),
            P(None, "head"),
            P(),
            P(None, "head"),
            P("head"),
        ),
        check_vma=False,
    )
```

```python
import jax
import jax.numpy as jnp
from jax import lax
from jax.experimental import pallas as pl
from jax.experimental.pallas import tpu as pltpu
from jax.sharding import PartitionSpec as P

SPAN = 64
epsilon = 1e-06


def mm(left, right, left_dim, right_dim):
    return lax.dot_general(
        left.astype(jnp.bfloat16),
        right.astype(jnp.bfloat16),
        (((left_dim,), (right_dim,)), ((), ())),
        preferred_element_type=jnp.float32,
    )


def halves(value):
    high = value.astype(jnp.bfloat16)
    return high, (value - high.astype(jnp.float32)).astype(jnp.bfloat16)


def mask_mm(mask, value, mask_dim, value_dim):
    high, low = halves(value)
    return mm(mask, high, mask_dim, value_dim) + mm(mask, low, mask_dim, value_dim)


def square_mm(rows, square):
    row_high, row_low = halves(rows)
    high, low = halves(square)
    return mm(row_high, low, 1, 0) + mm(row_low, high, 1, 0) + mm(row_high, high, 1, 0)


def norm_of(values):
    return lax.rsqrt(jnp.sum(values * values, axis=-1, keepdims=True) + epsilon)


def recurrence_passes(
    proj_ref, gate_ref, beta_ref, grad_ref,
    mixed_ref, proj_low_ref, gate_low_ref, logit_ref, bias_ref,
    state_ref, inverse_ref, scores_ref, coupling_ref, u_ref, carry_ref,
):
    heads, slots, width, _ = state_ref.shape
    blocks = slots - 1
    all_width = heads * width
    row_index = lax.broadcasted_iota(jnp.int32, (SPAN, SPAN), 0)
    col_index = lax.broadcasted_iota(jnp.int32, (SPAN, SPAN), 1)
    lower = row_index >= col_index
    strict = row_index > col_index
    eye = (row_index == col_index).astype(jnp.float32)
    lower_mask = lower.astype(jnp.bfloat16)
    ones = jnp.ones((SPAN, width), jnp.bfloat16)
    one_rows = jnp.ones((8, width), jnp.bfloat16)
    head_list = range(heads)

    def columns(head, part=0):
        return slice(part * all_width + head * width, part * all_width + (head + 1) * width)

    def prepare(rows):
        sig = lax.logistic(gate_ref[rows, :])
        decays = -0.25 * sig
        cumulative = mask_mm(lower_mask, decays, 1, 0)
        betas = lax.logistic(beta_ref[rows, :])
        made = []
        for head in head_list:
            cum = cumulative[:, columns(head)]
            query_raw = proj_ref[rows, columns(head, 0)]
            key_raw = proj_ref[rows, columns(head, 1)]
            query_norm, key_norm = norm_of(query_raw), norm_of(key_raw)
            queries, keys = query_raw * query_norm, key_raw * key_norm
            middle, final = cum[SPAN // 2 - 1 : SPAN // 2], cum[SPAN - 1 :]
            grow, back = jnp.exp(cum - middle), jnp.exp(middle - cum)
            start, end = jnp.exp(middle), jnp.exp(final - middle)
            key_fwd, key_back, query_fwd = grow * keys, back * keys, grow * queries
            made.append(dict(
                sig=sig[:, columns(head)],
                beta=betas[:, head : head + 1],
                queries=queries, keys=keys, query_norm=query_norm, key_norm=key_norm,
                grow=grow, back=back, start=start, end=end, final=final,
                key_fwd=key_fwd, key_back=key_back, query_fwd=query_fwd,
                key_start=key_fwd * start, query_start=query_fwd * start, key_end=key_back * end,
                decay=jnp.exp(sum(mm(half, ones, 0, 0) for half in halves(decays[:, columns(head)]))),
                values=proj_ref[rows, columns(head, 2)],
            ))
        return made

    def rows_of(block):
        return pl.ds(pl.multiple_of(block * SPAN, SPAN), SPAN)

    def forward(block, carried):
        rows = rows_of(block)
        made = prepare(rows)
        powers, inverses = [], []
        for head, it in enumerate(made):
            both = mm(jnp.concatenate([it["key_fwd"], it["query_fwd"]], axis=0), it["key_back"], 1, 1)
            coupling = jnp.where(strict, both[:SPAN], 0.0)
            scores = jnp.where(lower, both[SPAN:], 0.0)
            coupling_ref[head, block] = coupling
            scores_ref[head, block] = scores.astype(jnp.bfloat16)
            power = -it["beta"] * coupling
            powers.append(power)
            inverses.append(eye + power)
        powers = [square_mm(power, power) for power in powers]
        for section in range(2, (SPAN - 1).bit_length()):
            stacked = [
                square_mm(jnp.concatenate([inverse, power], axis=0), power)
                for inverse, power in zip(inverses, powers)
            ]
            inverses = [inverse + both[:SPAN] for inverse, both in zip(inverses, stacked)]
            powers = [both[SPAN:] for both in stacked]
        inverses = [inverse + square_mm(inverse, power) for inverse, power in zip(inverses, powers)]
        for head in head_list:
            inverse_ref[head, block] = inverses[head].astype(jnp.bfloat16)
        froms = [
            mm(jnp.concatenate([it["key_start"], it["query_start"]], axis=0), state_ref[head, block], 1, 0)
            for head, it in enumerate(made)
        ]
        us = [
            mm(inverse, it["beta"] * (it["values"] - both[:SPAN]), 1, 0)
            for inverse, it, both in zip(inverses, made, froms)
        ]
        for head, it in enumerate(made):
            state_ref[head, block + 1] = it["decay"] * state_ref[head, block] + mm(
                it["key_end"], us[head], 0, 0
            )
            u_ref[head, block] = us[head].astype(jnp.bfloat16)
            mixed = froms[head][SPAN:] + mm(scores_ref[head, block], us[head], 1, 0)
            mixed_ref[rows, columns(head)] = mixed.astype(jnp.bfloat16)
        return carried

    def backward(step, carried):
        block = blocks - 1 - step
        rows = rows_of(block)
        made = prepare(rows)
        grads = [grad_ref[rows, columns(head)] for head in head_list]
        dus = [
            mm(scores_ref[head, block], grads[head], 0, 0) + mm(it["key_end"], carry_ref[head], 1, 0)
            for head, it in enumerate(made)
        ]
        drs = [mm(inverse_ref[head, block], dus[head], 0, 0) for head in head_list]
        logits = jnp.zeros((SPAN, heads), jnp.float32)
        head_index = lax.broadcasted_iota(jnp.int32, (SPAN, heads), 1)
        for head, it in enumerate(made):
            beta, dr, out_grad = it["beta"], drs[head], grads[head]
            state, carry, u = state_ref[head, block], carry_ref[head], u_ref[head, block]
            scaled = beta * dr
            pair = jnp.concatenate([out_grad, -dr], axis=0)
            both = mm(pair, u, 1, 1)
            scores_grad = jnp.where(lower, both[:SPAN], 0.0)
            inner_grad = jnp.where(strict, both[SPAN:], 0.0)
            pair = jnp.concatenate([out_grad, -scaled], axis=0)
            both = mm(pair, state, 1, 1)
            query_start_grad, key_start_grad = both[:SPAN], both[SPAN:]
            key_end_grad = mm(u, carry, 1, 1)
            carry_ref[head] = it["decay"] * carry + mm(
                jnp.concatenate([it["query_start"], it["key_start"]], axis=0), pair, 0, 0
            )
            rest = it["values"] - mm(it["key_start"], state, 1, 0)
            beta_grad = jnp.sum(dr * rest, axis=1, keepdims=True) + jnp.sum(
                inner_grad * coupling_ref[head, block], axis=1, keepdims=True
            )
            square_grads = jnp.concatenate([scores_grad, beta * inner_grad], axis=0)
            both = mm(square_grads, it["key_back"], 1, 0)
            query_fwd_grad, key_fwd_grad = both[:SPAN], both[SPAN:]
            key_back_grad = mm(
                square_grads, jnp.concatenate([it["query_fwd"], it["key_fwd"]], axis=0), 0, 0
            )
            end_term = it["key_end"] * key_end_grad
            query_grow = query_fwd_grad + it["start"] * query_start_grad
            key_grow = key_fwd_grad + it["start"] * key_start_grad
            key_decay = key_back_grad + it["end"] * key_end_grad
            cum_grad = (
                it["query_fwd"] * query_grow + it["key_fwd"] * key_grow - it["key_back"] * key_decay
            )
            final_grad = jnp.sum(end_term, axis=0, keepdims=True) + jnp.exp(it["final"]) * mask_mm(
                one_rows, state * carry, 1, 1
            )[:1]
            decay_grad = mask_mm(lower_mask, cum_grad, 0, 0) + final_grad
            sig = it["sig"]
            gate_grad = decay_grad * (-0.25 * sig * (1.0 - sig))
            query_grad = it["grow"] * query_grow
            key_grad = it["grow"] * key_grow + it["back"] * key_decay

            def through_norm(values, inverse_norm, grad):
                return inverse_norm * (grad - values * jnp.sum(values * grad, axis=1, keepdims=True))

            parts = (
                through_norm(it["queries"], it["query_norm"], query_grad),
                through_norm(it["keys"], it["key_norm"], key_grad),
                scaled,
            )
            for part, value in enumerate(parts):
                proj_low_ref[rows, columns(head, part)] = value.astype(jnp.bfloat16)
            gate_low_ref[rows, columns(head)] = gate_grad.astype(jnp.bfloat16)
            bias_ref[:, columns(head)] += jnp.sum(gate_grad, axis=0, keepdims=True)
            logits = jnp.where(head_index == head, beta_grad * beta * (1.0 - beta), logits)
        logit_ref[rows, :] = logits
        return carried

    for head in head_list:
        state_ref[head, 0] = jnp.zeros((width, width), jnp.float32)
        carry_ref[head] = jnp.zeros((width, width), jnp.float32)
    bias_ref[...] = jnp.zeros_like(bias_ref)
    return (
        lambda first, last: lax.fori_loop(first, last, forward, 0),
        lambda first, last: lax.fori_loop(first, last, backward, 0),
    )


MESH = pl.DeviceIdType.MESH


def remote(source, target, send_sem, recv_sem, axis, index):
    return pltpu.make_async_remote_copy(
        src_ref=source, dst_ref=target, send_sem=send_sem, recv_sem=recv_sem,
        device_id={axis: index}, device_id_type=MESH,
    )


def meet(peers):
    barrier = pltpu.get_barrier_semaphore()
    for axis, index in peers:
        pl.semaphore_signal(barrier, inc=1, device_id={axis: index}, device_id_type=MESH)
    pl.semaphore_wait(barrier, len(peers))


def front_kernel(
    input_ref, grad_ref, qkv_ref, out_weight_ref, down_hbm, up_ref, beta_hbm, bias_hbm,
    turned_ref, low_rank_ref, mixed_ref, proj_low_ref, gate_low_ref, logit_ref, bias_sum_ref,
    layer_out_ref, out_grad_ref,
    gathered, weights, out_weights, up_own, down_ref, beta_weight_ref, bias_ref,
    proj_ref, gate_ref, beta_ref, mixed_grad_ref, turned_grad_ref,
    state_ref, inverse_ref, scores_ref, coupling_ref, u_ref, carry_ref,
    layer_weights, mixed_all, layer_send, layer_recv, layer_own,
    send_one, recv_one, send_two, recv_two, done_rows,
    own_sem, weight_sem, far_send, far_recv, head_send, head_recv, send_sems, recv_sems, local_sems,
):
    groups, count, block, features = gathered.shape[1:]
    heads = beta_ref.shape[1]
    width = up_own.shape[1]
    member, group = lax.axis_index("context"), lax.axis_index("head")
    tokens = count * block
    f32, bf16 = jnp.float32, jnp.bfloat16

    def context_at(offset):
        return lax.rem(member + offset, count)

    def head_at(offset):
        return lax.rem(group + offset, groups)

    row = lax.axis_index("dp")
    near = row + 1 - 2 * lax.rem(row, 2)
    across = lax.rem(row + 2, 4)
    opposite = 3 - row
    meet(
        [("context", context_at(offset)) for offset in range(1, count)]
        + [("head", head_at(offset)) for offset in range(1, groups)]
        + [("dp", near), ("dp", across)]
    )
    near_first = sorted(range(1, count), key=lambda k: min(k, count - k))
    sources = (input_ref, grad_ref)

    def own_copy(which):
        return pltpu.make_async_copy(
            sources[which], gathered.at[which, group, member], own_sem.at[which]
        )

    def far_copy(which, offset):
        return remote(
            sources[which], gathered.at[which, group, member],
            far_send.at[which, offset], far_recv.at[which, offset], "context", context_at(offset),
        )

    def head_copy(which, back, offset):
        source = lax.rem(member + count - back, count)
        place = gathered.at[which, group, source]
        return remote(
            place if back else sources[which], place,
            head_send.at[which, back, offset], head_recv.at[which, back, offset],
            "head", head_at(offset),
        )

    def begin(which):
        own_copy(which).start()
        for offset in range(1, groups):
            head_copy(which, 0, offset).start()
        for offset in near_first:
            far_copy(which, offset).start()

    def pass_on(which, backs):
        for back in backs:
            far_copy(which, back).wait_recv()
            for offset in range(1, groups):
                head_copy(which, back, offset).start()

    def arrive(which):
        own_copy(which).wait()
        for back in range(count):
            for offset in range(1, groups):
                head_copy(which, back, offset).wait_recv()

    mine = pl.ds(pl.multiple_of(member * width, width), width)
    loads = [
        pltpu.make_async_copy(
            qkv_ref.at[part, :, mine], weights.at[:, pl.ds(part * width, width)], weight_sem.at[part]
        )
        for part in range(3)
    ]
    loads.append(pltpu.make_async_copy(out_weight_ref.at[:, mine], out_weights, weight_sem.at[3]))
    loads.append(pltpu.make_async_copy(up_ref.at[:, mine], up_own, weight_sem.at[4]))
    loads.append(pltpu.make_async_copy(down_hbm, down_ref, weight_sem.at[5]))
    loads.append(pltpu.make_async_copy(beta_hbm, beta_weight_ref, weight_sem.at[6]))
    loads.append(pltpu.make_async_copy(bias_hbm.at[:, mine], bias_ref, weight_sem.at[7]))

    begin(0)
    for load in loads:
        load.start()
    pass_on(0, near_first)
    begin(1)
    for load in loads:
        load.wait()
    arrive(0)

    tile = min(width, 256)

    def rows_of(which, part):
        return gathered[which, part].reshape(tokens, features)

    def product(which, right_ref, columns):
        total = None
        for part in range(groups):
            value = jnp.dot(
                rows_of(which, part),
                right_ref[pl.ds(part * features, features), columns],
                preferred_element_type=f32,
            )
            total = value if total is None else total + value
        return total

    def project(step, carried):
        columns = pl.ds(pl.multiple_of(step * tile, tile), tile)
        proj_ref[:, columns] = product(0, weights, columns)
        return carried

    lax.fori_loop(0, 3 * width // tile, project, 0)
    low_rank = product(0, down_ref, slice(None)).astype(bf16)
    low_rank_ref[...] = low_rank
    gate_ref[...] = jnp.dot(low_rank, up_own[...], preferred_element_type=f32) + bias_ref[...]
    logits = None
    for part in range(groups):
        value = lax.dot_general(
            rows_of(0, part), beta_weight_ref[:, part * features : (part + 1) * features],
            (((1,), (1,)), ((), ())), preferred_element_type=f32,
        )
        logits = value if logits is None else logits + value
    lane = lax.broadcasted_iota(jnp.int32, logits.shape, 1)
    for head in range(heads):
        picked = jnp.where(lane == member * heads + head, logits, 0.0)
        beta_ref[:, head : head + 1] = jnp.sum(picked, axis=1, keepdims=True)

    def turn(which, target_ref):
        for part in range(groups):
            for index in range(count):
                target_ref[part * features : (part + 1) * features, index * block : (index + 1) * block] = (
                    gathered[which, part, index].T
                )

    forward, backward = recurrence_passes(
        proj_ref, gate_ref, beta_ref, mixed_grad_ref,
        mixed_ref, proj_low_ref, gate_low_ref, logit_ref, bias_sum_ref,
        state_ref, inverse_ref, scores_ref, coupling_ref, u_ref, carry_ref,
    )
    share = tokens // SPAN // count
    for part in range(count):
        if part < len(near_first):
            pass_on(1, [near_first[part]])
        forward(part * share, (part + 1) * share)

    numbers, flying = {}, {}

    def start(key, source, target, axis, index):
        number = numbers.setdefault(key, len(numbers))
        flying[key] = remote(
            source, target, send_sems.at[number], recv_sems.at[number], axis, index
        )
        flying[key].start()

    def arrived(*key):
        flying[key].wait_recv()

    def dot(left, right, left_dim=1, right_dim=0):
        return lax.dot_general(
            left, right, (((left_dim,), (right_dim,)), ((), ())), preferred_element_type=f32
        )

    far_first = near_first[::-1]
    offsets = far_first + [0]
    for offset in far_first:
        chosen = context_at(offset)
        start(
            ("mixed", offset),
            mixed_ref.at[pl.ds(pl.multiple_of(chosen * block, block), block), :],
            mixed_all.at[member], "context", chosen,
        )
    mixed_all[member] = mixed_ref[pl.ds(pl.multiple_of(member * block, block), block), :]
    group_order = list(range(1, groups)) + [0]
    height = 16 if features % 16 == 0 else 8

    def layer_load(offset):
        base = pl.multiple_of(head_at(offset) * features, height)
        return pltpu.make_async_copy(
            out_weight_ref.at[pl.ds(base, features), :], layer_weights, local_sems.at[0]
        )

    layer_load(group_order[0]).start()
    turn(0, turned_ref)
    arrive(1)
    turn(1, turned_grad_ref)
    slab = done_rows.shape[1]
    step_rows = 16 if slab % 16 == 0 else 8

    def out_term(chosen, index):
        rows = pl.ds(pl.multiple_of((chosen * 4 + index) * slab, step_rows), slab)
        return dot(turned_grad_ref[rows, :], mixed_ref[...])

    def out_one():
        def fill(chosen, carried):
            send_one[chosen, 0] = out_term(chosen, near).astype(bf16)
            send_one[chosen, 1] = out_term(chosen, opposite).astype(bf16)
            return carried

        lax.fori_loop(0, count, fill, 0)
        start(("one",), send_one, recv_one, "dp", near)

    def out_two():
        arrived("one")

        def fill(chosen, carried):
            total = out_term(chosen, across) + recv_one[chosen, 1].astype(f32)
            send_two[chosen] = total.astype(bf16)
            return carried

        lax.fori_loop(0, count, fill, 0)
        start(("two",), send_two, recv_two, "dp", across)

    mine_out = out_grad_ref.at[:, mine]

    def own_out():
        return pltpu.make_async_copy(done_rows.at[member], mine_out, local_sems.at[1])

    def out_three():
        arrived("two")

        def fill(chosen, carried):
            total = out_term(chosen, row) + recv_one[chosen, 0].astype(f32)
            total = total + recv_two[chosen].astype(f32)
            done_rows[chosen] = total.astype(bf16)
            return carried

        lax.fori_loop(0, count, fill, 0)
        for offset in far_first:
            chosen = context_at(offset)
            start(("far", offset), done_rows.at[chosen], mine_out, "context", chosen)
        own_out().start()

    stretch = 384 if features % 384 == 0 else features

    def layer_half(offset, store):
        layer_load(offset).wait()

        def some(step, carried):
            if stretch == features:
                rows = slice(None)
            else:
                rows = pl.ds(pl.multiple_of(step * stretch, stretch), stretch)
            value = None
            for index in range(count):
                one = dot(
                    mixed_all[index], layer_weights[rows, index * width : (index + 1) * width], 1, 1
                )
                value = one if value is None else value + one
            store(rows, value)
            return carried

        lax.fori_loop(0, features // stretch, some, 0)

    def layer_peers():
        for offset in far_first:
            arrived("mixed", offset)
        for place, offset in enumerate(group_order[:-1]):

            def store(lanes, value, offset=offset):
                layer_send[offset - 1, :, lanes] = value.astype(bf16)

            layer_half(offset, store)
            layer_load(group_order[place + 1]).start()
            start(
                ("layer", offset), layer_send.at[offset - 1], layer_recv.at[offset - 1],
                "head", head_at(offset),
            )

    def layer_mine():
        def store(lanes, value):
            layer_own[:, lanes] = value

        layer_half(0, store)

    def project_grad(step, carried):
        columns = pl.ds(pl.multiple_of(step * tile, tile), tile)
        mixed_grad_ref[:, columns] = product(1, out_weights, columns)
        return carried

    out_one()
    lax.fori_loop(0, width // tile, project_grad, 0)
    out_two()
    between = {0: [layer_peers], 1: [layer_mine], 2: [out_three]}
    for part in range(count):
        backward(part * share, (part + 1) * share)
        for action in between.get(part, []):
            action()
    total = layer_own[...]
    for offset in range(1, groups):
        arrived("layer", offset)
        total = total + layer_recv[offset - 1].astype(f32)
    layer_out_ref[...] = total.astype(bf16)
    for offset in far_first:
        arrived("far", offset)
    own_out().wait()
    for copy in flying.values():
        copy.wait_send()
    for which in range(2):
        for offset in range(1, count):
            far_copy(which, offset).wait_send()
        for back in range(count):
            for offset in range(1, groups):
                head_copy(which, back, offset).wait_send()


def front(inputs, output_grad, qkv, out_weight, down_weight, up_weight, beta_turned, gate_bias):
    count, groups = lax.axis_size("context"), lax.axis_size("head")
    block, features = inputs.shape
    tokens, model_width = count * block, groups * features
    all_width = out_weight.shape[1] // count
    heads = beta_turned.shape[0] // count
    rank = down_weight.shape[1]
    f32, bf16 = jnp.float32, jnp.bfloat16
    vmem = pl.BlockSpec(memory_space=pltpu.VMEM)
    hbm = pl.BlockSpec(memory_space=pltpu.HBM)
    dma = pltpu.SemaphoreType.DMA
    shape = jax.ShapeDtypeStruct
    blocks = tokens // SPAN
    head_width = all_width // heads
    slab = model_width // (4 * count)
    return pl.pallas_call(
        front_kernel,
        in_specs=[hbm] * 8,
        out_specs=[vmem] * 8 + [hbm],
        out_shape=[
            shape((model_width, tokens), bf16),
            shape((tokens, rank), bf16),
            shape((tokens, all_width), bf16),
            shape((tokens, 3 * all_width), bf16),
            shape((tokens, all_width), bf16),
            shape((tokens, heads), f32),
            shape((1, all_width), f32),
            shape((block, features), bf16),
            shape((slab, count * all_width), bf16),
        ],
        scratch_shapes=[
            pltpu.VMEM((2, groups, count, block, features), bf16),
            pltpu.VMEM((model_width, 3 * all_width), bf16),
            pltpu.VMEM((model_width, all_width), bf16),
            pltpu.VMEM((rank, all_width), bf16),
            pltpu.VMEM(down_weight.shape, bf16),
            pltpu.VMEM(beta_turned.shape, bf16),
            pltpu.VMEM((1, all_width), f32),
            pltpu.VMEM((tokens, 3 * all_width), f32),
            pltpu.VMEM((tokens, all_width), f32),
            pltpu.VMEM((tokens, heads), f32),
            pltpu.VMEM((tokens, all_width), f32),
            pltpu.VMEM((model_width, tokens), bf16),
            pltpu.VMEM((heads, blocks + 1, head_width, head_width), f32),
            pltpu.VMEM((heads, blocks, SPAN, SPAN), bf16),
            pltpu.VMEM((heads, blocks, SPAN, SPAN), bf16),
            pltpu.VMEM((heads, blocks, SPAN, SPAN), f32),
            pltpu.VMEM((heads, blocks, SPAN, head_width), bf16),
            pltpu.VMEM((heads, head_width, head_width), f32),
            pltpu.VMEM((features, count * all_width), bf16),
            pltpu.VMEM((count, block, all_width), bf16),
            pltpu.VMEM((groups - 1, block, features), bf16),
            pltpu.VMEM((groups - 1, block, features), bf16),
            pltpu.VMEM((block, features), f32),
            pltpu.VMEM((count, 2, slab, all_width), bf16),
            pltpu.VMEM((count, 2, slab, all_width), bf16),
            pltpu.VMEM((count, slab, all_width), bf16),
            pltpu.VMEM((count, slab, all_width), bf16),
            pltpu.VMEM((count, slab, all_width), bf16),
            dma((2,)), dma((8,)),
            dma((2, count)), dma((2, count)),
            dma((2, count, groups)), dma((2, count, groups)),
            dma((4 * count,)), dma((4 * count,)), dma((2,)),
        ],
        compiler_params=pltpu.CompilerParams(
            collective_id=2, has_side_effects=True, vmem_limit_bytes=60 * 1024 * 1024
        ),
    )(inputs, output_grad, qkv, out_weight, down_weight, up_weight, beta_turned, gate_bias)


def exchange_kernel(
    turned_ref, proj_ref, gate_ref, logit_ref, low_rank_ref, bias_ref,
    qkv_weight_ref, down_hbm, up_ref, beta_hbm,
    qkv_ref, input_ref, up_out_ref, down_out_ref, beta_out_ref, bias_out_ref,
    down_ref, beta_weight_ref, send_one, recv_one, send_two, recv_two, done_rows,
    parts, head_recv, part_send, part_recv,
    weights, up_own,
    low_grad, logit_keep, up_full, up_slots, up_one, up_two, up_across, up_all,
    down_slots, down_one, down_two, down_across, down_done, down_far, down_group, down_all,
    beta_own, beta_one, beta_sum, beta_two, beta_done, beta_far,
    send_sems, recv_sems, local_sems,
):
    groups, count, block, features = parts.shape
    width = gate_ref.shape[1]
    slab = done_rows.shape[1]
    heads = logit_ref.shape[1]
    rank = down_ref.shape[1]
    tokens = count * block
    quarter = rank // 4
    f32, bf16 = jnp.float32, jnp.bfloat16
    member, row, group = (lax.axis_index(name) for name in ("context", "dp", "head"))
    near = row + 1 - 2 * lax.rem(row, 2)
    across = lax.rem(row + 2, 4)
    opposite = 3 - row
    slots = (near, opposite, row, across)

    def context_at(offset):
        return lax.rem(member + offset, count)

    def head_at(offset):
        return lax.rem(group + offset, groups)

    meet(
        [("context", context_at(offset)) for offset in range(1, count)]
        + [("head", head_at(offset)) for offset in range(1, groups)]
        + [("dp", near), ("dp", across)]
    )
    offsets = sorted(range(1, count), key=lambda k: -min(k, count - k)) + [0]
    far_offsets = offsets[:-1]
    numbers, flying = {}, {}

    def begin(key, source, target, axis, index):
        number = numbers.setdefault(key, len(numbers))
        flying[key] = remote(
            source, target, send_sems.at[number], recv_sems.at[number], axis, index
        )
        flying[key].start()

    def arrived(*key):
        flying[key].wait_recv()

    def dot(left, right, left_dim=1, right_dim=0):
        return lax.dot_general(
            left, right, (((left_dim,), (right_dim,)), ((), ())), preferred_element_type=f32
        )

    def slab_rows(chosen, index):
        step = 16 if slab % 16 == 0 else 8
        return pl.ds(pl.multiple_of((chosen * 4 + index) * slab, step), slab)

    mine = pl.ds(pl.multiple_of(member * width, width), width)

    def features_of(index):
        step = 16 if features % 16 == 0 else 8
        return pl.multiple_of(index * features, step)

    loads = [
        pltpu.make_async_copy(
            qkv_weight_ref.at[part, :, mine], weights.at[:, pl.ds(part * width, width)],
            local_sems.at[part],
        )
        for part in range(3)
    ]
    loads.append(pltpu.make_async_copy(down_hbm, down_ref, local_sems.at[5]))
    loads.append(pltpu.make_async_copy(beta_hbm, beta_weight_ref, local_sems.at[6]))
    up_load = pltpu.make_async_copy(up_ref.at[:, mine], up_own, local_sems.at[3])

    bits = [1 << place for place in range((count - 1).bit_length())]

    def flip(mask):
        index = member
        for bit in bits:
            if mask & bit:
                index = index + bit - 2 * bit * lax.rem(member // bit, 2)
        return index

    masks = [mask for bit in bits for mask in range(count) if mask & -mask == bit] + [0]
    group_order = list(range(1, groups)) + [0]
    up_load.start()
    for load in loads:
        load.start()

    lane = lax.broadcasted_iota(jnp.int32, (tokens, beta_own.shape[0]), 1)
    logit_all = jnp.zeros(lane.shape, f32)
    for head in range(heads):
        logit_all = jnp.where(lane == member * heads + head, logit_ref[:, head : head + 1], logit_all)
    logit_low = logit_all.astype(bf16)
    logit_keep[...] = logit_low[:, : count * heads]
    up_load.wait()
    low_grad[...] = dot(gate_ref[...], up_own[...], 1, 1).astype(bf16)

    def small_one():
        beta_own[...] = dot(logit_low, turned_ref[...], 0, 1).astype(bf16)
        begin(("beta", 1), beta_own, beta_one, "dp", near)

        def down_terms(chosen, carried):
            for slot, index in enumerate(slots):
                down_slots[slot // 2, chosen, slot % 2] = dot(
                    turned_ref[slab_rows(chosen, index), :], low_grad[...]
                ).astype(bf16)
            return carried

        lax.fori_loop(0, count, down_terms, 0)
        begin(("down", 1), down_slots.at[0], down_one, "dp", near)
        up_full[...] = dot(low_rank_ref[...], gate_ref[...], 0, 0)
        for slot, index in enumerate(slots):
            rows = pl.ds(pl.multiple_of(index * quarter, 8), quarter)
            up_slots[slot, :quarter] = up_full[rows, :].astype(bf16)
            up_slots[slot, quarter:] = jnp.broadcast_to(bias_ref[...], (16, width)).astype(bf16)
        begin(("up", 1), up_slots.at[pl.ds(0, 2)], up_one, "dp", near)

    def products(step, targets):
        chosen = context_at(offsets[step])

        def fill(part, carried):
            columns = pl.ds(pl.multiple_of(part * width, width), width)
            for index, store in targets:
                store(columns, dot(turned_ref[slab_rows(chosen, index), :], proj_ref[:, columns]))
            return carried

        lax.fori_loop(0, 3, fill, 0)

    def first(step):
        def sender(slot):
            def store(columns, value):
                send_one[step, slot, :, columns] = value.astype(bf16)

            return store

        products(step, [(near, sender(0)), (opposite, sender(1))])
        begin(("one", step), send_one.at[step], recv_one.at[step], "dp", near)

    def second(step):
        arrived("one", step)

        def store(columns, value):
            total = value + recv_one[step, 1, :, columns].astype(f32)
            send_two[step, :, columns] = total.astype(bf16)

        products(step, [(across, store)])
        begin(("two", step), send_two.at[step], recv_two.at[step], "dp", across)

    def owner_ref(part):
        return qkv_ref.at[part, :, mine]

    def own_copy(step, part):
        return pltpu.make_async_copy(
            done_rows.at[step, :, pl.ds(part * width, width)], owner_ref(part), local_sems.at[part]
        )

    def third(step):
        arrived("two", step)

        def store(columns, value):
            total = value + recv_one[step, 0, :, columns].astype(f32)
            total = total + recv_two[step, :, columns].astype(f32)
            done_rows[step, :, columns] = total.astype(bf16)

        products(step, [(row, store)])
        offset = offsets[step]
        for part in range(3):
            if offset:
                begin(
                    ("far", offset, part), done_rows.at[step, :, pl.ds(part * width, width)],
                    owner_ref(part), "context", context_at(offset),
                )
            else:
                own_copy(step, part).start()

    tile = 384 if features % 384 == 0 else features

    def input_parts():
        for load in loads:
            load.wait()
        for offset in group_order:
            chosen = head_at(offset)
            base = features_of(chosen)

            def some(step, carried, chosen=chosen, base=base):
                if tile == features:
                    lanes, rows = slice(None), pl.ds(base, tile)
                else:
                    lanes = pl.ds(pl.multiple_of(step * tile, tile), tile)
                    rows = pl.ds(pl.multiple_of(base + step * tile, 128), tile)
                for index in range(count):
                    span = slice(index * block, (index + 1) * block)
                    value = dot(proj_ref[span, :], weights[rows, :], 1, 1)
                    value = value + dot(low_grad[span, :], down_ref[rows, :], 1, 1)
                    value = value + dot(logit_keep[span, :], beta_weight_ref[rows, :], 1, 1)
                    parts[chosen, index, :, lanes] = value.astype(bf16)
                return carried

            lax.fori_loop(0, features // tile, some, 0)
            if offset:
                for mask in masks:
                    begin(
                        ("part", offset, mask), parts.at[chosen, flip(mask)],
                        head_recv.at[offset - 1, flip(mask)], "head", chosen,
                    )

    taken = {mask: [] for mask in range(count)}
    part_slots = {}

    def part_total(mask):
        chosen = flip(mask)
        total = parts[group, chosen].astype(f32)
        for offset in range(1, groups):
            arrived("part", offset, mask)
            total = total + head_recv[offset - 1, chosen].astype(f32)
        for bit in taken[mask]:
            arrived("sum", bit, mask)
            total = total + part_recv[part_slots[bit, mask]].astype(f32)
        return total

    def part_step(bit):
        for mask in masks:
            if mask & -mask == bit:
                part_send[mask] = part_total(mask).astype(bf16)
                slot = part_slots.setdefault((bit, mask - bit), len(part_slots))
                begin(
                    ("sum", bit, mask - bit), part_send.at[mask], part_recv.at[slot],
                    "context", flip(bit),
                )
                taken[mask - bit].append(bit)

    def small_two():
        for name in ("beta", "down", "up"):
            arrived(name, 1)
        beta_sum[...] = (beta_own[...].astype(f32) + beta_one[...].astype(f32)).astype(bf16)
        begin(("beta", 2), beta_sum, beta_two, "dp", across)
        for index in range(count):
            down_two[index] = (
                down_slots[1, index, 1].astype(f32) + down_one[index, 1].astype(f32)
            ).astype(bf16)
        begin(("down", 2), down_two, down_across, "dp", across)
        up_two[...] = (up_slots[3].astype(f32) + up_one[1].astype(f32)).astype(bf16)
        begin(("up", 2), up_two, up_across, "dp", across)

    def small_three():
        for name in ("beta", "down", "up"):
            arrived(name, 2)
        for index in range(count):
            down_done[index] = (
                down_slots[1, index, 0].astype(f32)
                + down_one[index, 0].astype(f32)
                + down_across[index].astype(f32)
            ).astype(bf16)
        up_all[member, row] = (
            up_slots[2].astype(f32) + up_one[0].astype(f32) + up_across[...].astype(f32)
        ).astype(bf16)
        beta_done[0] = (beta_sum[...].astype(f32) + beta_two[...].astype(f32)).astype(bf16)
        for offset in far_offsets:
            chosen = context_at(offset)
            begin(("down", "far", offset), down_done.at[chosen], down_far.at[offset], "context", chosen)

    def spread(name, array, held, bit):
        for mask in held:
            place = array.at[flip(mask), row]
            begin((name, bit, mask), place, place, "context", flip(bit))

    def landed(name, held, bit):
        for mask in held:
            arrived(name, bit, mask)

    def up_step(bit, held):
        def run():
            spread("up far", up_all, held, bit)
            place = bits[::-1].index(bit)
            begin(("beta far", bit), beta_done.at[place], beta_far.at[place], "context", flip(bit))

        return run

    def up_wait(bit, held):
        def run():
            landed("up far", held, bit)
            place = bits[::-1].index(bit)
            arrived("beta far", bit)
            total = beta_done[place].astype(f32) + beta_far[place].astype(f32)
            beta_done[place + 1] = total.astype(bf16)

        return run

    def down_step(bit, held):
        return lambda: spread("down far", down_all, held, bit)

    def down_wait(bit, held):
        return lambda: landed("down far", held, bit)

    def small_four():
        total = down_done[member].astype(f32)
        for offset in far_offsets:
            arrived("down", "far", offset)
            total = total + down_far[offset].astype(f32)
        down_group[group] = total.astype(bf16)
        for offset in range(1, groups):
            begin(
                ("down", "head", offset), down_group.at[group], down_group.at[group],
                "head", head_at(offset),
            )

    def small_five():
        for offset in range(1, groups):
            arrived("down", "head", offset)
        total = down_group[0].astype(f32)
        for index in range(1, groups):
            total = total + down_group[index].astype(f32)
        down_all[member, row] = total.astype(bf16)

    def small_six():
        begin(("up", "across"), up_all.at[:, row], up_all.at[:, row], "dp", across)
        begin(("down", "across"), down_all.at[:, row], down_all.at[:, row], "dp", across)

    def small_seven():
        arrived("up", "across")
        arrived("down", "across")
        for place, index in enumerate((row, across)):
            begin(("up", "near", place), up_all.at[:, index], up_all.at[:, index], "dp", near)
            begin(("down", "near", place), down_all.at[:, index], down_all.at[:, index], "dp", near)

    def small_last():
        for place in range(2):
            arrived("up", "near", place)
            arrived("down", "near", place)
        for index in range(count):
            columns = slice(index * width, (index + 1) * width)
            for part in range(4):
                up_out_ref[part * quarter : (part + 1) * quarter, columns] = up_all[
                    index, part, :quarter
                ].astype(f32)
                start = (index * 4 + part) * slab
                down_out_ref[start : start + slab, :] = down_all[index, part].astype(f32)
            bias_out_ref[:, columns] = up_all[index, 0, quarter : quarter + 1].astype(f32)
        beta_out_ref[...] = beta_done[len(bits)].astype(f32)[: count * heads]

    steps_up, steps_down, held = [], [], [0]
    for bit in bits[::-1]:
        steps_up.append((up_step(bit, list(held)), up_wait(bit, list(held))))
        steps_down.append((down_step(bit, list(held)), down_wait(bit, list(held))))
        held += [mask + bit for mask in held]
    waiting = [[small_two], [small_three, steps_up[0][0]]]
    stage = [small_four, steps_up[0][1]]
    for later in range(1, len(bits)):
        waiting.append(stage + [steps_up[later][0]])
        stage = [steps_up[later][1]]
    waiting.append(stage + [small_five, steps_down[0][0]])
    for later in range(1, len(bits)):
        waiting.append([steps_down[later - 1][1], steps_down[later][0]])
    waiting += [[steps_down[-1][1], small_six], [small_seven]]
    part_steps = [lambda bit=bit: part_step(bit) for bit in bits]

    def advance(queue):
        if queue:
            ready = queue.pop(0)
            for action in ready if isinstance(ready, list) else [ready]:
                action()

    first(0)
    input_parts()
    second(0)
    small_one()
    for step in range(1, count):
        first(step)
        advance(waiting)
        second(step)
        advance(part_steps)
        third(step - 1)
        advance(waiting)
    while waiting:
        advance(waiting)
    while part_steps:
        advance(part_steps)
    third(count - 1)

    input_ref[...] = part_total(0).astype(bf16)
    small_last()
    for offset in far_offsets:
        for part in range(3):
            arrived("far", offset, part)
    for part in range(3):
        own_copy(count - 1, part).wait()
    for copy in flying.values():
        copy.wait_send()


def exchange(
    turned, proj_low, gate_low, logit_grad, low_rank, bias_term,
    qkv_weight, down_weight, up_weight, beta_weight,
):
    count, groups, parts = (lax.axis_size(name) for name in ("context", "head", "dp"))
    assert parts == 4
    model_width, tokens = turned.shape
    width, rank = gate_low.shape[1], down_weight.shape[1]
    head_count = beta_weight.shape[1]
    slab, block, features = model_width // (count * parts), tokens // count, model_width // groups
    quarter = rank // parts
    lines = max(16, head_count)
    f32, bf16 = jnp.float32, jnp.bfloat16
    vmem = pl.BlockSpec(memory_space=pltpu.VMEM)
    hbm = pl.BlockSpec(memory_space=pltpu.HBM)
    dma = pltpu.SemaphoreType.DMA
    shape = jax.ShapeDtypeStruct
    copies = 24 * count
    return pl.pallas_call(
        exchange_kernel,
        in_specs=[vmem] * 6 + [hbm] * 4,
        out_specs=[hbm] + [vmem] * 5,
        out_shape=[
            shape((3, slab, count * width), bf16),
            shape((block, features), bf16),
            shape((rank, count * width), f32),
            shape((model_width, rank), f32),
            shape((head_count, model_width), f32),
            shape((1, count * width), f32),
        ],
        scratch_shapes=[
            pltpu.VMEM(down_weight.shape, bf16),
            pltpu.VMEM(beta_weight.shape, bf16),
            pltpu.VMEM((count, 2, slab, 3 * width), bf16),
            pltpu.VMEM((count, 2, slab, 3 * width), bf16),
            pltpu.VMEM((count, slab, 3 * width), bf16),
            pltpu.VMEM((count, slab, 3 * width), bf16),
            pltpu.VMEM((count, slab, 3 * width), bf16),
            pltpu.VMEM((groups, count, block, features), bf16),
            pltpu.VMEM((groups - 1, count, block, features), bf16),
            pltpu.VMEM((count, block, features), bf16),
            pltpu.VMEM((count, block, features), bf16),
            pltpu.VMEM((model_width, 3 * width), bf16),
            pltpu.VMEM((rank, width), bf16),
            pltpu.VMEM((tokens, rank), bf16),
            pltpu.VMEM((tokens, head_count), bf16),
            pltpu.VMEM((rank, width), f32),
            pltpu.VMEM((4, quarter + 16, width), bf16),
            pltpu.VMEM((2, quarter + 16, width), bf16),
            pltpu.VMEM((quarter + 16, width), bf16),
            pltpu.VMEM((quarter + 16, width), bf16),
            pltpu.VMEM((count, 4, quarter + 16, width), bf16),
            pltpu.VMEM((2, count, 2, slab, rank), bf16),
            pltpu.VMEM((count, 2, slab, rank), bf16),
            pltpu.VMEM((count, slab, rank), bf16),
            pltpu.VMEM((count, slab, rank), bf16),
            pltpu.VMEM((count, slab, rank), bf16),
            pltpu.VMEM((count, slab, rank), bf16),
            pltpu.VMEM((groups, slab, rank), bf16),
            pltpu.VMEM((count, 4, slab, rank), bf16),
            pltpu.VMEM((lines, model_width), bf16),
            pltpu.VMEM((lines, model_width), bf16),
            pltpu.VMEM((lines, model_width), bf16),
            pltpu.VMEM((lines, model_width), bf16),
            pltpu.VMEM((count.bit_length(), lines, model_width), bf16),
            pltpu.VMEM((count.bit_length(), lines, model_width), bf16),
            dma((copies,)), dma((copies,)), dma((7,)),
        ],
        compiler_params=pltpu.CompilerParams(
            collective_id=1, has_side_effects=True, vmem_limit_bytes=60 * 1024 * 1024
        ),
    )(
        turned, proj_low, gate_low, logit_grad, low_rank, bias_term,
        qkv_weight, down_weight, up_weight, beta_weight,
    )


def finish_kernel(*refs):
    count = (len(refs) - 1) // 3
    sources, targets, held = refs[:count], refs[count : 2 * count], refs[2 * count : 3 * count]
    sems = refs[-1]
    into = [pltpu.make_async_copy(sources[k], held[k], sems.at[0, k]) for k in range(count)]
    out = [pltpu.make_async_copy(held[k], targets[k], sems.at[1, k]) for k in range(count)]
    for copy in into:
        copy.start()
    for first, second in zip(into, out):
        first.wait()
        second.start()
    for copy in out:
        copy.wait()


def finish(*arrays):
    hbm = pl.BlockSpec(memory_space=pltpu.HBM)
    return pl.pallas_call(
        finish_kernel,
        in_specs=[hbm] * len(arrays),
        out_specs=[hbm] * len(arrays),
        out_shape=[jax.ShapeDtypeStruct(array.shape, array.dtype) for array in arrays],
        scratch_shapes=[pltpu.VMEM(array.shape, array.dtype) for array in arrays]
        + [pltpu.SemaphoreType.DMA((2, len(arrays)))],
        compiler_params=pltpu.CompilerParams(vmem_limit_bytes=60 * 1024 * 1024),
    )(*arrays)


def shards(
    inputs, output_grad, qkv_weight, out_weight, down_weight, up_weight, beta_weight, gate_bias
):
    qkv_turned = jnp.transpose(qkv_weight, (1, 0, 2))
    turned, low_rank, mixed, proj_low, gate_low, logit_grad, bias_term, layer_out, out_grad = front(
        inputs[0], output_grad[0], qkv_turned, out_weight, down_weight, up_weight, beta_weight.T,
        gate_bias[None],
    )
    results = exchange(
        turned, proj_low, gate_low, logit_grad, low_rank, bias_term,
        qkv_turned, down_weight, up_weight, beta_weight,
    )
    layer_out, out_grad, qkv_grad, input_grad, up_grad, down_grad, beta_grad, bias_grad = finish(
        layer_out, out_grad, *results
    )
    qkv_grad = jnp.transpose(qkv_grad, (1, 0, 2))
    return (
        layer_out[None], input_grad[None], qkv_grad, out_grad, up_grad, down_grad, beta_grad.T,
        bias_grad[0],
    )


def solution(mesh):
    return jax.shard_map(
        shards,
        mesh=mesh,
        in_specs=(
            P("dp", "context", "head"),
            P("dp", "context", "head"),
            P(None, None, "head"),
            P(None, "head"),
            P(),
            P(None, "head"),
            P(None, "head"),
            P("head"),
        ),
        out_specs=(
            P("dp", "context", "head"),
            P("dp", "context", "head"),
            P(("context", "dp"), None, "head"),
            P(("context", "dp"), "head"),
            P(None, "head"),
            P(),
            P(None, "head"),
            P("head"),
        ),
        check_vma=False,
    )
```

```python
import jax
import jax.numpy as jnp
from jax import lax
from jax.experimental import pallas as pl
from jax.experimental.pallas import tpu as pltpu
from jax.sharding import PartitionSpec as P

SPAN = 64
epsilon = 1e-06


def mm(left, right, left_dim, right_dim):
    return lax.dot_general(
        left.astype(jnp.bfloat16),
        right.astype(jnp.bfloat16),
        (((left_dim,), (right_dim,)), ((), ())),
        preferred_element_type=jnp.float32,
    )


def halves(value):
    high = value.astype(jnp.bfloat16)
    return high, (value - high.astype(jnp.float32)).astype(jnp.bfloat16)


def mask_mm(mask, value, mask_dim, value_dim):
    high, low = halves(value)
    return mm(mask, high, mask_dim, value_dim) + mm(mask, low, mask_dim, value_dim)


def square_mm(rows, square):
    row_high, row_low = halves(rows)
    high, low = halves(square)
    return mm(row_high, low, 1, 0) + mm(row_low, high, 1, 0) + mm(row_high, high, 1, 0)


def norm_of(values):
    return lax.rsqrt(jnp.sum(values * values, axis=-1, keepdims=True) + epsilon)


def recurrence_passes(
    proj_ref, gate_ref, beta_ref, grad_ref,
    mixed_ref, proj_low_ref, gate_low_ref, logit_ref, bias_ref,
    state_ref, inverse_ref, scores_ref, coupling_ref, u_ref, carry_ref,
):
    heads, slots, width, _ = state_ref.shape
    blocks = slots - 1
    all_width = heads * width
    row_index = lax.broadcasted_iota(jnp.int32, (SPAN, SPAN), 0)
    col_index = lax.broadcasted_iota(jnp.int32, (SPAN, SPAN), 1)
    lower = row_index >= col_index
    strict = row_index > col_index
    eye = (row_index == col_index).astype(jnp.float32)
    lower_mask = lower.astype(jnp.bfloat16)
    ones = jnp.ones((SPAN, width), jnp.bfloat16)
    one_rows = jnp.ones((8, width), jnp.bfloat16)
    head_list = range(heads)

    def columns(head, part=0):
        return slice(part * all_width + head * width, part * all_width + (head + 1) * width)

    def prepare(rows):
        sig = lax.logistic(gate_ref[rows, :])
        decays = -0.25 * sig
        cumulative = mask_mm(lower_mask, decays, 1, 0)
        betas = lax.logistic(beta_ref[rows, :])
        made = []
        for head in head_list:
            cum = cumulative[:, columns(head)]
            query_raw = proj_ref[rows, columns(head, 0)]
            key_raw = proj_ref[rows, columns(head, 1)]
            query_norm, key_norm = norm_of(query_raw), norm_of(key_raw)
            queries, keys = query_raw * query_norm, key_raw * key_norm
            middle, final = cum[SPAN // 2 - 1 : SPAN // 2], cum[SPAN - 1 :]
            grow, back = jnp.exp(cum - middle), jnp.exp(middle - cum)
            start, end = jnp.exp(middle), jnp.exp(final - middle)
            key_fwd, key_back, query_fwd = grow * keys, back * keys, grow * queries
            made.append(dict(
                sig=sig[:, columns(head)],
                beta=betas[:, head : head + 1],
                queries=queries, keys=keys, query_norm=query_norm, key_norm=key_norm,
                grow=grow, back=back, start=start, end=end, final=final,
                key_fwd=key_fwd, key_back=key_back, query_fwd=query_fwd,
                key_start=key_fwd * start, query_start=query_fwd * start, key_end=key_back * end,
                decay=jnp.exp(sum(mm(half, ones, 0, 0) for half in halves(decays[:, columns(head)]))),
                values=proj_ref[rows, columns(head, 2)],
            ))
        return made

    def rows_of(block):
        return pl.ds(pl.multiple_of(block * SPAN, SPAN), SPAN)

    def forward(block, carried):
        rows = rows_of(block)
        made = prepare(rows)
        powers, inverses = [], []
        for head, it in enumerate(made):
            both = mm(jnp.concatenate([it["key_fwd"], it["query_fwd"]], axis=0), it["key_back"], 1, 1)
            coupling = jnp.where(strict, both[:SPAN], 0.0)
            scores = jnp.where(lower, both[SPAN:], 0.0)
            coupling_ref[head, block] = coupling
            scores_ref[head, block] = scores.astype(jnp.bfloat16)
            power = -it["beta"] * coupling
            powers.append(power)
            inverses.append(eye + power)
        powers = [square_mm(power, power) for power in powers]
        for section in range(2, (SPAN - 1).bit_length()):
            stacked = [
                square_mm(jnp.concatenate([inverse, power], axis=0), power)
                for inverse, power in zip(inverses, powers)
            ]
            inverses = [inverse + both[:SPAN] for inverse, both in zip(inverses, stacked)]
            powers = [both[SPAN:] for both in stacked]
        inverses = [inverse + square_mm(inverse, power) for inverse, power in zip(inverses, powers)]
        for head in head_list:
            inverse_ref[head, block] = inverses[head].astype(jnp.bfloat16)
        froms = [
            mm(jnp.concatenate([it["key_start"], it["query_start"]], axis=0), state_ref[head, block], 1, 0)
            for head, it in enumerate(made)
        ]
        us = [
            mm(inverse, it["beta"] * (it["values"] - both[:SPAN]), 1, 0)
            for inverse, it, both in zip(inverses, made, froms)
        ]
        for head, it in enumerate(made):
            state_ref[head, block + 1] = it["decay"] * state_ref[head, block] + mm(
                it["key_end"], us[head], 0, 0
            )
            u_ref[head, block] = us[head].astype(jnp.bfloat16)
            mixed = froms[head][SPAN:] + mm(scores_ref[head, block], us[head], 1, 0)
            mixed_ref[rows, columns(head)] = mixed.astype(jnp.bfloat16)
        return carried

    def backward(step, carried):
        block = blocks - 1 - step
        rows = rows_of(block)
        made = prepare(rows)
        grads = [grad_ref[rows, columns(head)] for head in head_list]
        dus = [
            mm(scores_ref[head, block], grads[head], 0, 0) + mm(it["key_end"], carry_ref[head], 1, 0)
            for head, it in enumerate(made)
        ]
        drs = [mm(inverse_ref[head, block], dus[head], 0, 0) for head in head_list]
        logits = jnp.zeros((SPAN, heads), jnp.float32)
        head_index = lax.broadcasted_iota(jnp.int32, (SPAN, heads), 1)
        for head, it in enumerate(made):
            beta, dr, out_grad = it["beta"], drs[head], grads[head]
            state, carry, u = state_ref[head, block], carry_ref[head], u_ref[head, block]
            scaled = beta * dr
            pair = jnp.concatenate([out_grad, -dr], axis=0)
            both = mm(pair, u, 1, 1)
            scores_grad = jnp.where(lower, both[:SPAN], 0.0)
            inner_grad = jnp.where(strict, both[SPAN:], 0.0)
            pair = jnp.concatenate([out_grad, -scaled], axis=0)
            both = mm(pair, state, 1, 1)
            query_start_grad, key_start_grad = both[:SPAN], both[SPAN:]
            key_end_grad = mm(u, carry, 1, 1)
            carry_ref[head] = it["decay"] * carry + mm(
                jnp.concatenate([it["query_start"], it["key_start"]], axis=0), pair, 0, 0
            )
            rest = it["values"] - mm(it["key_start"], state, 1, 0)
            beta_grad = jnp.sum(dr * rest, axis=1, keepdims=True) + jnp.sum(
                inner_grad * coupling_ref[head, block], axis=1, keepdims=True
            )
            square_grads = jnp.concatenate([scores_grad, beta * inner_grad], axis=0)
            both = mm(square_grads, it["key_back"], 1, 0)
            query_fwd_grad, key_fwd_grad = both[:SPAN], both[SPAN:]
            key_back_grad = mm(
                square_grads, jnp.concatenate([it["query_fwd"], it["key_fwd"]], axis=0), 0, 0
            )
            end_term = it["key_end"] * key_end_grad
            query_grow = query_fwd_grad + it["start"] * query_start_grad
            key_grow = key_fwd_grad + it["start"] * key_start_grad
            key_decay = key_back_grad + it["end"] * key_end_grad
            cum_grad = (
                it["query_fwd"] * query_grow + it["key_fwd"] * key_grow - it["key_back"] * key_decay
            )
            final_grad = jnp.sum(end_term, axis=0, keepdims=True) + jnp.exp(it["final"]) * mask_mm(
                one_rows, state * carry, 1, 1
            )[:1]
            decay_grad = mask_mm(lower_mask, cum_grad, 0, 0) + final_grad
            sig = it["sig"]
            gate_grad = decay_grad * (-0.25 * sig * (1.0 - sig))
            query_grad = it["grow"] * query_grow
            key_grad = it["grow"] * key_grow + it["back"] * key_decay

            def through_norm(values, inverse_norm, grad):
                return inverse_norm * (grad - values * jnp.sum(values * grad, axis=1, keepdims=True))

            parts = (
                through_norm(it["queries"], it["query_norm"], query_grad),
                through_norm(it["keys"], it["key_norm"], key_grad),
                scaled,
            )
            for part, value in enumerate(parts):
                proj_low_ref[rows, columns(head, part)] = value.astype(jnp.bfloat16)
            gate_low_ref[rows, columns(head)] = gate_grad.astype(jnp.bfloat16)
            bias_ref[:, columns(head)] += jnp.sum(gate_grad, axis=0, keepdims=True)
            logits = jnp.where(head_index == head, beta_grad * beta * (1.0 - beta), logits)
        logit_ref[rows, :] = logits
        return carried

    for head in head_list:
        state_ref[head, 0] = jnp.zeros((width, width), jnp.float32)
        carry_ref[head] = jnp.zeros((width, width), jnp.float32)
    bias_ref[...] = jnp.zeros_like(bias_ref)
    return (
        lambda first, last: lax.fori_loop(first, last, forward, 0),
        lambda first, last: lax.fori_loop(first, last, backward, 0),
    )


MESH = pl.DeviceIdType.MESH


def remote(source, target, send_sem, recv_sem, axis, index):
    return pltpu.make_async_remote_copy(
        src_ref=source, dst_ref=target, send_sem=send_sem, recv_sem=recv_sem,
        device_id={axis: index}, device_id_type=MESH,
    )


def meet(peers):
    barrier = pltpu.get_barrier_semaphore()
    for axis, index in peers:
        pl.semaphore_signal(barrier, inc=1, device_id={axis: index}, device_id_type=MESH)
    pl.semaphore_wait(barrier, len(peers))


def front_kernel(
    input_ref, grad_ref, qkv_ref, out_weight_ref, down_hbm, up_ref, beta_hbm, bias_hbm,
    turned_ref, low_rank_ref, mixed_ref, proj_low_ref, gate_low_ref, logit_ref, bias_sum_ref,
    layer_out_ref, out_grad_ref, low_grad_ref, logit_low_ref, parts_ref,
    gathered, weights, out_weights, up_own, down_ref, beta_weight_ref, bias_ref,
    proj_ref, gate_ref, beta_ref, mixed_grad_ref, turned_grad_ref,
    state_ref, inverse_ref, scores_ref, coupling_ref, u_ref, carry_ref,
    layer_weights, mixed_all, layer_send, layer_recv, layer_own,
    send_one, recv_one, send_two, recv_two, done_rows,
    own_sem, weight_sem, far_send, far_recv, head_send, head_recv, send_sems, recv_sems, local_sems,
):
    groups, count, block, features = gathered.shape[1:]
    heads = beta_ref.shape[1]
    width = up_own.shape[1]
    member, group = lax.axis_index("context"), lax.axis_index("head")
    tokens = count * block
    f32, bf16 = jnp.float32, jnp.bfloat16

    def context_at(offset):
        return lax.rem(member + offset, count)

    def head_at(offset):
        return lax.rem(group + offset, groups)

    row = lax.axis_index("dp")
    near = row + 1 - 2 * lax.rem(row, 2)
    across = lax.rem(row + 2, 4)
    opposite = 3 - row
    meet(
        [("context", context_at(offset)) for offset in range(1, count)]
        + [("head", head_at(offset)) for offset in range(1, groups)]
        + [("dp", near), ("dp", across)]
    )
    near_first = sorted(range(1, count), key=lambda k: min(k, count - k))
    sources = (input_ref, grad_ref)

    def own_copy(which):
        return pltpu.make_async_copy(
            sources[which], gathered.at[which, group, member], own_sem.at[which]
        )

    def far_copy(which, offset):
        sems = far_send.at[which, offset], far_recv.at[which, offset], "context"
        if offset == 2:
            place = gathered.at[which, group, lax.rem(member + count - 1, count)]
            return remote(place, place, *sems, context_at(1))
        return remote(
            sources[which], gathered.at[which, group, member], *sems, context_at(offset)
        )

    def head_copy(which, back, offset):
        source = lax.rem(member + count - back, count)
        place = gathered.at[which, group, source]
        return remote(
            place if back else sources[which], place,
            head_send.at[which, back, offset], head_recv.at[which, back, offset],
            "head", head_at(offset),
        )

    def begin(which):
        own_copy(which).start()
        for offset in range(1, groups):
            head_copy(which, 0, offset).start()
        for offset in near_first:
            if offset != 2:
                far_copy(which, offset).start()

    def pass_on(which, backs):
        for back in backs:
            far_copy(which, back).wait_recv()
            if back == 1 and count > 2:
                far_copy(which, 2).start()
            for offset in range(1, groups):
                head_copy(which, back, offset).start()

    def arrive(which):
        own_copy(which).wait()
        for back in range(count):
            for offset in range(1, groups):
                head_copy(which, back, offset).wait_recv()

    mine = pl.ds(pl.multiple_of(member * width, width), width)
    loads = [
        pltpu.make_async_copy(
            qkv_ref.at[part, :, mine], weights.at[:, pl.ds(part * width, width)], weight_sem.at[part]
        )
        for part in range(3)
    ]
    loads.append(pltpu.make_async_copy(out_weight_ref.at[:, mine], out_weights, weight_sem.at[3]))
    loads.append(pltpu.make_async_copy(up_ref.at[:, mine], up_own, weight_sem.at[4]))
    loads.append(pltpu.make_async_copy(down_hbm, down_ref, weight_sem.at[5]))
    loads.append(pltpu.make_async_copy(beta_hbm, beta_weight_ref, weight_sem.at[6]))
    loads.append(pltpu.make_async_copy(bias_hbm.at[:, mine], bias_ref, weight_sem.at[7]))

    begin(0)
    for load in loads:
        load.start()
    pass_on(0, near_first)
    begin(1)
    for load in loads:
        load.wait()
    arrive(0)

    tile = min(width, 256)

    def rows_of(which, part):
        return gathered[which, part].reshape(tokens, features)

    def product(which, right_ref, columns):
        total = None
        for part in range(groups):
            value = jnp.dot(
                rows_of(which, part),
                right_ref[pl.ds(part * features, features), columns],
                preferred_element_type=f32,
            )
            total = value if total is None else total + value
        return total

    def project(step, carried):
        columns = pl.ds(pl.multiple_of(step * tile, tile), tile)
        proj_ref[:, columns] = product(0, weights, columns)
        return carried

    tiles = 3 * width // tile
    lax.fori_loop(0, tiles // 2, project, 0)
    pass_on(1, near_first[:1])
    lax.fori_loop(tiles // 2, tiles, project, 0)
    low_rank = product(0, down_ref, slice(None)).astype(bf16)
    low_rank_ref[...] = low_rank
    gate_ref[...] = jnp.dot(low_rank, up_own[...], preferred_element_type=f32) + bias_ref[...]
    logits = None
    for part in range(groups):
        value = lax.dot_general(
            rows_of(0, part), beta_weight_ref[:, part * features : (part + 1) * features],
            (((1,), (1,)), ((), ())), preferred_element_type=f32,
        )
        logits = value if logits is None else logits + value
    lane = lax.broadcasted_iota(jnp.int32, logits.shape, 1)
    for head in range(heads):
        picked = jnp.where(lane == member * heads + head, logits, 0.0)
        beta_ref[:, head : head + 1] = jnp.sum(picked, axis=1, keepdims=True)

    def turn(which, target_ref):
        for part in range(groups):
            for index in range(count):
                target_ref[part * features : (part + 1) * features, index * block : (index + 1) * block] = (
                    gathered[which, part, index].T
                )

    forward, backward = recurrence_passes(
        proj_ref, gate_ref, beta_ref, mixed_grad_ref,
        mixed_ref, proj_low_ref, gate_low_ref, logit_ref, bias_sum_ref,
        state_ref, inverse_ref, scores_ref, coupling_ref, u_ref, carry_ref,
    )
    share = tokens // SPAN // count
    for part in range(count):
        if part + 1 < len(near_first):
            pass_on(1, [near_first[part + 1]])
        forward(part * share, (part + 1) * share)

    numbers, flying = {}, {}

    def start(key, source, target, axis, index):
        number = numbers.setdefault(key, len(numbers))
        flying[key] = remote(
            source, target, send_sems.at[number], recv_sems.at[number], axis, index
        )
        flying[key].start()

    def arrived(*key):
        flying[key].wait_recv()

    def dot(left, right, left_dim=1, right_dim=0):
        return lax.dot_general(
            left, right, (((left_dim,), (right_dim,)), ((), ())), preferred_element_type=f32
        )

    far_first = near_first[::-1]
    offsets = far_first + [0]
    for offset in far_first:
        chosen = context_at(offset)
        start(
            ("mixed", offset),
            mixed_ref.at[pl.ds(pl.multiple_of(chosen * block, block), block), :],
            mixed_all.at[member], "context", chosen,
        )
    mixed_all[member] = mixed_ref[pl.ds(pl.multiple_of(member * block, block), block), :]
    group_order = list(range(1, groups)) + [0]
    height = 16 if features % 16 == 0 else 8

    def layer_load(offset):
        base = pl.multiple_of(head_at(offset) * features, height)
        return pltpu.make_async_copy(
            out_weight_ref.at[pl.ds(base, features), :], layer_weights, local_sems.at[0]
        )

    layer_load(group_order[0]).start()
    turn(0, turned_ref)
    arrive(1)
    turn(1, turned_grad_ref)
    slab = done_rows.shape[1]
    step_rows = 16 if slab % 16 == 0 else 8

    def out_term(chosen, index):
        rows = pl.ds(pl.multiple_of((chosen * 4 + index) * slab, step_rows), slab)
        return dot(turned_grad_ref[rows, :], mixed_ref[...])

    def out_one():
        def fill(chosen, carried):
            send_one[chosen, 0] = out_term(chosen, near).astype(bf16)
            send_one[chosen, 1] = out_term(chosen, opposite).astype(bf16)
            return carried

        lax.fori_loop(0, count, fill, 0)
        start(("one",), send_one, recv_one, "dp", near)

    def out_two():
        arrived("one")

        def fill(chosen, carried):
            total = out_term(chosen, across) + recv_one[chosen, 1].astype(f32)
            send_two[chosen] = total.astype(bf16)
            return carried

        lax.fori_loop(0, count, fill, 0)
        start(("two",), send_two, recv_two, "dp", across)

    mine_out = out_grad_ref.at[:, mine]

    def own_out():
        return pltpu.make_async_copy(done_rows.at[member], mine_out, local_sems.at[1])

    def out_three():
        arrived("two")

        def fill(chosen, carried):
            total = out_term(chosen, row) + recv_one[chosen, 0].astype(f32)
            total = total + recv_two[chosen].astype(f32)
            done_rows[chosen] = total.astype(bf16)
            return carried

        lax.fori_loop(0, count, fill, 0)
        for offset in far_first:
            chosen = context_at(offset)
            start(("far", offset), done_rows.at[chosen], mine_out, "context", chosen)
        own_out().start()

    stretch = 384 if features % 384 == 0 else features

    def layer_half(offset, store):
        layer_load(offset).wait()

        def some(step, carried):
            if stretch == features:
                rows = slice(None)
            else:
                rows = pl.ds(pl.multiple_of(step * stretch, stretch), stretch)
            value = None
            for index in range(count):
                one = dot(
                    mixed_all[index], layer_weights[rows, index * width : (index + 1) * width], 1, 1
                )
                value = one if value is None else value + one
            store(rows, value)
            return carried

        lax.fori_loop(0, features // stretch, some, 0)

    def layer_peers():
        for offset in far_first:
            arrived("mixed", offset)
        for place, offset in enumerate(group_order[:-1]):

            def store(lanes, value, offset=offset):
                layer_send[offset - 1, :, lanes] = value.astype(bf16)

            layer_half(offset, store)
            layer_load(group_order[place + 1]).start()
            start(
                ("layer", offset), layer_send.at[offset - 1], layer_recv.at[offset - 1],
                "head", head_at(offset),
            )

    def layer_mine():
        def store(lanes, value):
            layer_own[:, lanes] = value

        layer_half(0, store)

    def project_grad(step, carried):
        columns = pl.ds(pl.multiple_of(step * tile, tile), tile)
        mixed_grad_ref[:, columns] = product(1, out_weights, columns)
        return carried

    out_one()
    lax.fori_loop(0, width // tile, project_grad, 0)
    out_two()
    between = {0: [layer_peers], 1: [layer_mine], 2: [out_three]}
    for part in range(count):
        backward(part * share, (part + 1) * share)
        for action in between.get(part, []):
            action()
    low_grad = dot(gate_low_ref[...], up_own[...], 1, 1).astype(bf16)
    low_grad_ref[...] = low_grad
    lane = lax.broadcasted_iota(jnp.int32, logit_low_ref.shape, 1)
    logit_all = jnp.zeros(lane.shape, f32)
    for head in range(heads):
        logit_all = jnp.where(lane == member * heads + head, logit_ref[:, head : head + 1], logit_all)
    logit_low_ref[...] = logit_all.astype(bf16)
    for part in range(groups):
        for index in range(features // stretch):
            lanes = slice(index * stretch, (index + 1) * stretch)
            rows = slice(part * features + lanes.start, part * features + lanes.stop)
            value = dot(proj_low_ref[...], weights[rows, :], 1, 1)
            value = value + dot(low_grad_ref[...], down_ref[rows, :], 1, 1)
            value = value + dot(
                logit_low_ref[:, : count * heads], beta_weight_ref[:, rows], 1, 0
            )
            parts_ref[part, :, :, lanes] = value.astype(bf16).reshape(count, block, stretch)
    total = layer_own[...]
    for offset in range(1, groups):
        arrived("layer", offset)
        total = total + layer_recv[offset - 1].astype(f32)
    layer_out_ref[...] = total.astype(bf16)
    for offset in far_first:
        arrived("far", offset)
    own_out().wait()
    for copy in flying.values():
        copy.wait_send()
    for which in range(2):
        for offset in range(1, count):
            far_copy(which, offset).wait_send()
        for back in range(count):
            for offset in range(1, groups):
                head_copy(which, back, offset).wait_send()


def front(inputs, output_grad, qkv, out_weight, down_weight, up_weight, beta_turned, gate_bias):
    count, groups = lax.axis_size("context"), lax.axis_size("head")
    block, features = inputs.shape
    tokens, model_width = count * block, groups * features
    all_width = out_weight.shape[1] // count
    heads = beta_turned.shape[0] // count
    rank = down_weight.shape[1]
    f32, bf16 = jnp.float32, jnp.bfloat16
    vmem = pl.BlockSpec(memory_space=pltpu.VMEM)
    hbm = pl.BlockSpec(memory_space=pltpu.HBM)
    dma = pltpu.SemaphoreType.DMA
    shape = jax.ShapeDtypeStruct
    blocks = tokens // SPAN
    head_width = all_width // heads
    slab = model_width // (4 * count)
    return pl.pallas_call(
        front_kernel,
        in_specs=[hbm] * 8,
        out_specs=[vmem] * 8 + [hbm] + [vmem] * 3,
        out_shape=[
            shape((model_width, tokens), bf16),
            shape((tokens, rank), bf16),
            shape((tokens, all_width), bf16),
            shape((tokens, 3 * all_width), bf16),
            shape((tokens, all_width), bf16),
            shape((tokens, heads), f32),
            shape((1, all_width), f32),
            shape((block, features), bf16),
            shape((slab, count * all_width), bf16),
            shape((tokens, rank), bf16),
            shape((tokens, max(16, count * heads)), bf16),
            shape((groups, count, block, features), bf16),
        ],
        scratch_shapes=[
            pltpu.VMEM((2, groups, count, block, features), bf16),
            pltpu.VMEM((model_width, 3 * all_width), bf16),
            pltpu.VMEM((model_width, all_width), bf16),
            pltpu.VMEM((rank, all_width), bf16),
            pltpu.VMEM(down_weight.shape, bf16),
            pltpu.VMEM(beta_turned.shape, bf16),
            pltpu.VMEM((1, all_width), f32),
            pltpu.VMEM((tokens, 3 * all_width), f32),
            pltpu.VMEM((tokens, all_width), f32),
            pltpu.VMEM((tokens, heads), f32),
            pltpu.VMEM((tokens, all_width), f32),
            pltpu.VMEM((model_width, tokens), bf16),
            pltpu.VMEM((heads, blocks + 1, head_width, head_width), f32),
            pltpu.VMEM((heads, blocks, SPAN, SPAN), bf16),
            pltpu.VMEM((heads, blocks, SPAN, SPAN), bf16),
            pltpu.VMEM((heads, blocks, SPAN, SPAN), f32),
            pltpu.VMEM((heads, blocks, SPAN, head_width), bf16),
            pltpu.VMEM((heads, head_width, head_width), f32),
            pltpu.VMEM((features, count * all_width), bf16),
            pltpu.VMEM((count, block, all_width), bf16),
            pltpu.VMEM((groups - 1, block, features), bf16),
            pltpu.VMEM((groups - 1, block, features), bf16),
            pltpu.VMEM((block, features), f32),
            pltpu.VMEM((count, 2, slab, all_width), bf16),
            pltpu.VMEM((count, 2, slab, all_width), bf16),
            pltpu.VMEM((count, slab, all_width), bf16),
            pltpu.VMEM((count, slab, all_width), bf16),
            pltpu.VMEM((count, slab, all_width), bf16),
            dma((2,)), dma((8,)),
            dma((2, count)), dma((2, count)),
            dma((2, count, groups)), dma((2, count, groups)),
            dma((4 * count,)), dma((4 * count,)), dma((2,)),
        ],
        compiler_params=pltpu.CompilerParams(
            collective_id=2, has_side_effects=True, vmem_limit_bytes=60 * 1024 * 1024
        ),
    )(inputs, output_grad, qkv, out_weight, down_weight, up_weight, beta_turned, gate_bias)


def exchange_kernel(
    turned_ref, proj_ref, gate_ref, low_grad, logit_low_ref, low_rank_ref, bias_ref, parts,
    qkv_ref, input_ref, up_out_ref, down_out_ref, beta_out_ref, bias_out_ref,
    send_one, recv_one, send_two, recv_two, done_rows,
    head_recv, part_send, part_recv,
    up_full, up_slots, up_one, up_two, up_across, up_all,
    down_slots, down_one, down_two, down_across, down_done, down_far, down_group, down_all,
    beta_own, beta_one, beta_sum, beta_two, beta_done, beta_far,
    send_sems, recv_sems, local_sems,
):
    groups, count, block, features = parts.shape
    width = gate_ref.shape[1]
    slab = done_rows.shape[1]
    head_count = beta_out_ref.shape[0]
    rank = low_grad.shape[1]
    tokens = count * block
    quarter = rank // 4
    f32, bf16 = jnp.float32, jnp.bfloat16
    member, row, group = (lax.axis_index(name) for name in ("context", "dp", "head"))
    near = row + 1 - 2 * lax.rem(row, 2)
    across = lax.rem(row + 2, 4)
    opposite = 3 - row
    slots = (near, opposite, row, across)

    def context_at(offset):
        return lax.rem(member + offset, count)

    def head_at(offset):
        return lax.rem(group + offset, groups)

    meet(
        [("context", context_at(offset)) for offset in range(1, count)]
        + [("head", head_at(offset)) for offset in range(1, groups)]
        + [("dp", near), ("dp", across)]
    )
    offsets = sorted(range(1, count), key=lambda k: -min(k, count - k)) + [0]
    far_offsets = offsets[:-1]
    numbers, flying = {}, {}

    def begin(key, source, target, axis, index):
        number = numbers.setdefault(key, len(numbers))
        flying[key] = remote(
            source, target, send_sems.at[number], recv_sems.at[number], axis, index
        )
        flying[key].start()

    def arrived(*key):
        flying[key].wait_recv()

    def dot(left, right, left_dim=1, right_dim=0):
        return lax.dot_general(
            left, right, (((left_dim,), (right_dim,)), ((), ())), preferred_element_type=f32
        )

    def slab_rows(chosen, index):
        step = 16 if slab % 16 == 0 else 8
        return pl.ds(pl.multiple_of((chosen * 4 + index) * slab, step), slab)

    mine = pl.ds(pl.multiple_of(member * width, width), width)

    bits = [1 << place for place in range((count - 1).bit_length())]

    def flip(mask):
        index = member
        for bit in bits:
            if mask & bit:
                index = index + bit - 2 * bit * lax.rem(member // bit, 2)
        return index

    masks = [mask for bit in bits for mask in range(count) if mask & -mask == bit] + [0]

    def send_parts(chosen_masks):
        for offset in range(1, groups):
            chosen = head_at(offset)
            for mask in chosen_masks:
                begin(
                    ("part", offset, mask), parts.at[chosen, flip(mask)],
                    head_recv.at[offset - 1, flip(mask)], "head", chosen,
                )

    def small_one():
        beta_own[...] = dot(logit_low_ref[...], turned_ref[...], 0, 1).astype(bf16)
        begin(("beta", 1), beta_own, beta_one, "dp", near)

        def down_terms(chosen, carried):
            for slot, index in enumerate(slots):
                down_slots[slot // 2, chosen, slot % 2] = dot(
                    turned_ref[slab_rows(chosen, index), :], low_grad[...]
                ).astype(bf16)
            return carried

        lax.fori_loop(0, count, down_terms, 0)
        begin(("down", 1), down_slots.at[0], down_one, "dp", near)
        up_full[...] = dot(low_rank_ref[...], gate_ref[...], 0, 0)
        for slot, index in enumerate(slots):
            rows = pl.ds(pl.multiple_of(index * quarter, 8), quarter)
            up_slots[slot, :quarter] = up_full[rows, :].astype(bf16)
            up_slots[slot, quarter:] = jnp.broadcast_to(bias_ref[...], (16, width)).astype(bf16)
        begin(("up", 1), up_slots.at[pl.ds(0, 2)], up_one, "dp", near)

    def products(step, targets):
        chosen = context_at(offsets[step])

        def fill(part, carried):
            columns = pl.ds(pl.multiple_of(part * width, width), width)
            for index, store in targets:
                store(columns, dot(turned_ref[slab_rows(chosen, index), :], proj_ref[:, columns]))
            return carried

        lax.fori_loop(0, 3, fill, 0)

    def first(step):
        def sender(slot):
            def store(columns, value):
                send_one[step, slot, :, columns] = value.astype(bf16)

            return store

        products(step, [(near, sender(0)), (opposite, sender(1))])
        begin(("one", step), send_one.at[step], recv_one.at[step], "dp", near)

    def second(step):
        arrived("one", step)

        def store(columns, value):
            total = value + recv_one[step, 1, :, columns].astype(f32)
            send_two[step, :, columns] = total.astype(bf16)

        products(step, [(across, store)])
        begin(("two", step), send_two.at[step], recv_two.at[step], "dp", across)

    def owner_ref(part):
        return qkv_ref.at[part, :, mine]

    def own_copy(step, part):
        return pltpu.make_async_copy(
            done_rows.at[step, :, pl.ds(part * width, width)], owner_ref(part), local_sems.at[part]
        )

    def third(step):
        arrived("two", step)

        def store(columns, value):
            total = value + recv_one[step, 0, :, columns].astype(f32)
            total = total + recv_two[step, :, columns].astype(f32)
            done_rows[step, :, columns] = total.astype(bf16)

        products(step, [(row, store)])
        offset = offsets[step]
        for part in range(3):
            if offset:
                begin(
                    ("far", offset, part), done_rows.at[step, :, pl.ds(part * width, width)],
                    owner_ref(part), "context", context_at(offset),
                )
            else:
                own_copy(step, part).start()

    taken = {mask: [] for mask in range(count)}
    part_slots = {}

    def part_total(mask):
        chosen = flip(mask)
        total = parts[group, chosen].astype(f32)
        for offset in range(1, groups):
            arrived("part", offset, mask)
            total = total + head_recv[offset - 1, chosen].astype(f32)
        for bit in taken[mask]:
            arrived("sum", bit, mask)
            total = total + part_recv[part_slots[bit, mask]].astype(f32)
        return total

    def part_step(bit):
        for mask in masks:
            if mask & -mask == bit:
                part_send[mask] = part_total(mask).astype(bf16)
                slot = part_slots.setdefault((bit, mask - bit), len(part_slots))
                begin(
                    ("sum", bit, mask - bit), part_send.at[mask], part_recv.at[slot],
                    "context", flip(bit),
                )
                taken[mask - bit].append(bit)

    def small_two():
        for name in ("beta", "down", "up"):
            arrived(name, 1)
        beta_sum[...] = (beta_own[...].astype(f32) + beta_one[...].astype(f32)).astype(bf16)
        begin(("beta", 2), beta_sum, beta_two, "dp", across)
        for index in range(count):
            down_two[index] = (
                down_slots[1, index, 1].astype(f32) + down_one[index, 1].astype(f32)
            ).astype(bf16)
        begin(("down", 2), down_two, down_across, "dp", across)
        up_two[...] = (up_slots[3].astype(f32) + up_one[1].astype(f32)).astype(bf16)
        begin(("up", 2), up_two, up_across, "dp", across)

    def small_three():
        for name in ("beta", "down", "up"):
            arrived(name, 2)
        for index in range(count):
            down_done[index] = (
                down_slots[1, index, 0].astype(f32)
                + down_one[index, 0].astype(f32)
                + down_across[index].astype(f32)
            ).astype(bf16)
        up_all[member, row] = (
            up_slots[2].astype(f32) + up_one[0].astype(f32) + up_across[...].astype(f32)
        ).astype(bf16)
        beta_done[0] = (beta_sum[...].astype(f32) + beta_two[...].astype(f32)).astype(bf16)
        for offset in far_offsets:
            chosen = context_at(offset)
            begin(("down", "far", offset), down_done.at[chosen], down_far.at[offset], "context", chosen)

    def spread(name, array, held, bit):
        for mask in held:
            place = array.at[flip(mask), row]
            begin((name, bit, mask), place, place, "context", flip(bit))

    def landed(name, held, bit):
        for mask in held:
            arrived(name, bit, mask)

    def up_step(bit, held):
        def run():
            spread("up far", up_all, held, bit)
            place = bits[::-1].index(bit)
            begin(("beta far", bit), beta_done.at[place], beta_far.at[place], "context", flip(bit))

        return run

    def up_wait(bit, held):
        def run():
            landed("up far", held, bit)
            place = bits[::-1].index(bit)
            arrived("beta far", bit)
            total = beta_done[place].astype(f32) + beta_far[place].astype(f32)
            beta_done[place + 1] = total.astype(bf16)

        return run

    def down_step(bit, held):
        return lambda: spread("down far", down_all, held, bit)

    def down_wait(bit, held):
        return lambda: landed("down far", held, bit)

    def small_four():
        total = down_done[member].astype(f32)
        for offset in far_offsets:
            arrived("down", "far", offset)
            total = total + down_far[offset].astype(f32)
        down_group[group] = total.astype(bf16)
        for offset in range(1, groups):
            begin(
                ("down", "head", offset), down_group.at[group], down_group.at[group],
                "head", head_at(offset),
            )

    def small_five():
        for offset in range(1, groups):
            arrived("down", "head", offset)
        total = down_group[0].astype(f32)
        for index in range(1, groups):
            total = total + down_group[index].astype(f32)
        down_all[member, row] = total.astype(bf16)

    def small_six():
        begin(("up", "across"), up_all.at[:, row], up_all.at[:, row], "dp", across)
        begin(("down", "across"), down_all.at[:, row], down_all.at[:, row], "dp", across)

    def small_seven():
        arrived("up", "across")
        arrived("down", "across")
        for place, index in enumerate((row, across)):
            begin(("up", "near", place), up_all.at[:, index], up_all.at[:, index], "dp", near)
            begin(("down", "near", place), down_all.at[:, index], down_all.at[:, index], "dp", near)

    def small_last():
        for place in range(2):
            arrived("up", "near", place)
            arrived("down", "near", place)
        for index in range(count):
            columns = slice(index * width, (index + 1) * width)
            for part in range(4):
                up_out_ref[part * quarter : (part + 1) * quarter, columns] = up_all[
                    index, part, :quarter
                ].astype(f32)
                start = (index * 4 + part) * slab
                down_out_ref[start : start + slab, :] = down_all[index, part].astype(f32)
            bias_out_ref[:, columns] = up_all[index, 0, quarter : quarter + 1].astype(f32)
        beta_out_ref[...] = beta_done[len(bits)].astype(f32)[:head_count]

    steps_up, steps_down, held = [], [], [0]
    for bit in bits[::-1]:
        steps_up.append((up_step(bit, list(held)), up_wait(bit, list(held))))
        steps_down.append((down_step(bit, list(held)), down_wait(bit, list(held))))
        held += [mask + bit for mask in held]
    waiting = [[small_two], [small_three, steps_up[0][0]]]
    stage = [small_four, steps_up[0][1]]
    for later in range(1, len(bits)):
        waiting.append(stage + [steps_up[later][0]])
        stage = [steps_up[later][1]]
    waiting.append(stage + [small_five, steps_down[0][0]])
    for later in range(1, len(bits)):
        waiting.append([steps_down[later - 1][1], steps_down[later][0]])
    waiting += [[steps_down[-1][1], small_six], [small_seven]]
    part_steps = [lambda bit=bit: part_step(bit) for bit in bits]

    def advance(queue):
        if queue:
            ready = queue.pop(0)
            for action in ready if isinstance(ready, list) else [ready]:
                action()

    early = [mask for mask in masks if mask & 1]
    send_parts(early)
    small_one()
    first(0)
    advance(waiting)
    second(0)
    for step in range(1, count):
        first(step)
        advance(waiting)
        second(step)
        if step == 1:
            advance(waiting)
            send_parts([mask for mask in masks if mask not in early])
        else:
            advance(part_steps)
        third(step - 1)
        advance(waiting)
    while waiting:
        advance(waiting)
    while part_steps:
        advance(part_steps)
    third(count - 1)

    input_ref[...] = part_total(0).astype(bf16)
    small_last()
    for offset in far_offsets:
        for part in range(3):
            arrived("far", offset, part)
    for part in range(3):
        own_copy(count - 1, part).wait()
    for copy in flying.values():
        copy.wait_send()


def exchange(
    turned, proj_low, gate_low, low_grad, logit_low, low_rank, bias_term, input_parts, head_count
):
    count, groups, parts = (lax.axis_size(name) for name in ("context", "head", "dp"))
    assert parts == 4
    model_width, tokens = turned.shape
    width, rank = gate_low.shape[1], low_grad.shape[1]
    slab, block, features = model_width // (count * parts), tokens // count, model_width // groups
    quarter = rank // parts
    lines = max(16, head_count)
    f32, bf16 = jnp.float32, jnp.bfloat16
    vmem = pl.BlockSpec(memory_space=pltpu.VMEM)
    hbm = pl.BlockSpec(memory_space=pltpu.HBM)
    dma = pltpu.SemaphoreType.DMA
    shape = jax.ShapeDtypeStruct
    copies = 24 * count
    return pl.pallas_call(
        exchange_kernel,
        in_specs=[vmem] * 8,
        out_specs=[hbm] + [vmem] * 5,
        out_shape=[
            shape((3, slab, count * width), bf16),
            shape((block, features), bf16),
            shape((rank, count * width), f32),
            shape((model_width, rank), f32),
            shape((head_count, model_width), f32),
            shape((1, count * width), f32),
        ],
        scratch_shapes=[
            pltpu.VMEM((count, 2, slab, 3 * width), bf16),
            pltpu.VMEM((count, 2, slab, 3 * width), bf16),
            pltpu.VMEM((count, slab, 3 * width), bf16),
            pltpu.VMEM((count, slab, 3 * width), bf16),
            pltpu.VMEM((count, slab, 3 * width), bf16),
            pltpu.VMEM((groups - 1, count, block, features), bf16),
            pltpu.VMEM((count, block, features), bf16),
            pltpu.VMEM((count, block, features), bf16),
            pltpu.VMEM((rank, width), f32),
            pltpu.VMEM((4, quarter + 16, width), bf16),
            pltpu.VMEM((2, quarter + 16, width), bf16),
            pltpu.VMEM((quarter + 16, width), bf16),
            pltpu.VMEM((quarter + 16, width), bf16),
            pltpu.VMEM((count, 4, quarter + 16, width), bf16),
            pltpu.VMEM((2, count, 2, slab, rank), bf16),
            pltpu.VMEM((count, 2, slab, rank), bf16),
            pltpu.VMEM((count, slab, rank), bf16),
            pltpu.VMEM((count, slab, rank), bf16),
            pltpu.VMEM((count, slab, rank), bf16),
            pltpu.VMEM((count, slab, rank), bf16),
            pltpu.VMEM((groups, slab, rank), bf16),
            pltpu.VMEM((count, 4, slab, rank), bf16),
            pltpu.VMEM((lines, model_width), bf16),
            pltpu.VMEM((lines, model_width), bf16),
            pltpu.VMEM((lines, model_width), bf16),
            pltpu.VMEM((lines, model_width), bf16),
            pltpu.VMEM((count.bit_length(), lines, model_width), bf16),
            pltpu.VMEM((count.bit_length(), lines, model_width), bf16),
            dma((copies,)), dma((copies,)), dma((3,)),
        ],
        compiler_params=pltpu.CompilerParams(
            collective_id=1, has_side_effects=True, vmem_limit_bytes=60 * 1024 * 1024
        ),
    )(
        turned, proj_low, gate_low, low_grad, logit_low, low_rank, bias_term, input_parts
    )


def finish_kernel(*refs):
    count = (len(refs) - 1) // 3
    sources, targets, held = refs[:count], refs[count : 2 * count], refs[2 * count : 3 * count]
    sems = refs[-1]
    into = [pltpu.make_async_copy(sources[k], held[k], sems.at[0, k]) for k in range(count)]
    out = [pltpu.make_async_copy(held[k], targets[k], sems.at[1, k]) for k in range(count)]
    for copy in into:
        copy.start()
    for first, second in zip(into, out):
        first.wait()
        second.start()
    for copy in out:
        copy.wait()


def finish(*arrays):
    hbm = pl.BlockSpec(memory_space=pltpu.HBM)
    return pl.pallas_call(
        finish_kernel,
        in_specs=[hbm] * len(arrays),
        out_specs=[hbm] * len(arrays),
        out_shape=[jax.ShapeDtypeStruct(array.shape, array.dtype) for array in arrays],
        scratch_shapes=[pltpu.VMEM(array.shape, array.dtype) for array in arrays]
        + [pltpu.SemaphoreType.DMA((2, len(arrays)))],
        compiler_params=pltpu.CompilerParams(vmem_limit_bytes=60 * 1024 * 1024),
    )(*arrays)


def shards(
    inputs, output_grad, qkv_weight, out_weight, down_weight, up_weight, beta_weight, gate_bias
):
    qkv_turned = jnp.transpose(qkv_weight, (1, 0, 2))
    turned, low_rank, _, proj_low, gate_low, _, bias_term, layer_out, out_grad, *more = front(
        inputs[0], output_grad[0], qkv_turned, out_weight, down_weight, up_weight, beta_weight.T,
        gate_bias[None],
    )
    low_grad, logit_low, input_parts = more
    results = exchange(
        turned, proj_low, gate_low, low_grad, logit_low, low_rank, bias_term, input_parts,
        beta_weight.shape[1],
    )
    layer_out, out_grad, qkv_grad, input_grad, up_grad, down_grad, beta_grad, bias_grad = finish(
        layer_out, out_grad, *results
    )
    qkv_grad = jnp.transpose(qkv_grad, (1, 0, 2))
    return (
        layer_out[None], input_grad[None], qkv_grad, out_grad, up_grad, down_grad, beta_grad.T,
        bias_grad[0],
    )


def solution(mesh):
    return jax.shard_map(
        shards,
        mesh=mesh,
        in_specs=(
            P("dp", "context", "head"),
            P("dp", "context", "head"),
            P(None, None, "head"),
            P(None, "head"),
            P(),
            P(None, "head"),
            P(None, "head"),
            P("head"),
        ),
        out_specs=(
            P("dp", "context", "head"),
            P("dp", "context", "head"),
            P(("context", "dp"), None, "head"),
            P(("context", "dp"), "head"),
            P(None, "head"),
            P(),
            P(None, "head"),
            P("head"),
        ),
        check_vma=False,
    )
```

```python
import jax
import jax.numpy as jnp
from jax import lax
from jax.experimental import pallas as pl
from jax.experimental.pallas import tpu as pltpu
from jax.sharding import PartitionSpec as P

SPAN = 64
epsilon = 1e-06


def mm(left, right, left_dim, right_dim):
    return lax.dot_general(
        left.astype(jnp.bfloat16),
        right.astype(jnp.bfloat16),
        (((left_dim,), (right_dim,)), ((), ())),
        preferred_element_type=jnp.float32,
    )


def halves(value):
    high = value.astype(jnp.bfloat16)
    return high, (value - high.astype(jnp.float32)).astype(jnp.bfloat16)


def mask_mm(mask, value, mask_dim, value_dim):
    high, low = halves(value)
    return mm(mask, high, mask_dim, value_dim) + mm(mask, low, mask_dim, value_dim)


def square_mm(rows, square):
    row_high, row_low = halves(rows)
    high, low = halves(square)
    return mm(row_high, low, 1, 0) + mm(row_low, high, 1, 0) + mm(row_high, high, 1, 0)


def norm_of(values):
    return lax.rsqrt(jnp.sum(values * values, axis=-1, keepdims=True) + epsilon)


def recurrence_passes(
    proj_ref, gate_ref, beta_ref, grad_ref,
    mixed_ref, proj_low_ref, gate_low_ref, logit_ref, bias_ref,
    state_ref, inverse_ref, scores_ref, coupling_ref, u_ref, carry_ref,
):
    heads, slots, width, _ = state_ref.shape
    blocks = slots - 1
    all_width = heads * width
    row_index = lax.broadcasted_iota(jnp.int32, (SPAN, SPAN), 0)
    col_index = lax.broadcasted_iota(jnp.int32, (SPAN, SPAN), 1)
    lower = row_index >= col_index
    strict = row_index > col_index
    eye = (row_index == col_index).astype(jnp.float32)
    lower_mask = lower.astype(jnp.bfloat16)
    ones = jnp.ones((SPAN, width), jnp.bfloat16)
    one_rows = jnp.ones((8, width), jnp.bfloat16)
    head_list = range(heads)

    def columns(head, part=0):
        return slice(part * all_width + head * width, part * all_width + (head + 1) * width)

    def prepare(rows):
        sig = lax.logistic(gate_ref[rows, :])
        decays = -0.25 * sig
        cumulative = mask_mm(lower_mask, decays, 1, 0)
        betas = lax.logistic(beta_ref[rows, :])
        made = []
        for head in head_list:
            cum = cumulative[:, columns(head)]
            query_raw = proj_ref[rows, columns(head, 0)]
            key_raw = proj_ref[rows, columns(head, 1)]
            query_norm, key_norm = norm_of(query_raw), norm_of(key_raw)
            queries, keys = query_raw * query_norm, key_raw * key_norm
            middle, final = cum[SPAN // 2 - 1 : SPAN // 2], cum[SPAN - 1 :]
            grow, back = jnp.exp(cum - middle), jnp.exp(middle - cum)
            start, end = jnp.exp(middle), jnp.exp(final - middle)
            key_fwd, key_back, query_fwd = grow * keys, back * keys, grow * queries
            made.append(dict(
                sig=sig[:, columns(head)],
                beta=betas[:, head : head + 1],
                queries=queries, keys=keys, query_norm=query_norm, key_norm=key_norm,
                grow=grow, back=back, start=start, end=end, final=final,
                key_fwd=key_fwd, key_back=key_back, query_fwd=query_fwd,
                key_start=key_fwd * start, query_start=query_fwd * start, key_end=key_back * end,
                decay=jnp.exp(sum(mm(half, ones, 0, 0) for half in halves(decays[:, columns(head)]))),
                values=proj_ref[rows, columns(head, 2)],
            ))
        return made

    def rows_of(block):
        return pl.ds(pl.multiple_of(block * SPAN, SPAN), SPAN)

    def forward(block, carried):
        rows = rows_of(block)
        made = prepare(rows)
        powers, inverses = [], []
        for head, it in enumerate(made):
            both = mm(jnp.concatenate([it["key_fwd"], it["query_fwd"]], axis=0), it["key_back"], 1, 1)
            coupling = jnp.where(strict, both[:SPAN], 0.0)
            scores = jnp.where(lower, both[SPAN:], 0.0)
            coupling_ref[head, block] = coupling
            scores_ref[head, block] = scores.astype(jnp.bfloat16)
            power = -it["beta"] * coupling
            powers.append(power)
            inverses.append(eye + power)
        powers = [square_mm(power, power) for power in powers]
        for section in range(2, (SPAN - 1).bit_length()):
            stacked = [
                square_mm(jnp.concatenate([inverse, power], axis=0), power)
                for inverse, power in zip(inverses, powers)
            ]
            inverses = [inverse + both[:SPAN] for inverse, both in zip(inverses, stacked)]
            powers = [both[SPAN:] for both in stacked]
        inverses = [inverse + square_mm(inverse, power) for inverse, power in zip(inverses, powers)]
        for head in head_list:
            inverse_ref[head, block] = inverses[head].astype(jnp.bfloat16)
        froms = [
            mm(jnp.concatenate([it["key_start"], it["query_start"]], axis=0), state_ref[head, block], 1, 0)
            for head, it in enumerate(made)
        ]
        us = [
            mm(inverse, it["beta"] * (it["values"] - both[:SPAN]), 1, 0)
            for inverse, it, both in zip(inverses, made, froms)
        ]
        for head, it in enumerate(made):
            state_ref[head, block + 1] = it["decay"] * state_ref[head, block] + mm(
                it["key_end"], us[head], 0, 0
            )
            u_ref[head, block] = us[head].astype(jnp.bfloat16)
            mixed = froms[head][SPAN:] + mm(scores_ref[head, block], us[head], 1, 0)
            mixed_ref[rows, columns(head)] = mixed.astype(jnp.bfloat16)
        return carried

    def backward(step, carried):
        block = blocks - 1 - step
        rows = rows_of(block)
        made = prepare(rows)
        grads = [grad_ref[rows, columns(head)] for head in head_list]
        dus = [
            mm(scores_ref[head, block], grads[head], 0, 0) + mm(it["key_end"], carry_ref[head], 1, 0)
            for head, it in enumerate(made)
        ]
        drs = [mm(inverse_ref[head, block], dus[head], 0, 0) for head in head_list]
        logits = jnp.zeros((SPAN, heads), jnp.float32)
        head_index = lax.broadcasted_iota(jnp.int32, (SPAN, heads), 1)
        for head, it in enumerate(made):
            beta, dr, out_grad = it["beta"], drs[head], grads[head]
            state, carry, u = state_ref[head, block], carry_ref[head], u_ref[head, block]
            scaled = beta * dr
            pair = jnp.concatenate([out_grad, -dr], axis=0)
            both = mm(pair, u, 1, 1)
            scores_grad = jnp.where(lower, both[:SPAN], 0.0)
            inner_grad = jnp.where(strict, both[SPAN:], 0.0)
            pair = jnp.concatenate([out_grad, -scaled], axis=0)
            both = mm(pair, state, 1, 1)
            query_start_grad, key_start_grad = both[:SPAN], both[SPAN:]
            key_end_grad = mm(u, carry, 1, 1)
            carry_ref[head] = it["decay"] * carry + mm(
                jnp.concatenate([it["query_start"], it["key_start"]], axis=0), pair, 0, 0
            )
            rest = it["values"] - mm(it["key_start"], state, 1, 0)
            beta_grad = jnp.sum(dr * rest, axis=1, keepdims=True) + jnp.sum(
                inner_grad * coupling_ref[head, block], axis=1, keepdims=True
            )
            square_grads = jnp.concatenate([scores_grad, beta * inner_grad], axis=0)
            both = mm(square_grads, it["key_back"], 1, 0)
            query_fwd_grad, key_fwd_grad = both[:SPAN], both[SPAN:]
            key_back_grad = mm(
                square_grads, jnp.concatenate([it["query_fwd"], it["key_fwd"]], axis=0), 0, 0
            )
            end_term = it["key_end"] * key_end_grad
            query_grow = query_fwd_grad + it["start"] * query_start_grad
            key_grow = key_fwd_grad + it["start"] * key_start_grad
            key_decay = key_back_grad + it["end"] * key_end_grad
            cum_grad = (
                it["query_fwd"] * query_grow + it["key_fwd"] * key_grow - it["key_back"] * key_decay
            )
            final_grad = jnp.sum(end_term, axis=0, keepdims=True) + jnp.exp(it["final"]) * mask_mm(
                one_rows, state * carry, 1, 1
            )[:1]
            decay_grad = mask_mm(lower_mask, cum_grad, 0, 0) + final_grad
            sig = it["sig"]
            gate_grad = decay_grad * (-0.25 * sig * (1.0 - sig))
            query_grad = it["grow"] * query_grow
            key_grad = it["grow"] * key_grow + it["back"] * key_decay

            def through_norm(values, inverse_norm, grad):
                return inverse_norm * (grad - values * jnp.sum(values * grad, axis=1, keepdims=True))

            parts = (
                through_norm(it["queries"], it["query_norm"], query_grad),
                through_norm(it["keys"], it["key_norm"], key_grad),
                scaled,
            )
            for part, value in enumerate(parts):
                proj_low_ref[rows, columns(head, part)] = value.astype(jnp.bfloat16)
            gate_low_ref[rows, columns(head)] = gate_grad.astype(jnp.bfloat16)
            bias_ref[:, columns(head)] += jnp.sum(gate_grad, axis=0, keepdims=True)
            logits = jnp.where(head_index == head, beta_grad * beta * (1.0 - beta), logits)
        logit_ref[rows, :] = logits
        return carried

    for head in head_list:
        state_ref[head, 0] = jnp.zeros((width, width), jnp.float32)
        carry_ref[head] = jnp.zeros((width, width), jnp.float32)
    bias_ref[...] = jnp.zeros_like(bias_ref)
    return (
        lambda first, last: lax.fori_loop(first, last, forward, 0),
        lambda first, last: lax.fori_loop(first, last, backward, 0),
    )


MESH = pl.DeviceIdType.MESH


def remote(source, target, send_sem, recv_sem, axis, index):
    return pltpu.make_async_remote_copy(
        src_ref=source, dst_ref=target, send_sem=send_sem, recv_sem=recv_sem,
        device_id={axis: index}, device_id_type=MESH,
    )


def meet(peers):
    barrier = pltpu.get_barrier_semaphore()
    for axis, index in peers:
        pl.semaphore_signal(barrier, inc=1, device_id={axis: index}, device_id_type=MESH)
    pl.semaphore_wait(barrier, len(peers))


def front_kernel(
    input_ref, grad_ref, qkv_ref, out_weight_ref, down_hbm, up_ref, beta_hbm, bias_hbm,
    turned_ref, low_rank_ref, mixed_ref, proj_low_ref, gate_low_ref, logit_ref, bias_sum_ref,
    layer_out_ref, out_grad_ref, low_grad_ref, logit_low_ref, parts_ref,
    gathered, weights, out_weights, up_own, down_ref, beta_weight_ref, bias_ref,
    proj_ref, gate_ref, beta_ref, mixed_grad_ref, turned_grad_ref,
    state_ref, inverse_ref, scores_ref, coupling_ref, u_ref, carry_ref,
    layer_weights, mixed_all, layer_send, layer_recv, layer_own,
    send_one, recv_one, send_two, recv_two, done_rows,
    own_sem, weight_sem, far_send, far_recv, head_send, head_recv, send_sems, recv_sems, local_sems,
):
    groups, count, block, features = gathered.shape[1:]
    heads = beta_ref.shape[1]
    width = up_own.shape[1]
    member, group = lax.axis_index("context"), lax.axis_index("head")
    tokens = count * block
    f32, bf16 = jnp.float32, jnp.bfloat16

    def context_at(offset):
        return lax.rem(member + offset, count)

    def head_at(offset):
        return lax.rem(group + offset, groups)

    row = lax.axis_index("dp")
    near = row + 1 - 2 * lax.rem(row, 2)
    across = lax.rem(row + 2, 4)
    opposite = 3 - row
    meet(
        [("context", context_at(offset)) for offset in range(1, count)]
        + [("head", head_at(offset)) for offset in range(1, groups)]
        + [("dp", near), ("dp", across)]
    )
    near_first = sorted(range(1, count), key=lambda k: min(k, count - k))
    sources = (input_ref, grad_ref)

    def own_copy(which):
        return pltpu.make_async_copy(
            sources[which], gathered.at[which, group, member], own_sem.at[which]
        )

    def far_copy(which, offset):
        sems = far_send.at[which, offset], far_recv.at[which, offset], "context"
        if offset == 2:
            place = gathered.at[which, group, lax.rem(member + count - 1, count)]
            return remote(place, place, *sems, context_at(1))
        return remote(
            sources[which], gathered.at[which, group, member], *sems, context_at(offset)
        )

    def head_copy(which, back, offset):
        source = lax.rem(member + count - back, count)
        place = gathered.at[which, group, source]
        return remote(
            place if back else sources[which], place,
            head_send.at[which, back, offset], head_recv.at[which, back, offset],
            "head", head_at(offset),
        )

    def begin(which):
        own_copy(which).start()
        for offset in range(1, groups):
            head_copy(which, 0, offset).start()
        for offset in near_first:
            if offset != 2:
                far_copy(which, offset).start()

    def pass_on(which, backs):
        for back in backs:
            far_copy(which, back).wait_recv()
            if back == 1 and count > 2:
                far_copy(which, 2).start()
            for offset in range(1, groups):
                head_copy(which, back, offset).start()

    def arrive(which):
        for back in range(count):
            for offset in range(1, groups):
                head_copy(which, back, offset).wait_recv()

    mine = pl.ds(pl.multiple_of(member * width, width), width)
    loads = [
        pltpu.make_async_copy(
            qkv_ref.at[part, :, mine], weights.at[:, pl.ds(part * width, width)], weight_sem.at[part]
        )
        for part in range(3)
    ]
    loads.append(pltpu.make_async_copy(out_weight_ref.at[:, mine], out_weights, weight_sem.at[3]))
    loads.append(pltpu.make_async_copy(up_ref.at[:, mine], up_own, weight_sem.at[4]))
    loads.append(pltpu.make_async_copy(down_hbm, down_ref, weight_sem.at[5]))
    loads.append(pltpu.make_async_copy(beta_hbm, beta_weight_ref, weight_sem.at[6]))
    loads.append(pltpu.make_async_copy(bias_hbm.at[:, mine], bias_ref, weight_sem.at[7]))

    begin(0)
    for load in loads:
        load.start()
    pass_on(0, near_first)
    begin(1)
    for load in loads:
        load.wait()
    own_copy(0).wait()

    tile = min(width, 256)

    def rows_of(which, part):
        return gathered[which, part].reshape(tokens, features)

    def one_product(which, part, right_ref, columns):
        base = pl.multiple_of(part * features, 16 if features % 16 == 0 else 8)
        return jnp.dot(
            rows_of(which, part), right_ref[pl.ds(base, features), columns],
            preferred_element_type=f32,
        )

    def product(which, right_ref, columns):
        total = None
        for part in range(groups):
            value = jnp.dot(
                rows_of(which, part),
                right_ref[pl.ds(part * features, features), columns],
                preferred_element_type=f32,
            )
            total = value if total is None else total + value
        return total

    def own_half(step, carried):
        columns = pl.ds(pl.multiple_of(step * tile, tile), tile)
        proj_ref[:, columns] = one_product(0, group, weights, columns)
        return carried

    def project(step, carried):
        columns = pl.ds(pl.multiple_of(step * tile, tile), tile)
        total = proj_ref[:, columns]
        for offset in range(1, groups):
            total = total + one_product(0, head_at(offset), weights, columns)
        proj_ref[:, columns] = total
        return carried

    tiles = 3 * width // tile
    lax.fori_loop(0, tiles, own_half, 0)
    arrive(0)
    lax.fori_loop(0, tiles // 2, project, 0)
    pass_on(1, near_first[:1])
    lax.fori_loop(tiles // 2, tiles, project, 0)
    low_rank = product(0, down_ref, slice(None)).astype(bf16)
    low_rank_ref[...] = low_rank
    gate_ref[...] = jnp.dot(low_rank, up_own[...], preferred_element_type=f32) + bias_ref[...]
    logits = None
    for part in range(groups):
        value = lax.dot_general(
            rows_of(0, part), beta_weight_ref[:, part * features : (part + 1) * features],
            (((1,), (1,)), ((), ())), preferred_element_type=f32,
        )
        logits = value if logits is None else logits + value
    lane = lax.broadcasted_iota(jnp.int32, logits.shape, 1)
    for head in range(heads):
        picked = jnp.where(lane == member * heads + head, logits, 0.0)
        beta_ref[:, head : head + 1] = jnp.sum(picked, axis=1, keepdims=True)

    def turn(which, target_ref):
        for part in range(groups):
            for index in range(count):
                target_ref[part * features : (part + 1) * features, index * block : (index + 1) * block] = (
                    gathered[which, part, index].T
                )

    forward, backward = recurrence_passes(
        proj_ref, gate_ref, beta_ref, mixed_grad_ref,
        mixed_ref, proj_low_ref, gate_low_ref, logit_ref, bias_sum_ref,
        state_ref, inverse_ref, scores_ref, coupling_ref, u_ref, carry_ref,
    )
    share = tokens // SPAN // count
    for part in range(count):
        if part + 1 < len(near_first):
            pass_on(1, [near_first[part + 1]])
        forward(part * share, (part + 1) * share)

    numbers, flying = {}, {}

    def start(key, source, target, axis, index):
        number = numbers.setdefault(key, len(numbers))
        flying[key] = remote(
            source, target, send_sems.at[number], recv_sems.at[number], axis, index
        )
        flying[key].start()

    def arrived(*key):
        flying[key].wait_recv()

    def dot(left, right, left_dim=1, right_dim=0):
        return lax.dot_general(
            left, right, (((left_dim,), (right_dim,)), ((), ())), preferred_element_type=f32
        )

    far_first = near_first[::-1]
    offsets = far_first + [0]
    for offset in far_first:
        chosen = context_at(offset)
        start(
            ("mixed", offset),
            mixed_ref.at[pl.ds(pl.multiple_of(chosen * block, block), block), :],
            mixed_all.at[member], "context", chosen,
        )
    mixed_all[member] = mixed_ref[pl.ds(pl.multiple_of(member * block, block), block), :]
    group_order = list(range(1, groups)) + [0]
    height = 16 if features % 16 == 0 else 8

    def layer_load(offset):
        base = pl.multiple_of(head_at(offset) * features, height)
        return pltpu.make_async_copy(
            out_weight_ref.at[pl.ds(base, features), :], layer_weights, local_sems.at[0]
        )

    layer_load(group_order[0]).start()
    turn(0, turned_ref)
    own_copy(1).wait()
    arrive(1)
    turn(1, turned_grad_ref)
    slab = done_rows.shape[1]
    step_rows = 16 if slab % 16 == 0 else 8

    def out_term(chosen, index):
        rows = pl.ds(pl.multiple_of((chosen * 4 + index) * slab, step_rows), slab)
        return dot(turned_grad_ref[rows, :], mixed_ref[...])

    def out_one():
        def fill(chosen, carried):
            send_one[chosen, 0] = out_term(chosen, near).astype(bf16)
            send_one[chosen, 1] = out_term(chosen, opposite).astype(bf16)
            return carried

        lax.fori_loop(0, count, fill, 0)
        start(("one",), send_one, recv_one, "dp", near)

    def out_two():
        arrived("one")

        def fill(chosen, carried):
            total = out_term(chosen, across) + recv_one[chosen, 1].astype(f32)
            send_two[chosen] = total.astype(bf16)
            return carried

        lax.fori_loop(0, count, fill, 0)
        start(("two",), send_two, recv_two, "dp", across)

    mine_out = out_grad_ref.at[:, mine]

    def own_out():
        return pltpu.make_async_copy(done_rows.at[member], mine_out, local_sems.at[1])

    def out_three():
        arrived("two")

        def fill(chosen, carried):
            total = out_term(chosen, row) + recv_one[chosen, 0].astype(f32)
            total = total + recv_two[chosen].astype(f32)
            done_rows[chosen] = total.astype(bf16)
            return carried

        lax.fori_loop(0, count, fill, 0)
        for offset in far_first:
            chosen = context_at(offset)
            start(("far", offset), done_rows.at[chosen], mine_out, "context", chosen)
        own_out().start()

    stretch = 384 if features % 384 == 0 else features

    def layer_half(offset, store):
        layer_load(offset).wait()

        def some(step, carried):
            if stretch == features:
                rows = slice(None)
            else:
                rows = pl.ds(pl.multiple_of(step * stretch, stretch), stretch)
            value = None
            for index in range(count):
                one = dot(
                    mixed_all[index], layer_weights[rows, index * width : (index + 1) * width], 1, 1
                )
                value = one if value is None else value + one
            store(rows, value)
            return carried

        lax.fori_loop(0, features // stretch, some, 0)

    def layer_peers():
        for offset in far_first:
            arrived("mixed", offset)
        for place, offset in enumerate(group_order[:-1]):

            def store(lanes, value, offset=offset):
                layer_send[offset - 1, :, lanes] = value.astype(bf16)

            layer_half(offset, store)
            layer_load(group_order[place + 1]).start()
            start(
                ("layer", offset), layer_send.at[offset - 1], layer_recv.at[offset - 1],
                "head", head_at(offset),
            )

    def layer_mine():
        def store(lanes, value):
            layer_own[:, lanes] = value

        layer_half(0, store)

    def project_grad(step, carried):
        columns = pl.ds(pl.multiple_of(step * tile, tile), tile)
        mixed_grad_ref[:, columns] = product(1, out_weights, columns)
        return carried

    out_one()
    lax.fori_loop(0, width // tile, project_grad, 0)
    out_two()
    between = {0: [layer_peers], 1: [layer_mine], 2: [out_three]}
    for part in range(count):
        backward(part * share, (part + 1) * share)
        for action in between.get(part, []):
            action()
    low_grad = dot(gate_low_ref[...], up_own[...], 1, 1).astype(bf16)
    low_grad_ref[...] = low_grad
    lane = lax.broadcasted_iota(jnp.int32, logit_low_ref.shape, 1)
    logit_all = jnp.zeros(lane.shape, f32)
    for head in range(heads):
        logit_all = jnp.where(lane == member * heads + head, logit_ref[:, head : head + 1], logit_all)
    logit_low_ref[...] = logit_all.astype(bf16)
    for part in range(groups):
        for index in range(features // stretch):
            lanes = slice(index * stretch, (index + 1) * stretch)
            rows = slice(part * features + lanes.start, part * features + lanes.stop)
            value = dot(proj_low_ref[...], weights[rows, :], 1, 1)
            value = value + dot(low_grad_ref[...], down_ref[rows, :], 1, 1)
            value = value + dot(
                logit_low_ref[:, : count * heads], beta_weight_ref[:, rows], 1, 0
            )
            parts_ref[part, :, :, lanes] = value.astype(bf16).reshape(count, block, stretch)
    total = layer_own[...]
    for offset in range(1, groups):
        arrived("layer", offset)
        total = total + layer_recv[offset - 1].astype(f32)
    layer_out_ref[...] = total.astype(bf16)
    for offset in far_first:
        arrived("far", offset)
    own_out().wait()
    for copy in flying.values():
        copy.wait_send()
    for which in range(2):
        for offset in range(1, count):
            far_copy(which, offset).wait_send()
        for back in range(count):
            for offset in range(1, groups):
                head_copy(which, back, offset).wait_send()


def front(inputs, output_grad, qkv, out_weight, down_weight, up_weight, beta_turned, gate_bias):
    count, groups = lax.axis_size("context"), lax.axis_size("head")
    block, features = inputs.shape
    tokens, model_width = count * block, groups * features
    all_width = out_weight.shape[1] // count
    heads = beta_turned.shape[0] // count
    rank = down_weight.shape[1]
    f32, bf16 = jnp.float32, jnp.bfloat16
    vmem = pl.BlockSpec(memory_space=pltpu.VMEM)
    hbm = pl.BlockSpec(memory_space=pltpu.HBM)
    dma = pltpu.SemaphoreType.DMA
    shape = jax.ShapeDtypeStruct
    blocks = tokens // SPAN
    head_width = all_width // heads
    slab = model_width // (4 * count)
    return pl.pallas_call(
        front_kernel,
        in_specs=[hbm] * 8,
        out_specs=[vmem] * 8 + [hbm] + [vmem] * 3,
        out_shape=[
            shape((model_width, tokens), bf16),
            shape((tokens, rank), bf16),
            shape((tokens, all_width), bf16),
            shape((tokens, 3 * all_width), bf16),
            shape((tokens, all_width), bf16),
            shape((tokens, heads), f32),
            shape((1, all_width), f32),
            shape((block, features), bf16),
            shape((slab, count * all_width), bf16),
            shape((tokens, rank), bf16),
            shape((tokens, max(16, count * heads)), bf16),
            shape((groups, count, block, features), bf16),
        ],
        scratch_shapes=[
            pltpu.VMEM((2, groups, count, block, features), bf16),
            pltpu.VMEM((model_width, 3 * all_width), bf16),
            pltpu.VMEM((model_width, all_width), bf16),
            pltpu.VMEM((rank, all_width), bf16),
            pltpu.VMEM(down_weight.shape, bf16),
            pltpu.VMEM(beta_turned.shape, bf16),
            pltpu.VMEM((1, all_width), f32),
            pltpu.VMEM((tokens, 3 * all_width), f32),
            pltpu.VMEM((tokens, all_width), f32),
            pltpu.VMEM((tokens, heads), f32),
            pltpu.VMEM((tokens, all_width), f32),
            pltpu.VMEM((model_width, tokens), bf16),
            pltpu.VMEM((heads, blocks + 1, head_width, head_width), f32),
            pltpu.VMEM((heads, blocks, SPAN, SPAN), bf16),
            pltpu.VMEM((heads, blocks, SPAN, SPAN), bf16),
            pltpu.VMEM((heads, blocks, SPAN, SPAN), f32),
            pltpu.VMEM((heads, blocks, SPAN, head_width), bf16),
            pltpu.VMEM((heads, head_width, head_width), f32),
            pltpu.VMEM((features, count * all_width), bf16),
            pltpu.VMEM((count, block, all_width), bf16),
            pltpu.VMEM((groups - 1, block, features), bf16),
            pltpu.VMEM((groups - 1, block, features), bf16),
            pltpu.VMEM((block, features), f32),
            pltpu.VMEM((count, 2, slab, all_width), bf16),
            pltpu.VMEM((count, 2, slab, all_width), bf16),
            pltpu.VMEM((count, slab, all_width), bf16),
            pltpu.VMEM((count, slab, all_width), bf16),
            pltpu.VMEM((count, slab, all_width), bf16),
            dma((2,)), dma((8,)),
            dma((2, count)), dma((2, count)),
            dma((2, count, groups)), dma((2, count, groups)),
            dma((4 * count,)), dma((4 * count,)), dma((2,)),
        ],
        compiler_params=pltpu.CompilerParams(
            collective_id=2, has_side_effects=True, vmem_limit_bytes=60 * 1024 * 1024
        ),
    )(inputs, output_grad, qkv, out_weight, down_weight, up_weight, beta_turned, gate_bias)


def exchange_kernel(
    turned_ref, proj_ref, gate_ref, low_grad, logit_low_ref, low_rank_ref, bias_ref, parts,
    qkv_ref, input_ref, up_out_ref, down_out_ref, beta_out_ref, bias_out_ref,
    send_one, recv_one, send_two, recv_two, done_rows,
    head_recv, part_send, part_recv,
    up_full, up_slots, up_one, up_two, up_across, up_all,
    down_slots, down_one, down_two, down_across, down_done, down_far, down_group, down_all,
    beta_own, beta_one, beta_sum, beta_two, beta_done, beta_far,
    send_sems, recv_sems, local_sems,
):
    groups, count, block, features = parts.shape
    width = gate_ref.shape[1]
    slab = done_rows.shape[1]
    head_count = beta_out_ref.shape[0]
    rank = low_grad.shape[1]
    tokens = count * block
    quarter = rank // 4
    f32, bf16 = jnp.float32, jnp.bfloat16
    member, row, group = (lax.axis_index(name) for name in ("context", "dp", "head"))
    near = row + 1 - 2 * lax.rem(row, 2)
    across = lax.rem(row + 2, 4)
    opposite = 3 - row
    slots = (near, opposite, row, across)

    def context_at(offset):
        return lax.rem(member + offset, count)

    def head_at(offset):
        return lax.rem(group + offset, groups)

    meet(
        [("context", context_at(offset)) for offset in range(1, count)]
        + [("head", head_at(offset)) for offset in range(1, groups)]
        + [("dp", near), ("dp", across)]
    )
    offsets = sorted(range(1, count), key=lambda k: -min(k, count - k)) + [0]
    far_offsets = offsets[:-1]
    numbers, flying = {}, {}

    def begin(key, source, target, axis, index):
        number = numbers.setdefault(key, len(numbers))
        flying[key] = remote(
            source, target, send_sems.at[number], recv_sems.at[number], axis, index
        )
        flying[key].start()

    def arrived(*key):
        flying[key].wait_recv()

    def dot(left, right, left_dim=1, right_dim=0):
        return lax.dot_general(
            left, right, (((left_dim,), (right_dim,)), ((), ())), preferred_element_type=f32
        )

    def slab_rows(chosen, index):
        step = 16 if slab % 16 == 0 else 8
        return pl.ds(pl.multiple_of((chosen * 4 + index) * slab, step), slab)

    mine = pl.ds(pl.multiple_of(member * width, width), width)

    bits = [1 << place for place in range((count - 1).bit_length())]

    def flip(mask):
        index = member
        for bit in bits:
            if mask & bit:
                index = index + bit - 2 * bit * lax.rem(member // bit, 2)
        return index

    masks = [mask for bit in bits for mask in range(count) if mask & -mask == bit] + [0]

    def send_parts(chosen_masks):
        for offset in range(1, groups):
            chosen = head_at(offset)
            for mask in chosen_masks:
                begin(
                    ("part", offset, mask), parts.at[chosen, flip(mask)],
                    head_recv.at[offset - 1, flip(mask)], "head", chosen,
                )

    def small_one():
        beta_own[...] = dot(logit_low_ref[...], turned_ref[...], 0, 1).astype(bf16)
        begin(("beta", 1), beta_own, beta_one, "dp", near)

        def down_terms(chosen, carried):
            for slot, index in enumerate(slots):
                down_slots[slot // 2, chosen, slot % 2] = dot(
                    turned_ref[slab_rows(chosen, index), :], low_grad[...]
                ).astype(bf16)
            return carried

        lax.fori_loop(0, count, down_terms, 0)
        begin(("down", 1), down_slots.at[0], down_one, "dp", near)
        up_full[...] = dot(low_rank_ref[...], gate_ref[...], 0, 0)
        for slot, index in enumerate(slots):
            rows = pl.ds(pl.multiple_of(index * quarter, 8), quarter)
            up_slots[slot, :quarter] = up_full[rows, :].astype(bf16)
            up_slots[slot, quarter:] = jnp.broadcast_to(bias_ref[...], (16, width)).astype(bf16)
        begin(("up", 1), up_slots.at[pl.ds(0, 2)], up_one, "dp", near)

    def products(step, targets):
        chosen = context_at(offsets[step])

        def fill(part, carried):
            columns = pl.ds(pl.multiple_of(part * width, width), width)
            for index, store in targets:
                store(columns, dot(turned_ref[slab_rows(chosen, index), :], proj_ref[:, columns]))
            return carried

        lax.fori_loop(0, 3, fill, 0)

    def first(step):
        def sender(slot):
            def store(columns, value):
                send_one[step, slot, :, columns] = value.astype(bf16)

            return store

        products(step, [(near, sender(0)), (opposite, sender(1))])
        begin(("one", step), send_one.at[step], recv_one.at[step], "dp", near)

    def second(step):
        arrived("one", step)

        def store(columns, value):
            total = value + recv_one[step, 1, :, columns].astype(f32)
            send_two[step, :, columns] = total.astype(bf16)

        products(step, [(across, store)])
        begin(("two", step), send_two.at[step], recv_two.at[step], "dp", across)

    def owner_ref(part):
        return qkv_ref.at[part, :, mine]

    def own_copy(step, part):
        return pltpu.make_async_copy(
            done_rows.at[step, :, pl.ds(part * width, width)], owner_ref(part), local_sems.at[part]
        )

    def third(step):
        arrived("two", step)

        def store(columns, value):
            total = value + recv_one[step, 0, :, columns].astype(f32)
            total = total + recv_two[step, :, columns].astype(f32)
            done_rows[step, :, columns] = total.astype(bf16)

        products(step, [(row, store)])
        offset = offsets[step]
        for part in range(3):
            if offset:
                begin(
                    ("far", offset, part), done_rows.at[step, :, pl.ds(part * width, width)],
                    owner_ref(part), "context", context_at(offset),
                )
            else:
                own_copy(step, part).start()

    taken = {mask: [] for mask in range(count)}
    part_slots = {}

    def part_total(mask):
        chosen = flip(mask)
        total = parts[group, chosen].astype(f32)
        for offset in range(1, groups):
            arrived("part", offset, mask)
            total = total + head_recv[offset - 1, chosen].astype(f32)
        for bit in taken[mask]:
            arrived("sum", bit, mask)
            total = total + part_recv[part_slots[bit, mask]].astype(f32)
        return total

    def part_step(bit):
        for mask in masks:
            if mask & -mask == bit:
                part_send[mask] = part_total(mask).astype(bf16)
                slot = part_slots.setdefault((bit, mask - bit), len(part_slots))
                begin(
                    ("sum", bit, mask - bit), part_send.at[mask], part_recv.at[slot],
                    "context", flip(bit),
                )
                taken[mask - bit].append(bit)

    def small_two():
        for name in ("beta", "down", "up"):
            arrived(name, 1)
        beta_sum[...] = (beta_own[...].astype(f32) + beta_one[...].astype(f32)).astype(bf16)
        begin(("beta", 2), beta_sum, beta_two, "dp", across)
        for index in range(count):
            down_two[index] = (
                down_slots[1, index, 1].astype(f32) + down_one[index, 1].astype(f32)
            ).astype(bf16)
        begin(("down", 2), down_two, down_across, "dp", across)
        up_two[...] = (up_slots[3].astype(f32) + up_one[1].astype(f32)).astype(bf16)
        begin(("up", 2), up_two, up_across, "dp", across)

    def small_three():
        for name in ("beta", "down", "up"):
            arrived(name, 2)
        for index in range(count):
            down_done[index] = (
                down_slots[1, index, 0].astype(f32)
                + down_one[index, 0].astype(f32)
                + down_across[index].astype(f32)
            ).astype(bf16)
        up_all[member, row] = (
            up_slots[2].astype(f32) + up_one[0].astype(f32) + up_across[...].astype(f32)
        ).astype(bf16)
        beta_done[0] = (beta_sum[...].astype(f32) + beta_two[...].astype(f32)).astype(bf16)
        for offset in far_offsets:
            chosen = context_at(offset)
            begin(("down", "far", offset), down_done.at[chosen], down_far.at[offset], "context", chosen)

    def spread(name, array, held, bit):
        for mask in held:
            place = array.at[flip(mask), row]
            begin((name, bit, mask), place, place, "context", flip(bit))

    def landed(name, held, bit):
        for mask in held:
            arrived(name, bit, mask)

    def up_step(bit, held):
        def run():
            spread("up far", up_all, held, bit)
            place = bits[::-1].index(bit)
            begin(("beta far", bit), beta_done.at[place], beta_far.at[place], "context", flip(bit))

        return run

    def up_wait(bit, held):
        def run():
            landed("up far", held, bit)
            place = bits[::-1].index(bit)
            arrived("beta far", bit)
            total = beta_done[place].astype(f32) + beta_far[place].astype(f32)
            beta_done[place + 1] = total.astype(bf16)

        return run

    def down_step(bit, held):
        return lambda: spread("down far", down_all, held, bit)

    def down_wait(bit, held):
        return lambda: landed("down far", held, bit)

    def small_four():
        total = down_done[member].astype(f32)
        for offset in far_offsets:
            arrived("down", "far", offset)
            total = total + down_far[offset].astype(f32)
        down_group[group] = total.astype(bf16)
        for offset in range(1, groups):
            begin(
                ("down", "head", offset), down_group.at[group], down_group.at[group],
                "head", head_at(offset),
            )

    def small_five():
        for offset in range(1, groups):
            arrived("down", "head", offset)
        total = down_group[0].astype(f32)
        for index in range(1, groups):
            total = total + down_group[index].astype(f32)
        down_all[member, row] = total.astype(bf16)

    def small_six():
        begin(("up", "across"), up_all.at[:, row], up_all.at[:, row], "dp", across)
        begin(("down", "across"), down_all.at[:, row], down_all.at[:, row], "dp", across)

    def small_seven():
        arrived("up", "across")
        arrived("down", "across")
        for place, index in enumerate((row, across)):
            begin(("up", "near", place), up_all.at[:, index], up_all.at[:, index], "dp", near)
            begin(("down", "near", place), down_all.at[:, index], down_all.at[:, index], "dp", near)

    def small_last():
        for place in range(2):
            arrived("up", "near", place)
            arrived("down", "near", place)
        for index in range(count):
            columns = slice(index * width, (index + 1) * width)
            for part in range(4):
                up_out_ref[part * quarter : (part + 1) * quarter, columns] = up_all[
                    index, part, :quarter
                ].astype(f32)
                start = (index * 4 + part) * slab
                down_out_ref[start : start + slab, :] = down_all[index, part].astype(f32)
            bias_out_ref[:, columns] = up_all[index, 0, quarter : quarter + 1].astype(f32)
        beta_out_ref[...] = beta_done[len(bits)].astype(f32)[:head_count]

    steps_up, steps_down, held = [], [], [0]
    for bit in bits[::-1]:
        steps_up.append((up_step(bit, list(held)), up_wait(bit, list(held))))
        steps_down.append((down_step(bit, list(held)), down_wait(bit, list(held))))
        held += [mask + bit for mask in held]
    waiting = [[small_two], [small_three, steps_up[0][0]]]
    stage = [small_four, steps_up[0][1]]
    for later in range(1, len(bits)):
        waiting.append(stage + [steps_up[later][0]])
        stage = [steps_up[later][1]]
    waiting.append(stage + [small_five, steps_down[0][0]])
    for later in range(1, len(bits)):
        waiting.append([steps_down[later - 1][1], steps_down[later][0]])
    waiting += [[steps_down[-1][1], small_six], [small_seven]]
    part_steps = [lambda bit=bit: part_step(bit) for bit in bits]

    def advance(queue):
        if queue:
            ready = queue.pop(0)
            for action in ready if isinstance(ready, list) else [ready]:
                action()

    early = [mask for mask in masks if mask & 1]
    send_parts(early)
    first(0)
    small_one()
    second(0)
    advance(waiting)
    for step in range(1, count):
        first(step)
        if step == 1:
            advance(part_steps)
        second(step)
        if step == 1:
            send_parts([mask for mask in masks if mask not in early])
        else:
            advance(waiting)
        third(step - 1)
        if step > 1:
            advance(part_steps)
        advance(waiting)
    third(count - 1)
    while waiting:
        advance(waiting)
    while part_steps:
        advance(part_steps)

    input_ref[...] = part_total(0).astype(bf16)
    small_last()
    for offset in far_offsets:
        for part in range(3):
            arrived("far", offset, part)
    for part in range(3):
        own_copy(count - 1, part).wait()
    for copy in flying.values():
        copy.wait_send()


def exchange(
    turned, proj_low, gate_low, low_grad, logit_low, low_rank, bias_term, input_parts, head_count
):
    count, groups, parts = (lax.axis_size(name) for name in ("context", "head", "dp"))
    assert parts == 4
    model_width, tokens = turned.shape
    width, rank = gate_low.shape[1], low_grad.shape[1]
    slab, block, features = model_width // (count * parts), tokens // count, model_width // groups
    quarter = rank // parts
    lines = max(16, head_count)
    f32, bf16 = jnp.float32, jnp.bfloat16
    vmem = pl.BlockSpec(memory_space=pltpu.VMEM)
    hbm = pl.BlockSpec(memory_space=pltpu.HBM)
    dma = pltpu.SemaphoreType.DMA
    shape = jax.ShapeDtypeStruct
    copies = 24 * count
    return pl.pallas_call(
        exchange_kernel,
        in_specs=[vmem] * 8,
        out_specs=[hbm] + [vmem] * 5,
        out_shape=[
            shape((3, slab, count * width), bf16),
            shape((block, features), bf16),
            shape((rank, count * width), f32),
            shape((model_width, rank), f32),
            shape((head_count, model_width), f32),
            shape((1, count * width), f32),
        ],
        scratch_shapes=[
            pltpu.VMEM((count, 2, slab, 3 * width), bf16),
            pltpu.VMEM((count, 2, slab, 3 * width), bf16),
            pltpu.VMEM((count, slab, 3 * width), bf16),
            pltpu.VMEM((count, slab, 3 * width), bf16),
            pltpu.VMEM((count, slab, 3 * width), bf16),
            pltpu.VMEM((groups - 1, count, block, features), bf16),
            pltpu.VMEM((count, block, features), bf16),
            pltpu.VMEM((count, block, features), bf16),
            pltpu.VMEM((rank, width), f32),
            pltpu.VMEM((4, quarter + 16, width), bf16),
            pltpu.VMEM((2, quarter + 16, width), bf16),
            pltpu.VMEM((quarter + 16, width), bf16),
            pltpu.VMEM((quarter + 16, width), bf16),
            pltpu.VMEM((count, 4, quarter + 16, width), bf16),
            pltpu.VMEM((2, count, 2, slab, rank), bf16),
            pltpu.VMEM((count, 2, slab, rank), bf16),
            pltpu.VMEM((count, slab, rank), bf16),
            pltpu.VMEM((count, slab, rank), bf16),
            pltpu.VMEM((count, slab, rank), bf16),
            pltpu.VMEM((count, slab, rank), bf16),
            pltpu.VMEM((groups, slab, rank), bf16),
            pltpu.VMEM((count, 4, slab, rank), bf16),
            pltpu.VMEM((lines, model_width), bf16),
            pltpu.VMEM((lines, model_width), bf16),
            pltpu.VMEM((lines, model_width), bf16),
            pltpu.VMEM((lines, model_width), bf16),
            pltpu.VMEM((count.bit_length(), lines, model_width), bf16),
            pltpu.VMEM((count.bit_length(), lines, model_width), bf16),
            dma((copies,)), dma((copies,)), dma((3,)),
        ],
        compiler_params=pltpu.CompilerParams(
            collective_id=1, has_side_effects=True, vmem_limit_bytes=60 * 1024 * 1024
        ),
    )(
        turned, proj_low, gate_low, low_grad, logit_low, low_rank, bias_term, input_parts
    )


def finish_kernel(*refs):
    count = (len(refs) - 1) // 3
    sources, targets, held = refs[:count], refs[count : 2 * count], refs[2 * count : 3 * count]
    sems = refs[-1]
    into = [pltpu.make_async_copy(sources[k], held[k], sems.at[0, k]) for k in range(count)]
    out = [pltpu.make_async_copy(held[k], targets[k], sems.at[1, k]) for k in range(count)]
    for copy in into:
        copy.start()
    for first, second in zip(into, out):
        first.wait()
        second.start()
    for copy in out:
        copy.wait()


def finish(*arrays):
    hbm = pl.BlockSpec(memory_space=pltpu.HBM)
    return pl.pallas_call(
        finish_kernel,
        in_specs=[hbm] * len(arrays),
        out_specs=[hbm] * len(arrays),
        out_shape=[jax.ShapeDtypeStruct(array.shape, array.dtype) for array in arrays],
        scratch_shapes=[pltpu.VMEM(array.shape, array.dtype) for array in arrays]
        + [pltpu.SemaphoreType.DMA((2, len(arrays)))],
        compiler_params=pltpu.CompilerParams(vmem_limit_bytes=60 * 1024 * 1024),
    )(*arrays)


def shards(
    inputs, output_grad, qkv_weight, out_weight, down_weight, up_weight, beta_weight, gate_bias
):
    qkv_turned = jnp.transpose(qkv_weight, (1, 0, 2))
    turned, low_rank, _, proj_low, gate_low, _, bias_term, layer_out, out_grad, *more = front(
        inputs[0], output_grad[0], qkv_turned, out_weight, down_weight, up_weight, beta_weight.T,
        gate_bias[None],
    )
    low_grad, logit_low, input_parts = more
    results = exchange(
        turned, proj_low, gate_low, low_grad, logit_low, low_rank, bias_term, input_parts,
        beta_weight.shape[1],
    )
    layer_out, out_grad, qkv_grad, input_grad, up_grad, down_grad, beta_grad, bias_grad = finish(
        layer_out, out_grad, *results
    )
    qkv_grad = jnp.transpose(qkv_grad, (1, 0, 2))
    return (
        layer_out[None], input_grad[None], qkv_grad, out_grad, up_grad, down_grad, beta_grad.T,
        bias_grad[0],
    )


def solution(mesh):
    return jax.shard_map(
        shards,
        mesh=mesh,
        in_specs=(
            P("dp", "context", "head"),
            P("dp", "context", "head"),
            P(None, None, "head"),
            P(None, "head"),
            P(),
            P(None, "head"),
            P(None, "head"),
            P("head"),
        ),
        out_specs=(
            P("dp", "context", "head"),
            P("dp", "context", "head"),
            P(("context", "dp"), None, "head"),
            P(("context", "dp"), "head"),
            P(None, "head"),
            P(),
            P(None, "head"),
            P("head"),
        ),
        check_vma=False,
    )
```
